256 devices in a mesh: shot: 32 (over z_lo, y, core), sub: 8 (over x, z_hi).
Axes of the slice: x: 4, y: 4, z: 8 (z_hi: 2, z_lo: 4; z = z_hi * 4 + z_lo), core: 2. Of those that a mesh axis runs over, the one named last changes fastest.
Arguments:
- velocity_tiles: float32 [384, 64, 256], P('shot', 'sub'), may hold values from 0.05 to 0.2
- forward_state: bfloat16 [32, 2, 64, 64, 128], P('shot', None, 'sub'), may hold values from -1.5 to 1.5
- adjoint_state: bfloat16 [32, 2, 64, 64, 128], P('shot', None, 'sub'), may hold values from -1.5 to 1.5
- wavelet: float32 [32, 4], P('shot'), may hold values from -4 to 4
- source_cell: int32 [32], P('shot'), may hold values from 0 to 524287
- receiver_cell: int32 [32, 256], P('shot'), may hold values from 0 to 524287
- residual: float32 [32, 4, 256], P('shot'), may hold values from -4 to 4
- aperture_row: int32 [32], replicated, may hold values from 0 to 12, as said below
- aperture_col: int32 [32], replicated, may hold values from 1 to 255, as said below
Outputs:
- gradient: float32 [384, 64, 256], P('shot', 'sub')
The draws below stay inside these ranges and needn't reach their ends.
Inputs may be any that keep to these rules, and one draw needn't show every extreme that they name: Every aperture lies in the model: rows aperture_row[s] to aperture_row[s] + 3 are model tile rows. aperture_col[s] is never a multiple of 16; the aperture's columns end inside the model.
All inputs are finite; a program needn't handle non-finite values.
Results may differ from the reference program's by a relative error of at most 0.0004.
Values sent between devices are 32-bit elements; how exact they have to be, the bound alone decides.
A program may use at most 64 MiB of HBM per device.

```python
import math
import jax
import jax.numpy as jnp
from jax import lax

TILE = 16
RX = 4
RY = 3
NT = 4
NREC = 256
AP_ROWS = 4
AP_COLS = 8
OWN_COLS = 8
GX = 16
GY = 24
NTILES = 384
Z = 64
AX = 64
AY = 128
SHOTS = 32


def draw_aperture_row(key, part):
    starts = jax.random.randint(key, (SHOTS,), 0, GX - AP_ROWS + 1)
    shuffle = jax.random.permutation(jax.random.fold_in(key, 7), SHOTS)
    starts = starts.at[shuffle[0]].set(GX - AP_ROWS)
    starts = starts.at[shuffle[1]].set(0)
    return starts.astype(jnp.int32)


def draw_aperture_col(key, part):
    tile_start = jax.random.randint(key, (SHOTS,), 0, GY - AP_COLS)
    within = jax.random.randint(jax.random.fold_in(key, 3), (SHOTS,), 1, TILE)
    columns = tile_start * TILE + within
    shuffle = jax.random.permutation(jax.random.fold_in(key, 5), SHOTS)
    columns = columns.at[shuffle[0]].set((GY - AP_COLS) * TILE - 1)
    columns = columns.at[shuffle[1]].set(1)
    return columns.astype(jnp.int32)


def set_ends(values, key, least, largest):
    extent = values.shape
    spot = [jax.random.randint(jax.random.fold_in(key, axis), (), 0, extent[axis]) for axis in range(len(extent))]
    values = values.at[tuple(spot)].set(least)
    longest = extent.index(max(extent))
    spot[longest] = (spot[longest] + 1) % extent[longest]
    return values.at[tuple(spot)].set(largest)


def shard_levels(stream_key, dims, cuts, least, high):
    level = 1.0
    for axis_at, blocks in cuts:
        steps = jax.random.uniform(jax.random.fold_in(jax.random.fold_in(stream_key, 6), axis_at), (blocks,), jnp.float32, least / len(cuts), high / len(cuts))
        level = level * jnp.repeat(jnp.exp(steps), dims[axis_at] // blocks).reshape((-1,) + (1,) * (len(dims) - 1 - axis_at))
    return level


def normal_values(key, extent, scale, most, split=(), held_as=jnp.bfloat16):
    values = jax.random.normal(key, extent, jnp.float32) * scale
    if len(split) > 0:
        values = shard_levels(key, extent, split, -0.22, 0.18) * values
    return jnp.clip(values, min=-most, max=most).astype(held_as)


def setup_inputs(seed: int = 0) -> dict:
    keys = jax.random.split(jax.random.key(seed), 10)
    return {
        "velocity_tiles": jnp.clip(jnp.exp(math.log(0.2) - 1.3862944 * jax.random.uniform(keys[0], (NTILES, Z, TILE * TILE), jnp.float32) ** shard_levels(keys[0], (NTILES, Z, TILE * TILE), ((0, 32), (1, 8)), -0.2, 0.2)), 0.05, 0.2),
        "forward_state": normal_values(keys[1], (SHOTS, 2, Z, AX, AY), 0.25, 1.5, ((0, 32), (2, 8))),
        "adjoint_state": normal_values(keys[2], (SHOTS, 2, Z, AX, AY), 0.25, 1.5, ((0, 32), (2, 8))),
        "wavelet": normal_values(keys[3], (SHOTS, NT), 1.0, 4.0, ((0, 32),), jnp.float32),
        "source_cell": set_ends(jax.random.randint(keys[4], (SHOTS,), 0, Z * AX * AY), jax.random.fold_in(keys[4], 1), 0, (Z * AX * AY) - 1).astype(jnp.int32),
        "receiver_cell": set_ends(jax.random.randint(keys[5], (SHOTS, NREC), 0, Z * AX * AY), jax.random.fold_in(keys[5], 1), 0, (Z * AX * AY) - 1).astype(jnp.int32),
        "residual": normal_values(keys[6], (SHOTS, NT, NREC), 1.0, 4.0, ((0, 32),), jnp.float32),
        "aperture_row": draw_aperture_row(jax.random.fold_in(keys[9], 71), 0),
        "aperture_col": draw_aperture_col(jax.random.fold_in(keys[9], 71), 0),
    }


COEFFS = (-205.0 / 72.0, 8.0 / 5.0, -1.0 / 5.0, 8.0 / 315.0, -1.0 / 560.0)
IMAGE_SCALE = 1.0 / 64.0


def laplace(padded, depth_cells, row_cells, column_cells):
    r = 4
    center = padded[r:r + depth_cells, r:r + row_cells, r:r + column_cells]
    summed = (3.0 * COEFFS[0]) * center
    for k in range(1, 5):
        nearby = padded[r + k:r + k + depth_cells, r:r + row_cells, r:r + column_cells]
        nearby = nearby + padded[r - k:r - k + depth_cells, r:r + row_cells, r:r + column_cells]
        nearby = nearby + padded[r:r + depth_cells, r + k:r + k + row_cells, r:r + column_cells]
        nearby = nearby + padded[r:r + depth_cells, r - k:r - k + row_cells, r:r + column_cells]
        nearby = nearby + padded[r:r + depth_cells, r:r + row_cells, r + k:r + k + column_cells]
        nearby = nearby + padded[r:r + depth_cells, r:r + row_cells, r - k:r - k + column_cells]
        summed = summed + COEFFS[k] * nearby
    return summed


def grid_from_tiles(tiles):
    shaped = tiles.reshape(AP_ROWS, OWN_COLS, RX, RY, Z, TILE, TILE)
    return shaped.transpose(4, 2, 0, 5, 3, 1, 6).reshape(Z, GX * TILE, GY * TILE)


def tiles_from_grid(grid):
    shaped = grid.reshape(Z, RX, AP_ROWS, TILE, RY, OWN_COLS, TILE)
    return shaped.transpose(2, 5, 1, 4, 0, 3, 6).reshape(NTILES, Z, TILE * TILE)


def apply_operator(field):
    return laplace(jnp.pad(field, 4), Z, AX, AY)


def one_shot(model, state_fwd, state_adj, wave, source, receivers, resid):
    current = state_fwd[0].astype(jnp.float32)
    previous = state_fwd[1].astype(jnp.float32)
    lapped = []
    for n in range(NT):
        stencil = apply_operator(current)
        following = 2.0 * current - previous + model * stencil
        following = following.reshape(-1).at[source].add(wave[n]).reshape(Z, AX, AY)
        lapped.append(stencil)
        previous = current
        current = following
    now_field = state_adj[0].astype(jnp.float32)
    later_field = state_adj[1].astype(jnp.float32)
    image = jnp.zeros((Z, AX, AY), jnp.float32)
    for n in range(NT, 0, -1):
        result = 2.0 * now_field - later_field + apply_operator(model * now_field)
        result = result.reshape(-1).at[receivers].add(resid[n - 1]).reshape(Z, AX, AY)
        image = image + result * lapped[n - 1]
        later_field = now_field
        now_field = result
    return IMAGE_SCALE * image


def reference(velocity_tiles, forward_state, adjoint_state, wavelet, source_cell, receiver_cell, residual, aperture_row, aperture_col):
    vel_grid = grid_from_tiles(velocity_tiles)

    def advance(summed, index):
        start = (jnp.int32(0), (aperture_row[index] * TILE).astype(jnp.int32), aperture_col[index].astype(jnp.int32))
        model = lax.dynamic_slice(vel_grid, start, (Z, AX, AY))
        image = one_shot(model, forward_state[index], adjoint_state[index], wavelet[index], source_cell[index], receiver_cell[index], residual[index])
        window = lax.dynamic_slice(summed, start, (Z, AX, AY))
        summed = lax.dynamic_update_slice(summed, window + image, start)
        return summed, None

    initial = jnp.zeros((Z, GX * TILE, GY * TILE), jnp.float32)
    summed, _ = lax.scan(advance, initial, jnp.arange(SHOTS, dtype=jnp.int32))
    return tiles_from_grid(summed)
```

```python
import jax
import jax.numpy as jnp
from jax import lax
from jax.sharding import PartitionSpec as P
from jax.experimental import pallas as pl
from jax.experimental.pallas import tpu as pltpu

TILE = 16
RY = 3
SHOTS_DEV = 1
NT = 4
RADIUS = 4
AP_ROWS = 4
AP_COLS = 8
TILE_DEV = 12
AX = 64
AY = 128


COEFFS = (-205.0 / 72.0, 8.0 / 5.0, -1.0 / 5.0, 8.0 / 315.0, -1.0 / 560.0)
IMAGE_SCALE = 1.0 / 64.0


def padded_2(array, sides, width):
    for axis, dim in sides:
        size, length = (lax.axis_size(axis), array.shape[dim])
        up = [(i, (i + 1) % size) for i in range(size - 1)]
        down = [(j, i) for i, j in up]
        last = lax.slice_in_dim(array, length - width, length, axis=dim)
        first = lax.slice_in_dim(array, 0, width, axis=dim)
        before = lax.ppermute(last, axis, up)
        after = lax.ppermute(first, axis, down)
        array = jnp.concatenate([before, array, after], axis=dim)
    return array


def laplace(padded, depth_cells, row_cells, column_cells):
    r = 4
    center = padded[r : r + depth_cells, r : r + row_cells, r : r + column_cells]
    summed = 3.0 * COEFFS[0] * center
    for k in range(1, 5):
        nearby = padded[r + k : r + k + depth_cells, r : r + row_cells, r : r + column_cells]
        nearby = (
            nearby + padded[r - k : r - k + depth_cells, r : r + row_cells, r : r + column_cells]
        )
        nearby = (
            nearby + padded[r : r + depth_cells, r + k : r + k + row_cells, r : r + column_cells]
        )
        nearby = (
            nearby + padded[r : r + depth_cells, r - k : r - k + row_cells, r : r + column_cells]
        )
        nearby = (
            nearby + padded[r : r + depth_cells, r : r + row_cells, r + k : r + k + column_cells]
        )
        nearby = (
            nearby + padded[r : r + depth_cells, r : r + row_cells, r - k : r - k + column_cells]
        )
        summed = summed + COEFFS[k] * nearby
    return summed


def wave_operator(field):
    padded = padded_2(field, (("sub", 0),), RADIUS)
    padded = jnp.pad(padded, ((0, 0), (4, 4), (4, 4)))
    return laplace(padded, field.shape[0], AX, AY)


def adjoint_operator(field):
    padded = padded_2(field, (("sub", 0),), RADIUS)
    padded = jnp.pad(padded, ((0, 0), (4, 4), (4, 4)))
    return laplace(padded, field.shape[0], AX, AY)


def slot_layout(row_start, col_start, owner_row, owner_col, own_cols, caps):
    block_row = (owner_row - row_start) % AP_ROWS
    first_col = (owner_col - col_start // TILE) % own_cols
    block_col = first_col + own_cols * jnp.arange(caps, dtype=jnp.int32)
    usable = block_col <= AP_COLS
    return (block_row, block_col, usable)


def owner_slots(row_table, col_table, shot_list, groups, own_cols, caps):
    myself = lax.axis_index("shot")
    owner_row = myself // own_cols
    owner_col = myself % own_cols
    senders = jnp.arange(groups, dtype=jnp.int32)[:, None]
    picked = senders * SHOTS_DEV + jnp.asarray(shot_list, dtype=jnp.int32)[None, :]
    row_start = row_table[picked][..., None]
    col_start = col_table[picked][..., None]
    block_row, block_col, usable = slot_layout(
        row_start, col_start, owner_row, owner_col, own_cols, caps
    )
    tile_row = row_start + block_row
    tile_col = col_start // TILE + block_col
    local = tile_row // AP_ROWS * RY + tile_col // own_cols
    local = jnp.clip(local, 0, TILE_DEV - 1)
    return (local.reshape(-1), usable.reshape(-1))


def outgoing(velocity_tiles, row_table, col_table, shot_list, groups, own_cols, caps):
    local, usable = owner_slots(row_table, col_table, shot_list, groups, own_cols, caps)
    chosen = velocity_tiles[local]
    chosen = jnp.where(usable[:, None, None], chosen, 0.0)
    return chosen.reshape(
        groups, len(shot_list) * caps, velocity_tiles.shape[1], velocity_tiles.shape[2]
    )


def accumulate(gradient, returned, row_table, col_table, shot_list, groups, own_cols, caps):
    local, usable = owner_slots(row_table, col_table, shot_list, groups, own_cols, caps)
    pieces = returned.reshape(-1, gradient.shape[1], gradient.shape[2])
    return gradient.at[local].add(jnp.where(usable[:, None, None], pieces, 0.0))


def assemble(received, slot_base, row_start, col_start, own_cols):
    depth_cells = received.shape[2]
    slot_count = received.shape[1]
    rel_row = jnp.arange(AP_ROWS, dtype=jnp.int32)[:, None]
    rel_col = jnp.arange(AP_COLS + 1, dtype=jnp.int32)[None, :]
    source_owner = (row_start + rel_row) % AP_ROWS * own_cols + (
        col_start // TILE + rel_col
    ) % own_cols
    flat_index = (source_owner * slot_count + slot_base + rel_col // own_cols).reshape(-1)
    pieces = received.reshape(-1, depth_cells, TILE * TILE)[flat_index]
    block = pieces.reshape(AP_ROWS, AP_COLS + 1, depth_cells, TILE, TILE)
    block = block.transpose(2, 0, 3, 1, 4).reshape(depth_cells, AX, (AP_COLS + 1) * TILE)
    return lax.dynamic_slice_in_dim(block, col_start % TILE, AY, 2)


def disperse(image, row_start, col_start, groups, own_cols, caps):
    depth_cells = image.shape[0]
    wide = jnp.zeros((depth_cells, AX, (AP_COLS + 1) * TILE), jnp.float32)
    wide = lax.dynamic_update_slice_in_dim(wide, image, col_start % TILE, 2)
    pieces = wide.reshape(depth_cells, AP_ROWS, TILE, AP_COLS + 1, TILE)
    pieces = pieces.transpose(1, 3, 0, 2, 4).reshape(
        AP_ROWS * (AP_COLS + 1), depth_cells, TILE * TILE
    )
    owners = jnp.arange(groups, dtype=jnp.int32)[:, None]
    block_row, block_col, usable = slot_layout(
        row_start, col_start, owners // own_cols, owners % own_cols, own_cols, caps
    )
    position = jnp.clip(block_row * (AP_COLS + 1) + block_col, 0, AP_ROWS * (AP_COLS + 1) - 1)
    return jnp.where(usable[..., None, None], pieces[position], 0.0)


def shift_rows(c, k, rows):
    if k > 0:
        moved = pltpu.roll(c, AX - k, 0)
        return jnp.where(rows < AX - k, moved, 0.0)
    moved = pltpu.roll(c, -k, 0)
    return jnp.where(rows >= -k, moved, 0.0)


def shift_lanes(c, k, lanes):
    if k > 0:
        moved = pltpu.roll(c, AY - k, 1)
        return jnp.where(lanes < AY - k, moved, 0.0)
    moved = pltpu.roll(c, -k, 1)
    return jnp.where(lanes >= -k, moved, 0.0)


def plane_stencil(buf, r, p, rows, lanes):
    c = buf[r, p]
    summed = (3.0 * COEFFS[0]) * c
    for k in range(1, 5):
        nearby = buf[r, p + k] + buf[r, p - k]
        nearby = nearby + shift_rows(c, k, rows)
        nearby = nearby + shift_rows(c, -k, rows)
        nearby = nearby + shift_lanes(c, k, lanes)
        nearby = nearby + shift_lanes(c, -k, lanes)
        summed = summed + COEFFS[k] * nearby
    return summed


def migrate_kernel(model_ref, pf_ref, qa_ref, inj_ref, img_ref, pad_p, pad_q, lap, qs, send_sem, recv_sem):
    me = lax.axis_index("sub")
    n_sub = lax.axis_size("sub")
    depth = model_ref.shape[0]
    halo = jnp.zeros((RADIUS, AX, AY), jnp.float32)
    for r in range(NT):
        for buf in (pad_p, pad_q):
            buf[r, 0:RADIUS] = halo
            buf[r, RADIUS + depth : 2 * RADIUS + depth] = halo
    pad_p[0, RADIUS : RADIUS + depth] = pf_ref[0]
    pad_q[0, RADIUS : RADIUS + depth] = model_ref[...] * qa_ref[0]
    up_dev = lax.rem(me + 1, n_sub)
    down_dev = lax.rem(me + n_sub - 1, n_sub)
    barrier = pltpu.get_barrier_semaphore()
    pl.semaphore_signal(barrier, 1, device_id={"sub": up_dev}, device_id_type=pl.DeviceIdType.MESH)
    pl.semaphore_signal(barrier, 1, device_id={"sub": down_dev}, device_id_type=pl.DeviceIdType.MESH)
    pl.semaphore_wait(barrier, 2)
    rows = lax.broadcasted_iota(jnp.int32, (AX, AY), 0)
    lanes = lax.broadcasted_iota(jnp.int32, (AX, AY), 1)

    def exchange(r):
        descs = []
        for f, buf in enumerate((pad_p, pad_q)):
            down = pltpu.make_async_remote_copy(
                src_ref=buf.at[r, RADIUS : 2 * RADIUS],
                dst_ref=buf.at[r, RADIUS + depth : 2 * RADIUS + depth],
                send_sem=send_sem.at[r, f, 0],
                recv_sem=recv_sem.at[r, f, 0],
                device_id={"sub": down_dev},
                device_id_type=pl.DeviceIdType.MESH,
            )
            up = pltpu.make_async_remote_copy(
                src_ref=buf.at[r, depth : RADIUS + depth],
                dst_ref=buf.at[r, 0:RADIUS],
                send_sem=send_sem.at[r, f, 1],
                recv_sem=recv_sem.at[r, f, 1],
                device_id={"sub": up_dev},
                device_id_type=pl.DeviceIdType.MESH,
            )
            descs.append((down, up))

        @pl.when(me > 0)
        def _():
            for down, up in descs:
                down.start()

        @pl.when(me < n_sub - 1)
        def _():
            for down, up in descs:
                up.start()

        @pl.when(me > 0)
        def _():
            for down, up in descs:
                down.wait_send()
                up.wait_recv()

        @pl.when(me < n_sub - 1)
        def _():
            for down, up in descs:
                up.wait_send()
                down.wait_recv()

    for r in range(NT):
        exchange(r)

        def plane(j, carry, r=r):
            p = j + RADIUS
            lp = plane_stencil(pad_p, r, p, rows, lanes)
            lap[r, j] = lp
            if r < NT - 1:
                before = pf_ref[1, j] if r == 0 else pad_p[r - 1, p]
                following = 2.0 * pad_p[r, p] - before + model_ref[j] * lp
                pad_p[r + 1, p] = following + inj_ref[r, j]
            lq = plane_stencil(pad_q, r, p, rows, lanes)
            now = qa_ref[0, j] if r == 0 else qs[r - 1, j]
            if r == 0:
                later = qa_ref[1, j]
            elif r == 1:
                later = qa_ref[0, j]
            else:
                later = qs[r - 2, j]
            result = 2.0 * now - later + lq
            result = result + inj_ref[NT - 1 + NT - 1 - r, j]
            qs[r, j] = result
            if r < NT - 1:
                pad_q[r + 1, p] = model_ref[j] * result
            return carry

        lax.fori_loop(0, depth, plane, 0)

    def image_plane(j, carry):
        image = jnp.zeros((AX, AY), jnp.float32)
        for r in range(NT):
            image = image + qs[r, j] * lap[NT - 1 - r, j]
        img_ref[j] = IMAGE_SCALE * image
        return carry

    lax.fori_loop(0, depth, image_plane, 0)


def migrate(model, state_fwd, state_adj, wave, source, receivers, resid):
    depth_cells = model.shape[0]
    plane = AX * AY
    block = depth_cells * plane
    offset = lax.axis_index("sub") * depth_cells
    slots = 2 * NT - 1

    def local(cells, slot):
        level = cells // plane - offset
        inside = (level >= 0) & (level < depth_cells)
        target = slot * block + level * plane + cells % plane
        return jnp.where(inside, target, slots * block)

    src_idx = jnp.stack([local(source, n) for n in range(NT - 1)])
    rcv_idx = jnp.concatenate([local(receivers, NT - 1 + n) for n in range(NT)])
    idx = jnp.concatenate([src_idx, rcv_idx])
    vals = jnp.concatenate([wave[: NT - 1], resid.reshape(-1)])
    inj = jnp.zeros((slots * block,), jnp.float32).at[idx].add(vals, mode="drop")
    inj = inj.reshape(slots, depth_cells, AX, AY)
    vmem = pl.BlockSpec(memory_space=pltpu.VMEM)
    padded = (NT, depth_cells + 2 * RADIUS, AX, AY)
    return pl.pallas_call(
        migrate_kernel,
        out_shape=jax.ShapeDtypeStruct(model.shape, jnp.float32),
        in_specs=[vmem] * 4,
        out_specs=vmem,
        scratch_shapes=[
            pltpu.VMEM(padded, jnp.float32),
            pltpu.VMEM(padded, jnp.float32),
            pltpu.VMEM((NT, depth_cells, AX, AY), jnp.float32),
            pltpu.VMEM((NT, depth_cells, AX, AY), jnp.float32),
            pltpu.SemaphoreType.DMA((NT, 2, 2)),
            pltpu.SemaphoreType.DMA((NT, 2, 2)),
        ],
        compiler_params=pltpu.CompilerParams(collective_id=0, has_side_effects=True),
    )(model, state_fwd.astype(jnp.float32), state_adj.astype(jnp.float32), inj)


def body(
    velocity_tiles,
    forward_state,
    adjoint_state,
    wavelet,
    source_cell,
    receiver_cell,
    residual,
    aperture_row,
    aperture_col,
):
    groups = lax.axis_size("shot")
    own_cols = groups // AP_ROWS
    caps = (AP_COLS + own_cols) // own_cols
    myself = lax.axis_index("shot")
    shots_here = forward_state.shape[0]
    gradient = jnp.zeros(velocity_tiles.shape, jnp.float32)
    every_shot = list(range(shots_here))
    sending = outgoing(
        velocity_tiles, aperture_row, aperture_col, every_shot, groups, own_cols, caps
    )
    fetched = lax.all_to_all(sending, "shot", split_axis=0, concat_axis=0, tiled=True)
    images = []
    for k in every_shot:
        slot_base = k * caps
        shot_id = myself * SHOTS_DEV + k
        row_start = aperture_row[shot_id]
        col_start = aperture_col[shot_id]
        model = assemble(fetched, slot_base, row_start, col_start, own_cols)
        image = migrate(
            model,
            forward_state[k],
            adjoint_state[k],
            wavelet[k],
            source_cell[k],
            receiver_cell[k],
            residual[k],
        )
        images.append(disperse(image, row_start, col_start, groups, own_cols, caps))
    returned = lax.all_to_all(images[0], "shot", split_axis=0, concat_axis=0, tiled=True)
    gradient = accumulate(
        gradient, returned, aperture_row, aperture_col, every_shot, groups, own_cols, caps
    )
    return gradient


def solution(mesh):
    placed = (
        P("shot", "sub", None),
        P("shot", None, "sub", None, None),
        P("shot", None, "sub", None, None),
        P("shot", None),
        P("shot"),
        P("shot", None),
        P("shot", None, None),
        P(),
        P(),
    )
    return jax.shard_map(
        body, mesh=mesh, in_specs=placed, out_specs=P("shot", "sub", None), check_vma=False
    )
```

```python
import jax
import jax.numpy as jnp
from jax import lax
from jax.sharding import PartitionSpec as P
from jax.experimental import pallas as pl
from jax.experimental.pallas import tpu as pltpu

TILE = 16
RY = 3
SHOTS_DEV = 1
NT = 4
RADIUS = 4
AP_ROWS = 4
AP_COLS = 8
TILE_DEV = 12
AX = 64
AY = 128


COEFFS = (-205.0 / 72.0, 8.0 / 5.0, -1.0 / 5.0, 8.0 / 315.0, -1.0 / 560.0)
IMAGE_SCALE = 1.0 / 64.0


def padded_2(array, sides, width):
    for axis, dim in sides:
        size, length = (lax.axis_size(axis), array.shape[dim])
        up = [(i, (i + 1) % size) for i in range(size - 1)]
        down = [(j, i) for i, j in up]
        last = lax.slice_in_dim(array, length - width, length, axis=dim)
        first = lax.slice_in_dim(array, 0, width, axis=dim)
        before = lax.ppermute(last, axis, up)
        after = lax.ppermute(first, axis, down)
        array = jnp.concatenate([before, array, after], axis=dim)
    return array


def laplace(padded, depth_cells, row_cells, column_cells):
    r = 4
    center = padded[r : r + depth_cells, r : r + row_cells, r : r + column_cells]
    summed = 3.0 * COEFFS[0] * center
    for k in range(1, 5):
        nearby = padded[r + k : r + k + depth_cells, r : r + row_cells, r : r + column_cells]
        nearby = (
            nearby + padded[r - k : r - k + depth_cells, r : r + row_cells, r : r + column_cells]
        )
        nearby = (
            nearby + padded[r : r + depth_cells, r + k : r + k + row_cells, r : r + column_cells]
        )
        nearby = (
            nearby + padded[r : r + depth_cells, r - k : r - k + row_cells, r : r + column_cells]
        )
        nearby = (
            nearby + padded[r : r + depth_cells, r : r + row_cells, r + k : r + k + column_cells]
        )
        nearby = (
            nearby + padded[r : r + depth_cells, r : r + row_cells, r - k : r - k + column_cells]
        )
        summed = summed + COEFFS[k] * nearby
    return summed


def wave_operator(field):
    padded = padded_2(field, (("sub", 0),), RADIUS)
    padded = jnp.pad(padded, ((0, 0), (4, 4), (4, 4)))
    return laplace(padded, field.shape[0], AX, AY)


def adjoint_operator(field):
    padded = padded_2(field, (("sub", 0),), RADIUS)
    padded = jnp.pad(padded, ((0, 0), (4, 4), (4, 4)))
    return laplace(padded, field.shape[0], AX, AY)


def slot_layout(row_start, col_start, owner_row, owner_col, own_cols, caps):
    block_row = (owner_row - row_start) % AP_ROWS
    first_col = (owner_col - col_start // TILE) % own_cols
    block_col = first_col + own_cols * jnp.arange(caps, dtype=jnp.int32)
    usable = block_col <= AP_COLS
    return (block_row, block_col, usable)


def owner_slots(row_table, col_table, shot_list, groups, own_cols, caps):
    myself = lax.axis_index("shot")
    owner_row = myself // own_cols
    owner_col = myself % own_cols
    senders = jnp.arange(groups, dtype=jnp.int32)[:, None]
    if SHOTS_DEV == 1 and list(shot_list) == [0]:
        row_start = row_table[:groups].reshape(groups, 1, 1)
        col_start = col_table[:groups].reshape(groups, 1, 1)
    else:
        picked = senders * SHOTS_DEV + jnp.asarray(shot_list, dtype=jnp.int32)[None, :]
        row_start = row_table[picked][..., None]
        col_start = col_table[picked][..., None]
    block_row, block_col, usable = slot_layout(
        row_start, col_start, owner_row, owner_col, own_cols, caps
    )
    tile_row = row_start + block_row
    tile_col = col_start // TILE + block_col
    local = tile_row // AP_ROWS * RY + tile_col // own_cols
    local = jnp.clip(local, 0, TILE_DEV - 1)
    return (local.reshape(-1), usable.reshape(-1))


def outgoing(velocity_tiles, row_table, col_table, shot_list, groups, own_cols, caps):
    local, usable = owner_slots(row_table, col_table, shot_list, groups, own_cols, caps)
    chosen = velocity_tiles[local]
    chosen = jnp.where(usable[:, None, None], chosen, 0.0)
    return chosen.reshape(
        groups, len(shot_list) * caps, velocity_tiles.shape[1], velocity_tiles.shape[2]
    )


def accumulate(gradient, returned, row_table, col_table, shot_list, groups, own_cols, caps):
    local, usable = owner_slots(row_table, col_table, shot_list, groups, own_cols, caps)
    pieces = returned.reshape(local.shape[0], -1)
    hot = (local[:, None] == jnp.arange(gradient.shape[0], dtype=jnp.int32)[None, :]) & usable[:, None]
    summed = jnp.einsum(
        "st,sf->tf", hot.astype(jnp.float32), pieces, precision=lax.Precision.HIGHEST
    )
    return gradient + summed.reshape(gradient.shape)


def assemble(received, slot_base, row_start, col_start, own_cols):
    depth_cells = received.shape[2]
    slot_count = received.shape[1]
    rel_row = jnp.arange(AP_ROWS, dtype=jnp.int32)[:, None]
    rel_col = jnp.arange(AP_COLS + 1, dtype=jnp.int32)[None, :]
    source_owner = (row_start + rel_row) % AP_ROWS * own_cols + (
        col_start // TILE + rel_col
    ) % own_cols
    flat_index = (source_owner * slot_count + slot_base + rel_col // own_cols).reshape(-1)
    pieces = received.reshape(-1, depth_cells, TILE * TILE)[flat_index]
    block = pieces.reshape(AP_ROWS, AP_COLS + 1, depth_cells, TILE, TILE)
    block = block.transpose(2, 0, 3, 1, 4).reshape(depth_cells, AX, (AP_COLS + 1) * TILE)
    return lax.dynamic_slice_in_dim(block, col_start % TILE, AY, 2)


def disperse(image, row_start, col_start, groups, own_cols, caps):
    depth_cells = image.shape[0]
    wide = jnp.zeros((depth_cells, AX, (AP_COLS + 1) * TILE), jnp.float32)
    wide = lax.dynamic_update_slice_in_dim(wide, image, col_start % TILE, 2)
    pieces = wide.reshape(depth_cells, AP_ROWS, TILE, AP_COLS + 1, TILE)
    pieces = pieces.transpose(1, 3, 0, 2, 4).reshape(
        AP_ROWS * (AP_COLS + 1), depth_cells, TILE * TILE
    )
    owners = jnp.arange(groups, dtype=jnp.int32)[:, None]
    block_row, block_col, usable = slot_layout(
        row_start, col_start, owners // own_cols, owners % own_cols, own_cols, caps
    )
    position = jnp.clip(block_row * (AP_COLS + 1) + block_col, 0, AP_ROWS * (AP_COLS + 1) - 1)
    return jnp.where(usable[..., None, None], pieces[position], 0.0)


def shift_rows(c, k, rows):
    if k > 0:
        moved = pltpu.roll(c, AX - k, 0)
        return jnp.where(rows < AX - k, moved, 0.0)
    moved = pltpu.roll(c, -k, 0)
    return jnp.where(rows >= -k, moved, 0.0)


def shift_lanes(c, k, lanes):
    if k > 0:
        moved = pltpu.roll(c, AY - k, 1)
        return jnp.where(lanes < AY - k, moved, 0.0)
    moved = pltpu.roll(c, -k, 1)
    return jnp.where(lanes >= -k, moved, 0.0)


def plane_stencil(buf, r, p, rows, lanes):
    c = buf[r, p]
    summed = (3.0 * COEFFS[0]) * c
    for k in range(1, 5):
        nearby = buf[r, p + k] + buf[r, p - k]
        nearby = nearby + shift_rows(c, k, rows)
        nearby = nearby + shift_rows(c, -k, rows)
        nearby = nearby + shift_lanes(c, k, lanes)
        nearby = nearby + shift_lanes(c, -k, lanes)
        summed = summed + COEFFS[k] * nearby
    return summed


def split_bf16(values):
    high = values.astype(jnp.bfloat16)
    rest = values - high.astype(jnp.float32)
    middle = rest.astype(jnp.bfloat16)
    low = (rest - middle.astype(jnp.float32)).astype(jnp.bfloat16)
    return (high, middle, low)


def migrate_kernel(
    src_ref, wave_ref, rrow_ref, rcol_ref, resid_ref, model_ref, pf_ref, qa_ref,
    img_ref, pad_p, pad_q, lap, qs, inject, send_sem, recv_sem,
):
    me = lax.axis_index("sub")
    n_sub = lax.axis_size("sub")
    depth = model_ref.shape[0]
    halo = jnp.zeros((RADIUS, AX, AY), jnp.float32)
    for r in range(NT):
        for buf in (pad_p, pad_q):
            buf[r, 0:RADIUS] = halo
            buf[r, RADIUS + depth : 2 * RADIUS + depth] = halo
    pad_p[0, RADIUS : RADIUS + depth] = pf_ref[0]
    pad_q[0, RADIUS : RADIUS + depth] = model_ref[...] * qa_ref[0]
    up_dev = lax.rem(me + 1, n_sub)
    down_dev = lax.rem(me + n_sub - 1, n_sub)
    barrier = pltpu.get_barrier_semaphore()
    pl.semaphore_signal(barrier, 1, device_id={"sub": up_dev}, device_id_type=pl.DeviceIdType.MESH)
    pl.semaphore_signal(barrier, 1, device_id={"sub": down_dev}, device_id_type=pl.DeviceIdType.MESH)
    pl.semaphore_wait(barrier, 2)
    rows = lax.broadcasted_iota(jnp.int32, (AX, AY), 0)
    lanes = lax.broadcasted_iota(jnp.int32, (AX, AY), 1)
    n_rec = rcol_ref.shape[0]
    src_level = src_ref[0]
    src_spot = (rows == src_ref[1]) & (lanes == src_ref[2])

    def build_injection(step):
        hit_y = lax.broadcasted_iota(jnp.int32, (n_rec, AY), 1) == rcol_ref[...]
        spread = jnp.where(hit_y, resid_ref[:, step : step + 1], 0.0)
        parts = split_bf16(spread)
        rec_level = rrow_ref[0:1, :]
        hit_x = lax.broadcasted_iota(jnp.int32, (AX, n_rec), 0) == rrow_ref[1:2, :]

        def plane(j, carry):
            picks = (hit_x & (rec_level == j)).astype(jnp.bfloat16)
            total = jnp.dot(picks, parts[0], preferred_element_type=jnp.float32)
            total = total + jnp.dot(picks, parts[1], preferred_element_type=jnp.float32)
            total = total + jnp.dot(picks, parts[2], preferred_element_type=jnp.float32)
            inject[j] = total
            return carry

        lax.fori_loop(0, depth, plane, 0)

    def exchange(r):
        descs = []
        for f, buf in enumerate((pad_p, pad_q)):
            down = pltpu.make_async_remote_copy(
                src_ref=buf.at[r, RADIUS : 2 * RADIUS],
                dst_ref=buf.at[r, RADIUS + depth : 2 * RADIUS + depth],
                send_sem=send_sem.at[r, f, 0],
                recv_sem=recv_sem.at[r, f, 0],
                device_id={"sub": down_dev},
                device_id_type=pl.DeviceIdType.MESH,
            )
            up = pltpu.make_async_remote_copy(
                src_ref=buf.at[r, depth : RADIUS + depth],
                dst_ref=buf.at[r, 0:RADIUS],
                send_sem=send_sem.at[r, f, 1],
                recv_sem=recv_sem.at[r, f, 1],
                device_id={"sub": up_dev},
                device_id_type=pl.DeviceIdType.MESH,
            )
            descs.append((down, up))

        @pl.when(me > 0)
        def _():
            for down, up in descs:
                down.start()

        @pl.when(me < n_sub - 1)
        def _():
            for down, up in descs:
                up.start()

        return descs

    def finish(descs):
        @pl.when(me > 0)
        def _():
            for down, up in descs:
                down.wait_send()
                up.wait_recv()

        @pl.when(me < n_sub - 1)
        def _():
            for down, up in descs:
                up.wait_send()
                down.wait_recv()

    for r in range(NT):
        descs = exchange(r)
        build_injection(NT - 1 - r)
        finish(descs)

        def plane(j, carry, r=r):
            p = j + RADIUS
            lp = plane_stencil(pad_p, r, p, rows, lanes)
            lap[r, j] = lp
            if r < NT - 1:
                before = pf_ref[1, j] if r == 0 else pad_p[r - 1, p]
                following = 2.0 * pad_p[r, p] - before + model_ref[j] * lp
                source = jnp.where(src_spot & (src_level == j), wave_ref[r], 0.0)
                pad_p[r + 1, p] = following + source
            lq = plane_stencil(pad_q, r, p, rows, lanes)
            now = qa_ref[0, j] if r == 0 else qs[r - 1, j]
            if r == 0:
                later = qa_ref[1, j]
            elif r == 1:
                later = qa_ref[0, j]
            else:
                later = qs[r - 2, j]
            result = 2.0 * now - later + lq
            result = result + inject[j]
            qs[r, j] = result
            if r < NT - 1:
                pad_q[r + 1, p] = model_ref[j] * result
            return carry

        lax.fori_loop(0, depth, plane, 0)

    def image_plane(j, carry):
        image = jnp.zeros((AX, AY), jnp.float32)
        for r in range(NT):
            image = image + qs[r, j] * lap[NT - 1 - r, j]
        img_ref[j] = IMAGE_SCALE * image
        return carry

    lax.fori_loop(0, depth, image_plane, 0)


def migrate(model, state_fwd, state_adj, wave, source, receivers, resid):
    depth_cells = model.shape[0]
    plane = AX * AY
    offset = lax.axis_index("sub") * depth_cells

    def level_of(cells):
        level = cells // plane - offset
        inside = (level >= 0) & (level < depth_cells)
        return jnp.where(inside, level, -1)

    src = jnp.stack([level_of(source), source % plane // AY, source % AY]).astype(jnp.int32)
    rrow = jnp.stack([level_of(receivers), receivers % plane // AY]).astype(jnp.int32)
    rcol = (receivers % AY).astype(jnp.int32).reshape(-1, 1)
    vmem = pl.BlockSpec(memory_space=pltpu.VMEM)
    smem = pl.BlockSpec(memory_space=pltpu.SMEM)
    padded = (NT, depth_cells + 2 * RADIUS, AX, AY)
    field = (NT, depth_cells, AX, AY)
    return pl.pallas_call(
        migrate_kernel,
        out_shape=jax.ShapeDtypeStruct(model.shape, jnp.float32),
        in_specs=[smem, smem] + [vmem] * 6,
        out_specs=vmem,
        scratch_shapes=[
            pltpu.VMEM(padded, jnp.float32),
            pltpu.VMEM(padded, jnp.float32),
            pltpu.VMEM(field, jnp.float32),
            pltpu.VMEM(field, jnp.float32),
            pltpu.VMEM(model.shape, jnp.float32),
            pltpu.SemaphoreType.DMA((NT, 2, 2)),
            pltpu.SemaphoreType.DMA((NT, 2, 2)),
        ],
        compiler_params=pltpu.CompilerParams(collective_id=0, has_side_effects=True),
    )(
        src,
        wave.astype(jnp.float32),
        rrow,
        rcol,
        resid.T,
        model,
        state_fwd.astype(jnp.float32),
        state_adj.astype(jnp.float32),
    )


def body(
    velocity_tiles,
    forward_state,
    adjoint_state,
    wavelet,
    source_cell,
    receiver_cell,
    residual,
    aperture_row,
    aperture_col,
):
    groups = lax.axis_size("shot")
    own_cols = groups // AP_ROWS
    caps = (AP_COLS + own_cols) // own_cols
    myself = lax.axis_index("shot")
    shots_here = forward_state.shape[0]
    gradient = jnp.zeros(velocity_tiles.shape, jnp.float32)
    every_shot = list(range(shots_here))
    sending = outgoing(
        velocity_tiles, aperture_row, aperture_col, every_shot, groups, own_cols, caps
    )
    fetched = lax.all_to_all(sending, "shot", split_axis=0, concat_axis=0, tiled=True)
    images = []
    for k in every_shot:
        slot_base = k * caps
        shot_id = myself * SHOTS_DEV + k
        row_start = aperture_row[shot_id]
        col_start = aperture_col[shot_id]
        model = assemble(fetched, slot_base, row_start, col_start, own_cols)
        image = migrate(
            model,
            forward_state[k],
            adjoint_state[k],
            wavelet[k],
            source_cell[k],
            receiver_cell[k],
            residual[k],
        )
        images.append(disperse(image, row_start, col_start, groups, own_cols, caps))
    returned = lax.all_to_all(images[0], "shot", split_axis=0, concat_axis=0, tiled=True)
    gradient = accumulate(
        gradient, returned, aperture_row, aperture_col, every_shot, groups, own_cols, caps
    )
    return gradient


def solution(mesh):
    placed = (
        P("shot", "sub", None),
        P("shot", None, "sub", None, None),
        P("shot", None, "sub", None, None),
        P("shot", None),
        P("shot"),
        P("shot", None),
        P("shot", None, None),
        P(),
        P(),
    )
    return jax.shard_map(
        body, mesh=mesh, in_specs=placed, out_specs=P("shot", "sub", None), check_vma=False
    )
```

```python
import jax
import jax.numpy as jnp
from jax import lax
from jax.sharding import PartitionSpec as P
from jax.experimental import pallas as pl
from jax.experimental.pallas import tpu as pltpu

TILE = 16
RY = 3
SHOTS_DEV = 1
NT = 4
RADIUS = 4
AP_ROWS = 4
AP_COLS = 8
TILE_DEV = 12
AX = 64
AY = 128


COEFFS = (-205.0 / 72.0, 8.0 / 5.0, -1.0 / 5.0, 8.0 / 315.0, -1.0 / 560.0)
IMAGE_SCALE = 1.0 / 64.0


def padded_2(array, sides, width):
    for axis, dim in sides:
        size, length = (lax.axis_size(axis), array.shape[dim])
        up = [(i, (i + 1) % size) for i in range(size - 1)]
        down = [(j, i) for i, j in up]
        last = lax.slice_in_dim(array, length - width, length, axis=dim)
        first = lax.slice_in_dim(array, 0, width, axis=dim)
        before = lax.ppermute(last, axis, up)
        after = lax.ppermute(first, axis, down)
        array = jnp.concatenate([before, array, after], axis=dim)
    return array


def laplace(padded, depth_cells, row_cells, column_cells):
    r = 4
    center = padded[r : r + depth_cells, r : r + row_cells, r : r + column_cells]
    summed = 3.0 * COEFFS[0] * center
    for k in range(1, 5):
        nearby = padded[r + k : r + k + depth_cells, r : r + row_cells, r : r + column_cells]
        nearby = (
            nearby + padded[r - k : r - k + depth_cells, r : r + row_cells, r : r + column_cells]
        )
        nearby = (
            nearby + padded[r : r + depth_cells, r + k : r + k + row_cells, r : r + column_cells]
        )
        nearby = (
            nearby + padded[r : r + depth_cells, r - k : r - k + row_cells, r : r + column_cells]
        )
        nearby = (
            nearby + padded[r : r + depth_cells, r : r + row_cells, r + k : r + k + column_cells]
        )
        nearby = (
            nearby + padded[r : r + depth_cells, r : r + row_cells, r - k : r - k + column_cells]
        )
        summed = summed + COEFFS[k] * nearby
    return summed


def wave_operator(field):
    padded = padded_2(field, (("sub", 0),), RADIUS)
    padded = jnp.pad(padded, ((0, 0), (4, 4), (4, 4)))
    return laplace(padded, field.shape[0], AX, AY)


def adjoint_operator(field):
    padded = padded_2(field, (("sub", 0),), RADIUS)
    padded = jnp.pad(padded, ((0, 0), (4, 4), (4, 4)))
    return laplace(padded, field.shape[0], AX, AY)


def slot_layout(row_start, col_start, owner_row, owner_col, own_cols, caps):
    block_row = (owner_row - row_start) % AP_ROWS
    first_col = (owner_col - col_start // TILE) % own_cols
    block_col = first_col + own_cols * jnp.arange(caps, dtype=jnp.int32)
    usable = block_col <= AP_COLS
    return (block_row, block_col, usable)


def owner_slots(row_table, col_table, shot_list, groups, own_cols, caps):
    myself = lax.axis_index("shot")
    owner_row = myself // own_cols
    owner_col = myself % own_cols
    senders = jnp.arange(groups, dtype=jnp.int32)[:, None]
    if SHOTS_DEV == 1 and list(shot_list) == [0]:
        row_start = row_table[:groups].reshape(groups, 1, 1)
        col_start = col_table[:groups].reshape(groups, 1, 1)
    else:
        picked = senders * SHOTS_DEV + jnp.asarray(shot_list, dtype=jnp.int32)[None, :]
        row_start = row_table[picked][..., None]
        col_start = col_table[picked][..., None]
    block_row, block_col, usable = slot_layout(
        row_start, col_start, owner_row, owner_col, own_cols, caps
    )
    tile_row = row_start + block_row
    tile_col = col_start // TILE + block_col
    local = tile_row // AP_ROWS * RY + tile_col // own_cols
    local = jnp.clip(local, 0, TILE_DEV - 1)
    return (local.reshape(-1), usable.reshape(-1))


def outgoing(velocity_tiles, row_table, col_table, shot_list, groups, own_cols, caps):
    local, usable = owner_slots(row_table, col_table, shot_list, groups, own_cols, caps)
    chosen = velocity_tiles[local]
    chosen = jnp.where(usable[:, None, None], chosen, 0.0)
    return chosen.reshape(
        groups, len(shot_list) * caps, velocity_tiles.shape[1], velocity_tiles.shape[2]
    )


def accumulate(gradient, returned, row_table, col_table, shot_list, groups, own_cols, caps):
    local, usable = owner_slots(row_table, col_table, shot_list, groups, own_cols, caps)
    pieces = returned.reshape(local.shape[0], -1)
    hot = (local[:, None] == jnp.arange(gradient.shape[0], dtype=jnp.int32)[None, :]) & usable[:, None]
    summed = jnp.einsum(
        "st,sf->tf", hot.astype(jnp.float32), pieces, precision=lax.Precision.HIGHEST
    )
    return gradient + summed.reshape(gradient.shape)


def assemble(received, slot_base, row_start, col_start, own_cols):
    depth_cells = received.shape[2]
    slot_count = received.shape[1]
    rel_row = jnp.arange(AP_ROWS, dtype=jnp.int32)[:, None]
    rel_col = jnp.arange(AP_COLS + 1, dtype=jnp.int32)[None, :]
    source_owner = (row_start + rel_row) % AP_ROWS * own_cols + (
        col_start // TILE + rel_col
    ) % own_cols
    flat_index = (source_owner * slot_count + slot_base + rel_col // own_cols).reshape(-1)
    pieces = received.reshape(-1, depth_cells, TILE * TILE)[flat_index]
    block = pieces.reshape(AP_ROWS, AP_COLS + 1, depth_cells, TILE, TILE)
    block = block.transpose(2, 0, 3, 1, 4).reshape(depth_cells, AX, (AP_COLS + 1) * TILE)
    return lax.dynamic_slice_in_dim(block, col_start % TILE, AY, 2)


def disperse(image, row_start, col_start, groups, own_cols, caps):
    depth_cells = image.shape[0]
    wide = jnp.zeros((depth_cells, AX, (AP_COLS + 1) * TILE), jnp.float32)
    wide = lax.dynamic_update_slice_in_dim(wide, image, col_start % TILE, 2)
    pieces = wide.reshape(depth_cells, AP_ROWS, TILE, AP_COLS + 1, TILE)
    pieces = pieces.transpose(1, 3, 0, 2, 4).reshape(
        AP_ROWS * (AP_COLS + 1), depth_cells, TILE * TILE
    )
    owners = jnp.arange(groups, dtype=jnp.int32)[:, None]
    block_row, block_col, usable = slot_layout(
        row_start, col_start, owners // own_cols, owners % own_cols, own_cols, caps
    )
    position = jnp.clip(block_row * (AP_COLS + 1) + block_col, 0, AP_ROWS * (AP_COLS + 1) - 1)
    return jnp.where(usable[..., None, None], pieces[position], 0.0)


def shift_rows(c, k, rows):
    if k > 0:
        moved = pltpu.roll(c, AX - k, 0)
        return jnp.where(rows < AX - k, moved, 0.0)
    moved = pltpu.roll(c, -k, 0)
    return jnp.where(rows >= -k, moved, 0.0)


def shift_lanes(c, k, lanes):
    if k > 0:
        moved = pltpu.roll(c, AY - k, 1)
        return jnp.where(lanes < AY - k, moved, 0.0)
    moved = pltpu.roll(c, -k, 1)
    return jnp.where(lanes >= -k, moved, 0.0)


def plane_stencil(buf, r, p, rows, lanes):
    c = buf[r, p]
    summed = (3.0 * COEFFS[0]) * c
    for k in range(1, 5):
        nearby = buf[r, p + k] + buf[r, p - k]
        nearby = nearby + shift_rows(c, k, rows)
        nearby = nearby + shift_rows(c, -k, rows)
        nearby = nearby + shift_lanes(c, k, lanes)
        nearby = nearby + shift_lanes(c, -k, lanes)
        summed = summed + COEFFS[k] * nearby
    return summed


def split_bf16(values):
    high = values.astype(jnp.bfloat16)
    rest = values - high.astype(jnp.float32)
    middle = rest.astype(jnp.bfloat16)
    low = (rest - middle.astype(jnp.float32)).astype(jnp.bfloat16)
    return (high, middle, low)


def migrate_kernel(
    src_ref, wave_ref, rrow_ref, rcol_ref, resid_ref, model_ref, pf_ref, qa_ref,
    img_ref, pad_p, pad_q, lap, qs, inject, send_sem, recv_sem,
):
    me = lax.axis_index("sub")
    n_sub = lax.axis_size("sub")
    depth = model_ref.shape[0]
    halo = jnp.zeros((RADIUS, AX, AY), jnp.float32)
    for r in range(NT):
        for buf in (pad_p, pad_q):
            buf[r, 0:RADIUS] = halo
            buf[r, RADIUS + depth : 2 * RADIUS + depth] = halo
    pad_p[0, RADIUS : RADIUS + depth] = pf_ref[0]
    pad_q[0, RADIUS : RADIUS + depth] = model_ref[...] * qa_ref[0]
    up_dev = lax.rem(me + 1, n_sub)
    down_dev = lax.rem(me + n_sub - 1, n_sub)
    barrier = pltpu.get_barrier_semaphore()
    pl.semaphore_signal(barrier, 1, device_id={"sub": up_dev}, device_id_type=pl.DeviceIdType.MESH)
    pl.semaphore_signal(barrier, 1, device_id={"sub": down_dev}, device_id_type=pl.DeviceIdType.MESH)
    pl.semaphore_wait(barrier, 2)
    rows = lax.broadcasted_iota(jnp.int32, (AX, AY), 0)
    lanes = lax.broadcasted_iota(jnp.int32, (AX, AY), 1)
    n_rec = rcol_ref.shape[0]
    src_level = src_ref[0]
    src_spot = (rows == src_ref[1]) & (lanes == src_ref[2])

    def build_injection(step):
        hit_y = lax.broadcasted_iota(jnp.int32, (n_rec, AY), 1) == rcol_ref[...]
        spread = jnp.where(hit_y, resid_ref[:, step : step + 1], 0.0)
        parts = split_bf16(spread)
        rec_level = rrow_ref[0:1, :]
        hit_x = lax.broadcasted_iota(jnp.int32, (AX, n_rec), 0) == rrow_ref[1:2, :]

        def plane(j, carry):
            picks = (hit_x & (rec_level == j)).astype(jnp.bfloat16)
            total = jnp.dot(picks, parts[0], preferred_element_type=jnp.float32)
            total = total + jnp.dot(picks, parts[1], preferred_element_type=jnp.float32)
            total = total + jnp.dot(picks, parts[2], preferred_element_type=jnp.float32)
            inject[j] = total
            return carry

        lax.fori_loop(0, depth, plane, 0)

    def exchange(r, f):
        buf = (pad_p, pad_q)[f]
        down = pltpu.make_async_remote_copy(
            src_ref=buf.at[r, RADIUS : 2 * RADIUS],
            dst_ref=buf.at[r, RADIUS + depth : 2 * RADIUS + depth],
            send_sem=send_sem.at[r, f, 0],
            recv_sem=recv_sem.at[r, f, 0],
            device_id={"sub": down_dev},
            device_id_type=pl.DeviceIdType.MESH,
        )
        up = pltpu.make_async_remote_copy(
            src_ref=buf.at[r, depth : RADIUS + depth],
            dst_ref=buf.at[r, 0:RADIUS],
            send_sem=send_sem.at[r, f, 1],
            recv_sem=recv_sem.at[r, f, 1],
            device_id={"sub": up_dev},
            device_id_type=pl.DeviceIdType.MESH,
        )

        @pl.when(me > 0)
        def _():
            down.start()

        @pl.when(me < n_sub - 1)
        def _():
            up.start()

        return (down, up)

    def finish(pair):
        down, up = pair

        @pl.when(me > 0)
        def _():
            down.wait_send()
            up.wait_recv()

        @pl.when(me < n_sub - 1)
        def _():
            up.wait_send()
            down.wait_recv()

    def forward_round(r):
        def plane(j, carry):
            p = j + RADIUS
            lp = plane_stencil(pad_p, r, p, rows, lanes)
            lap[r, j] = lp
            if r < NT - 1:
                before = pf_ref[1, j] if r == 0 else pad_p[r - 1, p]
                following = 2.0 * pad_p[r, p] - before + model_ref[j] * lp
                source = jnp.where(src_spot & (src_level == j), wave_ref[r], 0.0)
                pad_p[r + 1, p] = following + source
            return carry

        lax.fori_loop(0, depth, plane, 0)

    def adjoint_round(r):
        def plane(j, carry):
            p = j + RADIUS
            lq = plane_stencil(pad_q, r, p, rows, lanes)
            now = qa_ref[0, j] if r == 0 else qs[r - 1, j]
            if r == 0:
                later = qa_ref[1, j]
            elif r == 1:
                later = qa_ref[0, j]
            else:
                later = qs[r - 2, j]
            result = 2.0 * now - later + lq
            result = result + inject[j]
            if r < NT - 1:
                qs[r, j] = result
                pad_q[r + 1, p] = model_ref[j] * result
            else:
                image = jnp.zeros((AX, AY), jnp.float32)
                for s in range(NT - 1):
                    image = image + qs[s, j] * lap[NT - 1 - s, j]
                image = image + result * lap[0, j]
                img_ref[j] = IMAGE_SCALE * image
            return carry

        lax.fori_loop(0, depth, plane, 0)

    fwd = exchange(0, 0)
    adj = exchange(0, 1)
    build_injection(NT - 1)
    for r in range(NT):
        finish(fwd)
        forward_round(r)
        if r < NT - 1:
            fwd = exchange(r + 1, 0)
        finish(adj)
        adjoint_round(r)
        if r < NT - 1:
            adj = exchange(r + 1, 1)
            build_injection(NT - 2 - r)


def migrate(model, state_fwd, state_adj, wave, source, receivers, resid):
    depth_cells = model.shape[0]
    plane = AX * AY
    offset = lax.axis_index("sub") * depth_cells

    def level_of(cells):
        level = cells // plane - offset
        inside = (level >= 0) & (level < depth_cells)
        return jnp.where(inside, level, -1)

    src = jnp.stack([level_of(source), source % plane // AY, source % AY]).astype(jnp.int32)
    rrow = jnp.stack([level_of(receivers), receivers % plane // AY]).astype(jnp.int32)
    rcol = (receivers % AY).astype(jnp.int32).reshape(-1, 1)
    vmem = pl.BlockSpec(memory_space=pltpu.VMEM)
    smem = pl.BlockSpec(memory_space=pltpu.SMEM)
    padded = (NT, depth_cells + 2 * RADIUS, AX, AY)
    field = (NT, depth_cells, AX, AY)
    return pl.pallas_call(
        migrate_kernel,
        out_shape=jax.ShapeDtypeStruct(model.shape, jnp.float32),
        in_specs=[smem, smem] + [vmem] * 6,
        out_specs=vmem,
        scratch_shapes=[
            pltpu.VMEM(padded, jnp.float32),
            pltpu.VMEM(padded, jnp.float32),
            pltpu.VMEM(field, jnp.float32),
            pltpu.VMEM(field, jnp.float32),
            pltpu.VMEM(model.shape, jnp.float32),
            pltpu.SemaphoreType.DMA((NT, 2, 2)),
            pltpu.SemaphoreType.DMA((NT, 2, 2)),
        ],
        compiler_params=pltpu.CompilerParams(collective_id=0, has_side_effects=True),
    )(
        src,
        wave.astype(jnp.float32),
        rrow,
        rcol,
        resid.T,
        model,
        state_fwd.astype(jnp.float32),
        state_adj.astype(jnp.float32),
    )


def body(
    velocity_tiles,
    forward_state,
    adjoint_state,
    wavelet,
    source_cell,
    receiver_cell,
    residual,
    aperture_row,
    aperture_col,
):
    groups = lax.axis_size("shot")
    own_cols = groups // AP_ROWS
    caps = (AP_COLS + own_cols) // own_cols
    myself = lax.axis_index("shot")
    shots_here = forward_state.shape[0]
    gradient = jnp.zeros(velocity_tiles.shape, jnp.float32)
    every_shot = list(range(shots_here))
    sending = outgoing(
        velocity_tiles, aperture_row, aperture_col, every_shot, groups, own_cols, caps
    )
    fetched = lax.all_to_all(sending, "shot", split_axis=0, concat_axis=0, tiled=True)
    images = []
    for k in every_shot:
        slot_base = k * caps
        shot_id = myself * SHOTS_DEV + k
        row_start = aperture_row[shot_id]
        col_start = aperture_col[shot_id]
        model = assemble(fetched, slot_base, row_start, col_start, own_cols)
        image = migrate(
            model,
            forward_state[k],
            adjoint_state[k],
            wavelet[k],
            source_cell[k],
            receiver_cell[k],
            residual[k],
        )
        images.append(disperse(image, row_start, col_start, groups, own_cols, caps))
    returned = lax.all_to_all(images[0], "shot", split_axis=0, concat_axis=0, tiled=True)
    gradient = accumulate(
        gradient, returned, aperture_row, aperture_col, every_shot, groups, own_cols, caps
    )
    return gradient


def solution(mesh):
    placed = (
        P("shot", "sub", None),
        P("shot", None, "sub", None, None),
        P("shot", None, "sub", None, None),
        P("shot", None),
        P("shot"),
        P("shot", None),
        P("shot", None, None),
        P(),
        P(),
    )
    return jax.shard_map(
        body, mesh=mesh, in_specs=placed, out_specs=P("shot", "sub", None), check_vma=False
    )
```

```python
import jax
import jax.numpy as jnp
from jax import lax
from jax.sharding import PartitionSpec as P
from jax.experimental import pallas as pl
from jax.experimental.pallas import tpu as pltpu

TILE = 16
RY = 3
SHOTS_DEV = 1
NT = 4
RADIUS = 4
AP_ROWS = 4
AP_COLS = 8
TILE_DEV = 12
AX = 64
AY = 128


COEFFS = (-205.0 / 72.0, 8.0 / 5.0, -1.0 / 5.0, 8.0 / 315.0, -1.0 / 560.0)
IMAGE_SCALE = 1.0 / 64.0


def padded_2(array, sides, width):
    for axis, dim in sides:
        size, length = (lax.axis_size(axis), array.shape[dim])
        up = [(i, (i + 1) % size) for i in range(size - 1)]
        down = [(j, i) for i, j in up]
        last = lax.slice_in_dim(array, length - width, length, axis=dim)
        first = lax.slice_in_dim(array, 0, width, axis=dim)
        before = lax.ppermute(last, axis, up)
        after = lax.ppermute(first, axis, down)
        array = jnp.concatenate([before, array, after], axis=dim)
    return array


def laplace(padded, depth_cells, row_cells, column_cells):
    r = 4
    center = padded[r : r + depth_cells, r : r + row_cells, r : r + column_cells]
    summed = 3.0 * COEFFS[0] * center
    for k in range(1, 5):
        nearby = padded[r + k : r + k + depth_cells, r : r + row_cells, r : r + column_cells]
        nearby = (
            nearby + padded[r - k : r - k + depth_cells, r : r + row_cells, r : r + column_cells]
        )
        nearby = (
            nearby + padded[r : r + depth_cells, r + k : r + k + row_cells, r : r + column_cells]
        )
        nearby = (
            nearby + padded[r : r + depth_cells, r - k : r - k + row_cells, r : r + column_cells]
        )
        nearby = (
            nearby + padded[r : r + depth_cells, r : r + row_cells, r + k : r + k + column_cells]
        )
        nearby = (
            nearby + padded[r : r + depth_cells, r : r + row_cells, r - k : r - k + column_cells]
        )
        summed = summed + COEFFS[k] * nearby
    return summed


def wave_operator(field):
    padded = padded_2(field, (("sub", 0),), RADIUS)
    padded = jnp.pad(padded, ((0, 0), (4, 4), (4, 4)))
    return laplace(padded, field.shape[0], AX, AY)


def adjoint_operator(field):
    padded = padded_2(field, (("sub", 0),), RADIUS)
    padded = jnp.pad(padded, ((0, 0), (4, 4), (4, 4)))
    return laplace(padded, field.shape[0], AX, AY)


def slot_layout(row_start, col_start, owner_row, owner_col, own_cols, caps):
    block_row = (owner_row - row_start) % AP_ROWS
    first_col = (owner_col - col_start // TILE) % own_cols
    block_col = first_col + own_cols * jnp.arange(caps, dtype=jnp.int32)
    usable = block_col <= AP_COLS
    return (block_row, block_col, usable)


def owner_slots(row_table, col_table, shot_list, groups, own_cols, caps):
    myself = lax.axis_index("shot")
    owner_row = myself // own_cols
    owner_col = myself % own_cols
    senders = jnp.arange(groups, dtype=jnp.int32)[:, None]
    if SHOTS_DEV == 1 and list(shot_list) == [0]:
        row_start = row_table[:groups].reshape(groups, 1, 1)
        col_start = col_table[:groups].reshape(groups, 1, 1)
    else:
        picked = senders * SHOTS_DEV + jnp.asarray(shot_list, dtype=jnp.int32)[None, :]
        row_start = row_table[picked][..., None]
        col_start = col_table[picked][..., None]
    block_row, block_col, usable = slot_layout(
        row_start, col_start, owner_row, owner_col, own_cols, caps
    )
    tile_row = row_start + block_row
    tile_col = col_start // TILE + block_col
    local = tile_row // AP_ROWS * RY + tile_col // own_cols
    local = jnp.clip(local, 0, TILE_DEV - 1)
    return (local.reshape(-1), usable.reshape(-1))


def lane_column():
    return jnp.arange(TILE * TILE, dtype=jnp.int32) % TILE


def merge_slots(pair, spare_ok, offset):
    lower = spare_ok & (lane_column() < offset)
    return jnp.where(lower, pair[:, 1], pair[:, 0])


def outgoing(velocity_tiles, row_table, col_table, shot_list, groups, own_cols, caps):
    local, usable = owner_slots(row_table, col_table, shot_list, groups, own_cols, caps)
    chosen = velocity_tiles[local]
    chosen = jnp.where(usable[:, None, None], chosen, 0.0)
    chosen = chosen.reshape(groups, caps, velocity_tiles.shape[1], velocity_tiles.shape[2])
    usable = usable.reshape(groups, caps)
    offset = (col_table[:groups] % TILE).reshape(groups, 1, 1)
    merged = merge_slots(chosen, usable[:, 1, None, None], offset)
    return merged.reshape(groups, 1, velocity_tiles.shape[1], velocity_tiles.shape[2])


def accumulate(gradient, returned, row_table, col_table, shot_list, groups, own_cols, caps):
    local, usable = owner_slots(row_table, col_table, shot_list, groups, own_cols, caps)
    usable = usable.reshape(groups, caps)
    offset = (col_table[:groups] % TILE).reshape(groups, 1, 1)
    lower = lane_column() < offset
    piece = returned.reshape(groups, gradient.shape[1], gradient.shape[2])
    spare = usable[:, 1, None, None]
    first = jnp.where(spare & lower, 0.0, piece)
    second = jnp.where(spare & lower, piece, 0.0)
    pieces = jnp.stack([first, second], axis=1).reshape(groups * caps, -1)
    hot = (local[:, None] == jnp.arange(gradient.shape[0], dtype=jnp.int32)[None, :]) & usable.reshape(-1)[:, None]
    summed = jnp.einsum(
        "st,sf->tf", hot.astype(jnp.float32), pieces, precision=lax.Precision.HIGHEST
    )
    return gradient + summed.reshape(gradient.shape)


def assemble(received, row_start, col_start, own_cols):
    depth_cells = received.shape[2]
    rel_row = jnp.arange(AP_ROWS, dtype=jnp.int32)[:, None]
    rel_col = jnp.arange(AP_COLS + 1, dtype=jnp.int32)[None, :]
    source_owner = (row_start + rel_row) % AP_ROWS * own_cols + (
        col_start // TILE + rel_col
    ) % own_cols
    flat_index = source_owner.reshape(-1)
    pieces = received.reshape(-1, depth_cells, TILE * TILE)[flat_index]
    block = pieces.reshape(AP_ROWS, AP_COLS + 1, depth_cells, TILE, TILE)
    block = block.transpose(2, 0, 3, 1, 4).reshape(depth_cells, AX, (AP_COLS + 1) * TILE)
    return lax.dynamic_slice_in_dim(block, col_start % TILE, AY, 2)


def disperse(image, row_start, col_start, groups, own_cols, caps):
    depth_cells = image.shape[0]
    wide = jnp.zeros((depth_cells, AX, (AP_COLS + 1) * TILE), jnp.float32)
    wide = lax.dynamic_update_slice_in_dim(wide, image, col_start % TILE, 2)
    pieces = wide.reshape(depth_cells, AP_ROWS, TILE, AP_COLS + 1, TILE)
    pieces = pieces.transpose(1, 3, 0, 2, 4).reshape(
        AP_ROWS * (AP_COLS + 1), depth_cells, TILE * TILE
    )
    owners = jnp.arange(groups, dtype=jnp.int32)[:, None]
    block_row, block_col, usable = slot_layout(
        row_start, col_start, owners // own_cols, owners % own_cols, own_cols, caps
    )
    position = jnp.clip(block_row * (AP_COLS + 1) + block_col, 0, AP_ROWS * (AP_COLS + 1) - 1)
    chosen = jnp.where(usable[..., None, None], pieces[position], 0.0)
    merged = merge_slots(chosen, usable[:, 1, None, None], col_start % TILE)
    return merged.reshape(groups, 1, depth_cells, TILE * TILE)


def shift_rows(c, k, rows):
    if k > 0:
        moved = pltpu.roll(c, AX - k, 0)
        return jnp.where(rows < AX - k, moved, 0.0)
    moved = pltpu.roll(c, -k, 0)
    return jnp.where(rows >= -k, moved, 0.0)


def shift_lanes(c, k, lanes):
    if k > 0:
        moved = pltpu.roll(c, AY - k, 1)
        return jnp.where(lanes < AY - k, moved, 0.0)
    moved = pltpu.roll(c, -k, 1)
    return jnp.where(lanes >= -k, moved, 0.0)


def plane_stencil(buf, r, p, rows, lanes):
    c = buf[r, p]
    summed = (3.0 * COEFFS[0]) * c
    for k in range(1, 5):
        nearby = buf[r, p + k] + buf[r, p - k]
        nearby = nearby + shift_rows(c, k, rows)
        nearby = nearby + shift_rows(c, -k, rows)
        nearby = nearby + shift_lanes(c, k, lanes)
        nearby = nearby + shift_lanes(c, -k, lanes)
        summed = summed + COEFFS[k] * nearby
    return summed


def split_bf16(values):
    high = values.astype(jnp.bfloat16)
    rest = values - high.astype(jnp.float32)
    middle = rest.astype(jnp.bfloat16)
    low = (rest - middle.astype(jnp.float32)).astype(jnp.bfloat16)
    return (high, middle, low)


def migrate_kernel(
    src_ref, wave_ref, rrow_ref, rcol_ref, resid_ref, model_ref, pf_ref, qa_ref,
    img_ref, pad_p, pad_q, lap, qs, inject, send_sem, recv_sem,
):
    me = lax.axis_index("sub")
    n_sub = lax.axis_size("sub")
    depth = model_ref.shape[0]
    halo = jnp.zeros((RADIUS, AX, AY), jnp.float32)
    for r in range(NT):
        for buf in (pad_p, pad_q):
            buf[r, 0:RADIUS] = halo
            buf[r, RADIUS + depth : 2 * RADIUS + depth] = halo
    pad_p[0, RADIUS : RADIUS + depth] = pf_ref[0]
    pad_q[0, RADIUS : RADIUS + depth] = model_ref[...] * qa_ref[0]
    up_dev = lax.rem(me + 1, n_sub)
    down_dev = lax.rem(me + n_sub - 1, n_sub)
    barrier = pltpu.get_barrier_semaphore()
    pl.semaphore_signal(barrier, 1, device_id={"sub": up_dev}, device_id_type=pl.DeviceIdType.MESH)
    pl.semaphore_signal(barrier, 1, device_id={"sub": down_dev}, device_id_type=pl.DeviceIdType.MESH)
    pl.semaphore_wait(barrier, 2)
    rows = lax.broadcasted_iota(jnp.int32, (AX, AY), 0)
    lanes = lax.broadcasted_iota(jnp.int32, (AX, AY), 1)
    n_rec = rcol_ref.shape[0]
    src_level = src_ref[0]
    src_spot = (rows == src_ref[1]) & (lanes == src_ref[2])

    def build_injection(step):
        hit_y = lax.broadcasted_iota(jnp.int32, (n_rec, AY), 1) == rcol_ref[...]
        spread = jnp.where(hit_y, resid_ref[:, step : step + 1], 0.0)
        parts = split_bf16(spread)
        rec_level = rrow_ref[0:1, :]
        hit_x = lax.broadcasted_iota(jnp.int32, (AX, n_rec), 0) == rrow_ref[1:2, :]

        def plane(j, carry):
            picks = (hit_x & (rec_level == j)).astype(jnp.bfloat16)
            total = jnp.dot(picks, parts[0], preferred_element_type=jnp.float32)
            total = total + jnp.dot(picks, parts[1], preferred_element_type=jnp.float32)
            total = total + jnp.dot(picks, parts[2], preferred_element_type=jnp.float32)
            inject[j] = total
            return carry

        lax.fori_loop(0, depth, plane, 0)

    def exchange(r, f):
        buf = (pad_p, pad_q)[f]
        down = pltpu.make_async_remote_copy(
            src_ref=buf.at[r, RADIUS : 2 * RADIUS],
            dst_ref=buf.at[r, RADIUS + depth : 2 * RADIUS + depth],
            send_sem=send_sem.at[r, f, 0],
            recv_sem=recv_sem.at[r, f, 0],
            device_id={"sub": down_dev},
            device_id_type=pl.DeviceIdType.MESH,
        )
        up = pltpu.make_async_remote_copy(
            src_ref=buf.at[r, depth : RADIUS + depth],
            dst_ref=buf.at[r, 0:RADIUS],
            send_sem=send_sem.at[r, f, 1],
            recv_sem=recv_sem.at[r, f, 1],
            device_id={"sub": up_dev},
            device_id_type=pl.DeviceIdType.MESH,
        )

        @pl.when(me > 0)
        def _():
            down.start()

        @pl.when(me < n_sub - 1)
        def _():
            up.start()

        return (down, up)

    def finish(pair):
        down, up = pair

        @pl.when(me > 0)
        def _():
            down.wait_send()
            up.wait_recv()

        @pl.when(me < n_sub - 1)
        def _():
            up.wait_send()
            down.wait_recv()

    def forward_round(r):
        def plane(j, carry):
            p = j + RADIUS
            lp = plane_stencil(pad_p, r, p, rows, lanes)
            lap[r, j] = lp
            if r < NT - 1:
                before = pf_ref[1, j] if r == 0 else pad_p[r - 1, p]
                following = 2.0 * pad_p[r, p] - before + model_ref[j] * lp
                source = jnp.where(src_spot & (src_level == j), wave_ref[r], 0.0)
                pad_p[r + 1, p] = following + source
            return carry

        lax.fori_loop(0, depth, plane, 0)

    def adjoint_round(r):
        def plane(j, carry):
            p = j + RADIUS
            lq = plane_stencil(pad_q, r, p, rows, lanes)
            now = qa_ref[0, j] if r == 0 else qs[r - 1, j]
            if r == 0:
                later = qa_ref[1, j]
            elif r == 1:
                later = qa_ref[0, j]
            else:
                later = qs[r - 2, j]
            result = 2.0 * now - later + lq
            result = result + inject[j]
            if r < NT - 1:
                qs[r, j] = result
                pad_q[r + 1, p] = model_ref[j] * result
            else:
                image = jnp.zeros((AX, AY), jnp.float32)
                for s in range(NT - 1):
                    image = image + qs[s, j] * lap[NT - 1 - s, j]
                image = image + result * lap[0, j]
                img_ref[j] = IMAGE_SCALE * image
            return carry

        lax.fori_loop(0, depth, plane, 0)

    fwd = exchange(0, 0)
    adj = exchange(0, 1)
    build_injection(NT - 1)
    for r in range(NT):
        finish(fwd)
        forward_round(r)
        if r < NT - 1:
            fwd = exchange(r + 1, 0)
        finish(adj)
        adjoint_round(r)
        if r < NT - 1:
            adj = exchange(r + 1, 1)
            build_injection(NT - 2 - r)


def migrate(model, state_fwd, state_adj, wave, source, receivers, resid):
    depth_cells = model.shape[0]
    plane = AX * AY
    offset = lax.axis_index("sub") * depth_cells

    def level_of(cells):
        level = cells // plane - offset
        inside = (level >= 0) & (level < depth_cells)
        return jnp.where(inside, level, -1)

    src = jnp.stack([level_of(source), source % plane // AY, source % AY]).astype(jnp.int32)
    rrow = jnp.stack([level_of(receivers), receivers % plane // AY]).astype(jnp.int32)
    rcol = (receivers % AY).astype(jnp.int32).reshape(-1, 1)
    vmem = pl.BlockSpec(memory_space=pltpu.VMEM)
    smem = pl.BlockSpec(memory_space=pltpu.SMEM)
    padded = (NT, depth_cells + 2 * RADIUS, AX, AY)
    field = (NT, depth_cells, AX, AY)
    return pl.pallas_call(
        migrate_kernel,
        out_shape=jax.ShapeDtypeStruct(model.shape, jnp.float32),
        in_specs=[smem, smem] + [vmem] * 6,
        out_specs=vmem,
        scratch_shapes=[
            pltpu.VMEM(padded, jnp.float32),
            pltpu.VMEM(padded, jnp.float32),
            pltpu.VMEM(field, jnp.float32),
            pltpu.VMEM(field, jnp.float32),
            pltpu.VMEM(model.shape, jnp.float32),
            pltpu.SemaphoreType.DMA((NT, 2, 2)),
            pltpu.SemaphoreType.DMA((NT, 2, 2)),
        ],
        compiler_params=pltpu.CompilerParams(collective_id=0, has_side_effects=True),
    )(
        src,
        wave.astype(jnp.float32),
        rrow,
        rcol,
        resid.T,
        model,
        state_fwd.astype(jnp.float32),
        state_adj.astype(jnp.float32),
    )


def body(
    velocity_tiles,
    forward_state,
    adjoint_state,
    wavelet,
    source_cell,
    receiver_cell,
    residual,
    aperture_row,
    aperture_col,
):
    groups = lax.axis_size("shot")
    own_cols = groups // AP_ROWS
    caps = (AP_COLS + own_cols) // own_cols
    assert own_cols == AP_COLS and caps == 2 and forward_state.shape[0] == 1
    myself = lax.axis_index("shot")
    shots_here = forward_state.shape[0]
    gradient = jnp.zeros(velocity_tiles.shape, jnp.float32)
    every_shot = list(range(shots_here))
    sending = outgoing(
        velocity_tiles, aperture_row, aperture_col, every_shot, groups, own_cols, caps
    )
    fetched = lax.all_to_all(sending, "shot", split_axis=0, concat_axis=0, tiled=True)
    images = []
    for k in every_shot:
        shot_id = myself * SHOTS_DEV + k
        row_start = aperture_row[shot_id]
        col_start = aperture_col[shot_id]
        model = assemble(fetched, row_start, col_start, own_cols)
        image = migrate(
            model,
            forward_state[k],
            adjoint_state[k],
            wavelet[k],
            source_cell[k],
            receiver_cell[k],
            residual[k],
        )
        images.append(disperse(image, row_start, col_start, groups, own_cols, caps))
    returned = lax.all_to_all(images[0], "shot", split_axis=0, concat_axis=0, tiled=True)
    gradient = accumulate(
        gradient, returned, aperture_row, aperture_col, every_shot, groups, own_cols, caps
    )
    return gradient


def solution(mesh):
    placed = (
        P("shot", "sub", None),
        P("shot", None, "sub", None, None),
        P("shot", None, "sub", None, None),
        P("shot", None),
        P("shot"),
        P("shot", None),
        P("shot", None, None),
        P(),
        P(),
    )
    return jax.shard_map(
        body, mesh=mesh, in_specs=placed, out_specs=P("shot", "sub", None), check_vma=False
    )
```

```python
import jax
import jax.numpy as jnp
from jax import lax
from jax.sharding import PartitionSpec as P
from jax.experimental import pallas as pl
from jax.experimental.pallas import tpu as pltpu

TILE = 16
RY = 3
SHOTS_DEV = 1
NT = 4
RADIUS = 4
AP_ROWS = 4
AP_COLS = 8
TILE_DEV = 12
AX = 64
AY = 128


COEFFS = (-205.0 / 72.0, 8.0 / 5.0, -1.0 / 5.0, 8.0 / 315.0, -1.0 / 560.0)
IMAGE_SCALE = 1.0 / 64.0


def padded_2(array, sides, width):
    for axis, dim in sides:
        size, length = (lax.axis_size(axis), array.shape[dim])
        up = [(i, (i + 1) % size) for i in range(size - 1)]
        down = [(j, i) for i, j in up]
        last = lax.slice_in_dim(array, length - width, length, axis=dim)
        first = lax.slice_in_dim(array, 0, width, axis=dim)
        before = lax.ppermute(last, axis, up)
        after = lax.ppermute(first, axis, down)
        array = jnp.concatenate([before, array, after], axis=dim)
    return array


def laplace(padded, depth_cells, row_cells, column_cells):
    r = 4
    center = padded[r : r + depth_cells, r : r + row_cells, r : r + column_cells]
    summed = 3.0 * COEFFS[0] * center
    for k in range(1, 5):
        nearby = padded[r + k : r + k + depth_cells, r : r + row_cells, r : r + column_cells]
        nearby = (
            nearby + padded[r - k : r - k + depth_cells, r : r + row_cells, r : r + column_cells]
        )
        nearby = (
            nearby + padded[r : r + depth_cells, r + k : r + k + row_cells, r : r + column_cells]
        )
        nearby = (
            nearby + padded[r : r + depth_cells, r - k : r - k + row_cells, r : r + column_cells]
        )
        nearby = (
            nearby + padded[r : r + depth_cells, r : r + row_cells, r + k : r + k + column_cells]
        )
        nearby = (
            nearby + padded[r : r + depth_cells, r : r + row_cells, r - k : r - k + column_cells]
        )
        summed = summed + COEFFS[k] * nearby
    return summed


def wave_operator(field):
    padded = padded_2(field, (("sub", 0),), RADIUS)
    padded = jnp.pad(padded, ((0, 0), (4, 4), (4, 4)))
    return laplace(padded, field.shape[0], AX, AY)


def adjoint_operator(field):
    padded = padded_2(field, (("sub", 0),), RADIUS)
    padded = jnp.pad(padded, ((0, 0), (4, 4), (4, 4)))
    return laplace(padded, field.shape[0], AX, AY)


def slot_layout(row_start, col_start, owner_row, owner_col, own_cols, caps):
    block_row = (owner_row - row_start) % AP_ROWS
    first_col = (owner_col - col_start // TILE) % own_cols
    block_col = first_col + own_cols * jnp.arange(caps, dtype=jnp.int32)
    usable = block_col <= AP_COLS
    return (block_row, block_col, usable)


def owner_slots(row_table, col_table, shot_list, groups, own_cols, caps):
    myself = lax.axis_index("shot")
    owner_row = myself // own_cols
    owner_col = myself % own_cols
    senders = jnp.arange(groups, dtype=jnp.int32)[:, None]
    if SHOTS_DEV == 1 and list(shot_list) == [0]:
        row_start = row_table[:groups].reshape(groups, 1, 1)
        col_start = col_table[:groups].reshape(groups, 1, 1)
    else:
        picked = senders * SHOTS_DEV + jnp.asarray(shot_list, dtype=jnp.int32)[None, :]
        row_start = row_table[picked][..., None]
        col_start = col_table[picked][..., None]
    block_row, block_col, usable = slot_layout(
        row_start, col_start, owner_row, owner_col, own_cols, caps
    )
    tile_row = row_start + block_row
    tile_col = col_start // TILE + block_col
    local = tile_row // AP_ROWS * RY + tile_col // own_cols
    local = jnp.clip(local, 0, TILE_DEV - 1)
    return (local.reshape(-1), usable.reshape(-1))


def lane_column():
    return jnp.arange(TILE * TILE, dtype=jnp.int32) % TILE


def merge_slots(pair, spare_ok, offset):
    lower = spare_ok & (lane_column() < offset)
    return jnp.where(lower, pair[:, 1], pair[:, 0])


def outgoing(velocity_tiles, row_table, col_table, shot_list, groups, own_cols, caps):
    local, usable = owner_slots(row_table, col_table, shot_list, groups, own_cols, caps)
    chosen = velocity_tiles[local]
    chosen = jnp.where(usable[:, None, None], chosen, 0.0)
    chosen = chosen.reshape(groups, caps, velocity_tiles.shape[1], velocity_tiles.shape[2])
    usable = usable.reshape(groups, caps)
    offset = (col_table[:groups] % TILE).reshape(groups, 1, 1)
    merged = merge_slots(chosen, usable[:, 1, None, None], offset)
    return merged.reshape(groups, 1, velocity_tiles.shape[1], velocity_tiles.shape[2])


def accumulate(gradient, returned, row_table, col_table, shot_list, groups, own_cols, caps):
    local, usable = owner_slots(row_table, col_table, shot_list, groups, own_cols, caps)
    usable = usable.reshape(groups, caps)
    offset = (col_table[:groups] % TILE).reshape(groups, 1, 1)
    lower = lane_column() < offset
    piece = returned.reshape(groups, gradient.shape[1], gradient.shape[2])
    spare = usable[:, 1, None, None]
    first = jnp.where(spare & lower, 0.0, piece)
    second = jnp.where(spare & lower, piece, 0.0)
    pieces = jnp.stack([first, second], axis=1).reshape(groups * caps, -1)
    hot = (local[:, None] == jnp.arange(gradient.shape[0], dtype=jnp.int32)[None, :]) & usable.reshape(-1)[:, None]
    summed = jnp.einsum(
        "st,sf->tf", hot.astype(jnp.float32), pieces, precision=lax.Precision.HIGHEST
    )
    return gradient + summed.reshape(gradient.shape)


def assemble(received, row_start, col_start, own_cols):
    depth_cells = received.shape[2]
    rel_row = jnp.arange(AP_ROWS, dtype=jnp.int32)[:, None]
    rel_col = jnp.arange(AP_COLS + 1, dtype=jnp.int32)[None, :]
    source_owner = (row_start + rel_row) % AP_ROWS * own_cols + (
        col_start // TILE + rel_col
    ) % own_cols
    flat_index = source_owner.reshape(-1)
    pieces = received.reshape(-1, depth_cells, TILE * TILE)[flat_index]
    block = pieces.reshape(AP_ROWS, AP_COLS + 1, depth_cells, TILE, TILE)
    block = block.transpose(2, 0, 3, 1, 4).reshape(depth_cells, AX, (AP_COLS + 1) * TILE)
    return lax.dynamic_slice_in_dim(block, col_start % TILE, AY, 2)


def disperse(image, row_start, col_start, groups, own_cols, caps):
    depth_cells = image.shape[0]
    wide = jnp.zeros((depth_cells, AX, (AP_COLS + 1) * TILE), jnp.float32)
    wide = lax.dynamic_update_slice_in_dim(wide, image, col_start % TILE, 2)
    pieces = wide.reshape(depth_cells, AP_ROWS, TILE, AP_COLS + 1, TILE)
    pieces = pieces.transpose(1, 3, 0, 2, 4).reshape(
        AP_ROWS * (AP_COLS + 1), depth_cells, TILE * TILE
    )
    owners = jnp.arange(groups, dtype=jnp.int32)[:, None]
    block_row, block_col, usable = slot_layout(
        row_start, col_start, owners // own_cols, owners % own_cols, own_cols, caps
    )
    position = jnp.clip(block_row * (AP_COLS + 1) + block_col, 0, AP_ROWS * (AP_COLS + 1) - 1)
    chosen = jnp.where(usable[..., None, None], pieces[position], 0.0)
    merged = merge_slots(chosen, usable[:, 1, None, None], col_start % TILE)
    return merged.reshape(groups, 1, depth_cells, TILE * TILE)


X_CHIPS = 4
GROUP_ROW = 8


def crossing(group):
    return (group // GROUP_ROW * 2 + group % 2) % X_CHIPS


def block_of(group, sub):
    cross = crossing(group)
    x, half = sub // 2, sub % 2
    low = (x - cross + 2 * X_CHIPS - 1) % X_CHIPS
    high = X_CHIPS + (cross - x + X_CHIPS) % X_CHIPS
    return (1 - half) * low + half * high


def device_of(group, block):
    cross = crossing(group)
    half = block // X_CHIPS
    low = (cross + 1 + block) % X_CHIPS
    high = (cross - block + 2 * X_CHIPS) % X_CHIPS
    return ((1 - half) * low + half * high) * 2 + half


def shift_rows(c, k, rows):
    if k > 0:
        moved = pltpu.roll(c, AX - k, 0)
        return jnp.where(rows < AX - k, moved, 0.0)
    moved = pltpu.roll(c, -k, 0)
    return jnp.where(rows >= -k, moved, 0.0)


def shift_lanes(c, k, lanes):
    if k > 0:
        moved = pltpu.roll(c, AY - k, 1)
        return jnp.where(lanes < AY - k, moved, 0.0)
    moved = pltpu.roll(c, -k, 1)
    return jnp.where(lanes >= -k, moved, 0.0)


def plane_stencil(buf, r, p, rows, lanes):
    c = buf[r, p]
    summed = (3.0 * COEFFS[0]) * c
    for k in range(1, 5):
        nearby = buf[r, p + k] + buf[r, p - k]
        nearby = nearby + shift_rows(c, k, rows)
        nearby = nearby + shift_rows(c, -k, rows)
        nearby = nearby + shift_lanes(c, k, lanes)
        nearby = nearby + shift_lanes(c, -k, lanes)
        summed = summed + COEFFS[k] * nearby
    return summed


def split_bf16(values):
    high = values.astype(jnp.bfloat16)
    rest = values - high.astype(jnp.float32)
    middle = rest.astype(jnp.bfloat16)
    low = (rest - middle.astype(jnp.float32)).astype(jnp.bfloat16)
    return (high, middle, low)


def migrate_kernel(
    src_ref, wave_ref, rrow_ref, rcol_ref, resid_ref, model_ref, pf_ref, qa_ref,
    img_ref, pad_p, pad_q, lap, qs, inject, send_sem, recv_sem,
):
    group = lax.axis_index("shot")
    me = block_of(group, lax.axis_index("sub"))
    n_sub = lax.axis_size("sub")
    depth = model_ref.shape[0]
    halo = jnp.zeros((RADIUS, AX, AY), jnp.float32)
    for r in range(NT):
        for buf in (pad_p, pad_q):
            buf[r, 0:RADIUS] = halo
            buf[r, RADIUS + depth : 2 * RADIUS + depth] = halo
    pad_p[0, RADIUS : RADIUS + depth] = pf_ref[0]
    pad_q[0, RADIUS : RADIUS + depth] = model_ref[...] * qa_ref[0]
    up_dev = device_of(group, (me + 1) % n_sub)
    down_dev = device_of(group, (me + n_sub - 1) % n_sub)
    barrier = pltpu.get_barrier_semaphore()
    pl.semaphore_signal(barrier, 1, device_id={"sub": up_dev}, device_id_type=pl.DeviceIdType.MESH)
    pl.semaphore_signal(barrier, 1, device_id={"sub": down_dev}, device_id_type=pl.DeviceIdType.MESH)
    pl.semaphore_wait(barrier, 2)
    rows = lax.broadcasted_iota(jnp.int32, (AX, AY), 0)
    lanes = lax.broadcasted_iota(jnp.int32, (AX, AY), 1)
    n_rec = rcol_ref.shape[0]
    src_level = src_ref[0]
    src_spot = (rows == src_ref[1]) & (lanes == src_ref[2])

    def build_injection(step):
        hit_y = lax.broadcasted_iota(jnp.int32, (n_rec, AY), 1) == rcol_ref[...]
        spread = jnp.where(hit_y, resid_ref[:, step : step + 1], 0.0)
        parts = split_bf16(spread)
        rec_level = rrow_ref[0:1, :]
        hit_x = lax.broadcasted_iota(jnp.int32, (AX, n_rec), 0) == rrow_ref[1:2, :]

        def plane(j, carry):
            picks = (hit_x & (rec_level == j)).astype(jnp.bfloat16)
            total = jnp.dot(picks, parts[0], preferred_element_type=jnp.float32)
            total = total + jnp.dot(picks, parts[1], preferred_element_type=jnp.float32)
            total = total + jnp.dot(picks, parts[2], preferred_element_type=jnp.float32)
            inject[j] = total
            return carry

        lax.fori_loop(0, depth, plane, 0)

    def exchange(r, f):
        buf = (pad_p, pad_q)[f]
        down = pltpu.make_async_remote_copy(
            src_ref=buf.at[r, RADIUS : 2 * RADIUS],
            dst_ref=buf.at[r, RADIUS + depth : 2 * RADIUS + depth],
            send_sem=send_sem.at[r, f, 0],
            recv_sem=recv_sem.at[r, f, 0],
            device_id={"sub": down_dev},
            device_id_type=pl.DeviceIdType.MESH,
        )
        up = pltpu.make_async_remote_copy(
            src_ref=buf.at[r, depth : RADIUS + depth],
            dst_ref=buf.at[r, 0:RADIUS],
            send_sem=send_sem.at[r, f, 1],
            recv_sem=recv_sem.at[r, f, 1],
            device_id={"sub": up_dev},
            device_id_type=pl.DeviceIdType.MESH,
        )

        @pl.when(me > 0)
        def _():
            down.start()

        @pl.when(me < n_sub - 1)
        def _():
            up.start()

        return (down, up)

    def finish(pair):
        down, up = pair

        @pl.when(me > 0)
        def _():
            down.wait_send()
            up.wait_recv()

        @pl.when(me < n_sub - 1)
        def _():
            up.wait_send()
            down.wait_recv()

    def forward_round(r):
        def plane(j, carry):
            p = j + RADIUS
            lp = plane_stencil(pad_p, r, p, rows, lanes)
            lap[r, j] = lp
            if r < NT - 1:
                before = pf_ref[1, j] if r == 0 else pad_p[r - 1, p]
                following = 2.0 * pad_p[r, p] - before + model_ref[j] * lp
                source = jnp.where(src_spot & (src_level == j), wave_ref[r], 0.0)
                pad_p[r + 1, p] = following + source
            return carry

        lax.fori_loop(0, depth, plane, 0)

    def adjoint_round(r):
        def plane(j, carry):
            p = j + RADIUS
            lq = plane_stencil(pad_q, r, p, rows, lanes)
            now = qa_ref[0, j] if r == 0 else qs[r - 1, j]
            if r == 0:
                later = qa_ref[1, j]
            elif r == 1:
                later = qa_ref[0, j]
            else:
                later = qs[r - 2, j]
            result = 2.0 * now - later + lq
            result = result + inject[j]
            if r < NT - 1:
                qs[r, j] = result
                pad_q[r + 1, p] = model_ref[j] * result
            else:
                image = jnp.zeros((AX, AY), jnp.float32)
                for s in range(NT - 1):
                    image = image + qs[s, j] * lap[NT - 1 - s, j]
                image = image + result * lap[0, j]
                img_ref[j] = IMAGE_SCALE * image
            return carry

        lax.fori_loop(0, depth, plane, 0)

    fwd = exchange(0, 0)
    adj = exchange(0, 1)
    build_injection(NT - 1)
    for r in range(NT):
        finish(fwd)
        forward_round(r)
        if r < NT - 1:
            fwd = exchange(r + 1, 0)
        finish(adj)
        adjoint_round(r)
        if r < NT - 1:
            adj = exchange(r + 1, 1)
            build_injection(NT - 2 - r)


def migrate(model, state_fwd, state_adj, wave, source, receivers, resid):
    depth_cells = model.shape[0]
    plane = AX * AY
    offset = block_of(lax.axis_index("shot"), lax.axis_index("sub")) * depth_cells

    def level_of(cells):
        level = cells // plane - offset
        inside = (level >= 0) & (level < depth_cells)
        return jnp.where(inside, level, -1)

    src = jnp.stack([level_of(source), source % plane // AY, source % AY]).astype(jnp.int32)
    rrow = jnp.stack([level_of(receivers), receivers % plane // AY]).astype(jnp.int32)
    rcol = (receivers % AY).astype(jnp.int32).reshape(-1, 1)
    vmem = pl.BlockSpec(memory_space=pltpu.VMEM)
    smem = pl.BlockSpec(memory_space=pltpu.SMEM)
    padded = (NT, depth_cells + 2 * RADIUS, AX, AY)
    field = (NT, depth_cells, AX, AY)
    return pl.pallas_call(
        migrate_kernel,
        out_shape=jax.ShapeDtypeStruct(model.shape, jnp.float32),
        in_specs=[smem, smem] + [vmem] * 6,
        out_specs=vmem,
        scratch_shapes=[
            pltpu.VMEM(padded, jnp.float32),
            pltpu.VMEM(padded, jnp.float32),
            pltpu.VMEM(field, jnp.float32),
            pltpu.VMEM(field, jnp.float32),
            pltpu.VMEM(model.shape, jnp.float32),
            pltpu.SemaphoreType.DMA((NT, 2, 2)),
            pltpu.SemaphoreType.DMA((NT, 2, 2)),
        ],
        compiler_params=pltpu.CompilerParams(collective_id=0, has_side_effects=True),
    )(
        src,
        wave.astype(jnp.float32),
        rrow,
        rcol,
        resid.T,
        model,
        state_fwd.astype(jnp.float32),
        state_adj.astype(jnp.float32),
    )


def body(
    velocity_tiles,
    forward_state,
    adjoint_state,
    wavelet,
    source_cell,
    receiver_cell,
    residual,
    aperture_row,
    aperture_col,
):
    groups = lax.axis_size("shot")
    own_cols = groups // AP_ROWS
    caps = (AP_COLS + own_cols) // own_cols
    assert own_cols == AP_COLS and caps == 2 and forward_state.shape[0] == 1
    n_sub = lax.axis_size("sub")
    assert n_sub == 2 * X_CHIPS and groups % GROUP_ROW == 0
    outbound = [
        (g * n_sub + b, g * n_sub + device_of(g, b)) for g in range(groups) for b in range(n_sub)
    ]
    myself = lax.axis_index("shot")
    shots_here = forward_state.shape[0]
    gradient = jnp.zeros(velocity_tiles.shape, jnp.float32)
    every_shot = list(range(shots_here))
    sending = outgoing(
        velocity_tiles, aperture_row, aperture_col, every_shot, groups, own_cols, caps
    )
    fetched = lax.all_to_all(sending, "shot", split_axis=0, concat_axis=0, tiled=True)
    images = []
    for k in every_shot:
        shot_id = myself * SHOTS_DEV + k
        row_start = aperture_row[shot_id]
        col_start = aperture_col[shot_id]
        model = assemble(fetched, row_start, col_start, own_cols)
        moving = jnp.concatenate(
            [
                model[None],
                forward_state[k].astype(jnp.float32),
                adjoint_state[k].astype(jnp.float32),
            ]
        )
        moving = lax.ppermute(moving, ("shot", "sub"), outbound)
        image = migrate(
            moving[0],
            moving[1:3],
            moving[3:5],
            wavelet[k],
            source_cell[k],
            receiver_cell[k],
            residual[k],
        )
        image = lax.ppermute(image, ("shot", "sub"), [(b, a) for a, b in outbound])
        images.append(disperse(image, row_start, col_start, groups, own_cols, caps))
    returned = lax.all_to_all(images[0], "shot", split_axis=0, concat_axis=0, tiled=True)
    gradient = accumulate(
        gradient, returned, aperture_row, aperture_col, every_shot, groups, own_cols, caps
    )
    return gradient


def solution(mesh):
    placed = (
        P("shot", "sub", None),
        P("shot", None, "sub", None, None),
        P("shot", None, "sub", None, None),
        P("shot", None),
        P("shot"),
        P("shot", None),
        P("shot", None, None),
        P(),
        P(),
    )
    return jax.shard_map(
        body, mesh=mesh, in_specs=placed, out_specs=P("shot", "sub", None), check_vma=False
    )
```

```python
import jax
import jax.numpy as jnp
from jax import lax
from jax.sharding import PartitionSpec as P
from jax.experimental import pallas as pl
from jax.experimental.pallas import tpu as pltpu

TILE = 16
RY = 3
SHOTS_DEV = 1
NT = 4
RADIUS = 4
AP_ROWS = 4
AP_COLS = 8
TILE_DEV = 12
AX = 64
AY = 128


COEFFS = (-205.0 / 72.0, 8.0 / 5.0, -1.0 / 5.0, 8.0 / 315.0, -1.0 / 560.0)
IMAGE_SCALE = 1.0 / 64.0


def padded_2(array, sides, width):
    for axis, dim in sides:
        size, length = (lax.axis_size(axis), array.shape[dim])
        up = [(i, (i + 1) % size) for i in range(size - 1)]
        down = [(j, i) for i, j in up]
        last = lax.slice_in_dim(array, length - width, length, axis=dim)
        first = lax.slice_in_dim(array, 0, width, axis=dim)
        before = lax.ppermute(last, axis, up)
        after = lax.ppermute(first, axis, down)
        array = jnp.concatenate([before, array, after], axis=dim)
    return array


def laplace(padded, depth_cells, row_cells, column_cells):
    r = 4
    center = padded[r : r + depth_cells, r : r + row_cells, r : r + column_cells]
    summed = 3.0 * COEFFS[0] * center
    for k in range(1, 5):
        nearby = padded[r + k : r + k + depth_cells, r : r + row_cells, r : r + column_cells]
        nearby = (
            nearby + padded[r - k : r - k + depth_cells, r : r + row_cells, r : r + column_cells]
        )
        nearby = (
            nearby + padded[r : r + depth_cells, r + k : r + k + row_cells, r : r + column_cells]
        )
        nearby = (
            nearby + padded[r : r + depth_cells, r - k : r - k + row_cells, r : r + column_cells]
        )
        nearby = (
            nearby + padded[r : r + depth_cells, r : r + row_cells, r + k : r + k + column_cells]
        )
        nearby = (
            nearby + padded[r : r + depth_cells, r : r + row_cells, r - k : r - k + column_cells]
        )
        summed = summed + COEFFS[k] * nearby
    return summed


def wave_operator(field):
    padded = padded_2(field, (("sub", 0),), RADIUS)
    padded = jnp.pad(padded, ((0, 0), (4, 4), (4, 4)))
    return laplace(padded, field.shape[0], AX, AY)


def adjoint_operator(field):
    padded = padded_2(field, (("sub", 0),), RADIUS)
    padded = jnp.pad(padded, ((0, 0), (4, 4), (4, 4)))
    return laplace(padded, field.shape[0], AX, AY)


def slot_layout(row_start, col_start, owner_row, owner_col, own_cols, caps):
    block_row = (owner_row - row_start) % AP_ROWS
    first_col = (owner_col - col_start // TILE) % own_cols
    block_col = first_col + own_cols * jnp.arange(caps, dtype=jnp.int32)
    usable = block_col <= AP_COLS
    return (block_row, block_col, usable)


def owner_slots(row_table, col_table, shot_list, groups, own_cols, caps):
    myself = lax.axis_index("shot")
    owner_row = myself // own_cols
    owner_col = myself % own_cols
    senders = jnp.arange(groups, dtype=jnp.int32)[:, None]
    if SHOTS_DEV == 1 and list(shot_list) == [0]:
        row_start = row_table[:groups].reshape(groups, 1, 1)
        col_start = col_table[:groups].reshape(groups, 1, 1)
    else:
        picked = senders * SHOTS_DEV + jnp.asarray(shot_list, dtype=jnp.int32)[None, :]
        row_start = row_table[picked][..., None]
        col_start = col_table[picked][..., None]
    block_row, block_col, usable = slot_layout(
        row_start, col_start, owner_row, owner_col, own_cols, caps
    )
    tile_row = row_start + block_row
    tile_col = col_start // TILE + block_col
    local = tile_row // AP_ROWS * RY + tile_col // own_cols
    local = jnp.clip(local, 0, TILE_DEV - 1)
    return (local.reshape(-1), usable.reshape(-1))


def lane_column():
    return jnp.arange(TILE * TILE, dtype=jnp.int32) % TILE


def merge_slots(pair, spare_ok, offset):
    lower = spare_ok & (lane_column() < offset)
    return jnp.where(lower, pair[:, 1], pair[:, 0])


def outgoing(velocity_tiles, row_table, col_table, shot_list, groups, own_cols, caps):
    local, usable = owner_slots(row_table, col_table, shot_list, groups, own_cols, caps)
    chosen = velocity_tiles[local]
    chosen = jnp.where(usable[:, None, None], chosen, 0.0)
    chosen = chosen.reshape(groups, caps, velocity_tiles.shape[1], velocity_tiles.shape[2])
    usable = usable.reshape(groups, caps)
    offset = (col_table[:groups] % TILE).reshape(groups, 1, 1)
    merged = merge_slots(chosen, usable[:, 1, None, None], offset)
    return merged.reshape(groups, 1, velocity_tiles.shape[1], velocity_tiles.shape[2])


def accumulate(gradient, returned, row_table, col_table, shot_list, groups, own_cols, caps):
    local, usable = owner_slots(row_table, col_table, shot_list, groups, own_cols, caps)
    usable = usable.reshape(groups, caps)
    offset = (col_table[:groups] % TILE).reshape(groups, 1, 1)
    lower = lane_column() < offset
    piece = returned.reshape(groups, gradient.shape[1], gradient.shape[2])
    spare = usable[:, 1, None, None]
    first = jnp.where(spare & lower, 0.0, piece)
    second = jnp.where(spare & lower, piece, 0.0)
    pieces = jnp.stack([first, second], axis=1).reshape(groups * caps, -1)
    hot = (local[:, None] == jnp.arange(gradient.shape[0], dtype=jnp.int32)[None, :]) & usable.reshape(-1)[:, None]
    summed = jnp.einsum(
        "st,sf->tf", hot.astype(jnp.float32), pieces, precision=lax.Precision.HIGHEST
    )
    return gradient + summed.reshape(gradient.shape)


def assemble(received, row_start, col_start, own_cols):
    depth_cells = received.shape[2]
    rel_row = jnp.arange(AP_ROWS, dtype=jnp.int32)[:, None]
    rel_col = jnp.arange(AP_COLS + 1, dtype=jnp.int32)[None, :]
    source_owner = (row_start + rel_row) % AP_ROWS * own_cols + (
        col_start // TILE + rel_col
    ) % own_cols
    flat_index = source_owner.reshape(-1)
    pieces = received.reshape(-1, depth_cells, TILE * TILE)[flat_index]
    block = pieces.reshape(AP_ROWS, AP_COLS + 1, depth_cells, TILE, TILE)
    block = block.transpose(2, 0, 3, 1, 4).reshape(depth_cells, AX, (AP_COLS + 1) * TILE)
    return lax.dynamic_slice_in_dim(block, col_start % TILE, AY, 2)


def disperse(image, row_start, col_start, groups, own_cols, caps):
    depth_cells = image.shape[0]
    wide = jnp.zeros((depth_cells, AX, (AP_COLS + 1) * TILE), jnp.float32)
    wide = lax.dynamic_update_slice_in_dim(wide, image, col_start % TILE, 2)
    pieces = wide.reshape(depth_cells, AP_ROWS, TILE, AP_COLS + 1, TILE)
    pieces = pieces.transpose(1, 3, 0, 2, 4).reshape(
        AP_ROWS * (AP_COLS + 1), depth_cells, TILE * TILE
    )
    owners = jnp.arange(groups, dtype=jnp.int32)[:, None]
    block_row, block_col, usable = slot_layout(
        row_start, col_start, owners // own_cols, owners % own_cols, own_cols, caps
    )
    position = jnp.clip(block_row * (AP_COLS + 1) + block_col, 0, AP_ROWS * (AP_COLS + 1) - 1)
    chosen = jnp.where(usable[..., None, None], pieces[position], 0.0)
    merged = merge_slots(chosen, usable[:, 1, None, None], col_start % TILE)
    return merged.reshape(groups, 1, depth_cells, TILE * TILE)


X_CHIPS = 4
GROUP_ROW = 8


def crossing(group):
    return (group // GROUP_ROW * 2 + group % 2) % X_CHIPS


def block_of(group, sub):
    cross = crossing(group)
    x, half = sub // 2, sub % 2
    low = (x - cross + 2 * X_CHIPS - 1) % X_CHIPS
    high = X_CHIPS + (cross - x + X_CHIPS) % X_CHIPS
    return (1 - half) * low + half * high


def device_of(group, block):
    cross = crossing(group)
    half = block // X_CHIPS
    low = (cross + 1 + block) % X_CHIPS
    high = (cross - block + 2 * X_CHIPS) % X_CHIPS
    return ((1 - half) * low + half * high) * 2 + half


def shift_rows(c, k, rows):
    if k > 0:
        moved = pltpu.roll(c, AX - k, 0)
        return jnp.where(rows < AX - k, moved, 0.0)
    moved = pltpu.roll(c, -k, 0)
    return jnp.where(rows >= -k, moved, 0.0)


def shift_lanes(c, k, lanes):
    if k > 0:
        moved = pltpu.roll(c, AY - k, 1)
        return jnp.where(lanes < AY - k, moved, 0.0)
    moved = pltpu.roll(c, -k, 1)
    return jnp.where(lanes >= -k, moved, 0.0)


def plane_stencil(buf, r, p, rows, lanes):
    c = buf[r, p]
    summed = (3.0 * COEFFS[0]) * c
    for k in range(1, 5):
        nearby = buf[r, p + k] + buf[r, p - k]
        nearby = nearby + shift_rows(c, k, rows)
        nearby = nearby + shift_rows(c, -k, rows)
        nearby = nearby + shift_lanes(c, k, lanes)
        nearby = nearby + shift_lanes(c, -k, lanes)
        summed = summed + COEFFS[k] * nearby
    return summed


def split_bf16(values):
    high = values.astype(jnp.bfloat16)
    rest = values - high.astype(jnp.float32)
    middle = rest.astype(jnp.bfloat16)
    low = (rest - middle.astype(jnp.float32)).astype(jnp.bfloat16)
    return (high, middle, low)


def migrate_kernel(
    src_ref, wave_ref, rrow_ref, rcol_ref, resid_ref, model_ref, pf_ref, qa_ref,
    img_ref, pad_p, pad_q, lap, qs, inject, send_sem, recv_sem,
):
    group = lax.axis_index("shot")
    me = block_of(group, lax.axis_index("sub"))
    n_sub = lax.axis_size("sub")
    depth = model_ref.shape[0]
    halo = jnp.zeros((RADIUS, AX, AY), jnp.float32)
    for r in range(NT):
        for buf in (pad_p, pad_q):
            buf[r, 0:RADIUS] = halo
            buf[r, RADIUS + depth : 2 * RADIUS + depth] = halo
    pad_p[0, RADIUS : RADIUS + depth] = pf_ref[0]
    pad_q[0, RADIUS : RADIUS + depth] = model_ref[...] * qa_ref[0]
    up_dev = device_of(group, (me + 1) % n_sub)
    down_dev = device_of(group, (me + n_sub - 1) % n_sub)
    barrier = pltpu.get_barrier_semaphore()
    pl.semaphore_signal(barrier, 1, device_id={"sub": up_dev}, device_id_type=pl.DeviceIdType.MESH)
    pl.semaphore_signal(barrier, 1, device_id={"sub": down_dev}, device_id_type=pl.DeviceIdType.MESH)
    pl.semaphore_wait(barrier, 2)
    rows = lax.broadcasted_iota(jnp.int32, (AX, AY), 0)
    lanes = lax.broadcasted_iota(jnp.int32, (AX, AY), 1)
    n_rec = rcol_ref.shape[0]
    src_level = src_ref[0]
    src_spot = (rows == src_ref[1]) & (lanes == src_ref[2])

    def build_injection(step):
        hit_y = lax.broadcasted_iota(jnp.int32, (n_rec, AY), 1) == rcol_ref[...]
        spread = jnp.where(hit_y, resid_ref[:, step : step + 1], 0.0)
        parts = split_bf16(spread)
        rec_level = rrow_ref[0:1, :]
        hit_x = lax.broadcasted_iota(jnp.int32, (AX, n_rec), 0) == rrow_ref[1:2, :]

        def plane(j, carry):
            picks = (hit_x & (rec_level == j)).astype(jnp.bfloat16)
            total = jnp.dot(picks, parts[0], preferred_element_type=jnp.float32)
            total = total + jnp.dot(picks, parts[1], preferred_element_type=jnp.float32)
            total = total + jnp.dot(picks, parts[2], preferred_element_type=jnp.float32)
            inject[j] = total
            return carry

        lax.fori_loop(0, depth, plane, 0)

    def exchange(r, f):
        buf = (pad_p, pad_q)[f]
        down = pltpu.make_async_remote_copy(
            src_ref=buf.at[r, RADIUS : 2 * RADIUS],
            dst_ref=buf.at[r, RADIUS + depth : 2 * RADIUS + depth],
            send_sem=send_sem.at[r, f, 0],
            recv_sem=recv_sem.at[r, f, 0],
            device_id={"sub": down_dev},
            device_id_type=pl.DeviceIdType.MESH,
        )
        up = pltpu.make_async_remote_copy(
            src_ref=buf.at[r, depth : RADIUS + depth],
            dst_ref=buf.at[r, 0:RADIUS],
            send_sem=send_sem.at[r, f, 1],
            recv_sem=recv_sem.at[r, f, 1],
            device_id={"sub": up_dev},
            device_id_type=pl.DeviceIdType.MESH,
        )

        @pl.when(me > 0)
        def _():
            down.start()

        @pl.when(me < n_sub - 1)
        def _():
            up.start()

        return (down, up)

    def finish(pair):
        down, up = pair

        @pl.when(me > 0)
        def _():
            down.wait_send()
            up.wait_recv()

        @pl.when(me < n_sub - 1)
        def _():
            up.wait_send()
            down.wait_recv()

    def forward_round(r):
        def plane(j, carry):
            p = j + RADIUS
            lp = plane_stencil(pad_p, r, p, rows, lanes)
            lap[r, j] = lp
            if r < NT - 1:
                before = pf_ref[1, j] if r == 0 else pad_p[r - 1, p]
                following = 2.0 * pad_p[r, p] - before + model_ref[j] * lp
                source = jnp.where(src_spot & (src_level == j), wave_ref[r], 0.0)
                pad_p[r + 1, p] = following + source
            return carry

        lax.fori_loop(0, depth, plane, 0)

    def adjoint_round(r):
        def plane(j, carry):
            p = j + RADIUS
            lq = plane_stencil(pad_q, r, p, rows, lanes)
            now = qa_ref[0, j] if r == 0 else qs[r - 1, j]
            if r == 0:
                later = qa_ref[1, j]
            elif r == 1:
                later = qa_ref[0, j]
            else:
                later = qs[r - 2, j]
            result = 2.0 * now - later + lq
            result = result + inject[j]
            if r < NT - 1:
                qs[r, j] = result
                pad_q[r + 1, p] = model_ref[j] * result
            else:
                image = jnp.zeros((AX, AY), jnp.float32)
                for s in range(NT - 1):
                    image = image + qs[s, j] * lap[NT - 1 - s, j]
                image = image + result * lap[0, j]
                img_ref[j] = IMAGE_SCALE * image
            return carry

        lax.fori_loop(0, depth, plane, 0)

    fwd = exchange(0, 0)
    adj = exchange(0, 1)
    build_injection(NT - 1)
    for r in range(NT):
        finish(fwd)
        forward_round(r)
        if r < NT - 1:
            fwd = exchange(r + 1, 0)
        finish(adj)
        adjoint_round(r)
        if r < NT - 1:
            adj = exchange(r + 1, 1)
            build_injection(NT - 2 - r)


def migrate(model, state_fwd, state_adj, wave, source, receivers, resid):
    depth_cells = model.shape[0]
    plane = AX * AY
    offset = block_of(lax.axis_index("shot"), lax.axis_index("sub")) * depth_cells

    def level_of(cells):
        level = cells // plane - offset
        inside = (level >= 0) & (level < depth_cells)
        return jnp.where(inside, level, -1)

    src = jnp.stack([level_of(source), source % plane // AY, source % AY]).astype(jnp.int32)
    rrow = jnp.stack([level_of(receivers), receivers % plane // AY]).astype(jnp.int32)
    rcol = (receivers % AY).astype(jnp.int32).reshape(-1, 1)
    vmem = pl.BlockSpec(memory_space=pltpu.VMEM)
    smem = pl.BlockSpec(memory_space=pltpu.SMEM)
    padded = (NT, depth_cells + 2 * RADIUS, AX, AY)
    field = (NT, depth_cells, AX, AY)
    return pl.pallas_call(
        migrate_kernel,
        out_shape=jax.ShapeDtypeStruct(model.shape, jnp.float32),
        in_specs=[smem, smem] + [vmem] * 6,
        out_specs=vmem,
        scratch_shapes=[
            pltpu.VMEM(padded, jnp.float32),
            pltpu.VMEM(padded, jnp.float32),
            pltpu.VMEM(field, jnp.float32),
            pltpu.VMEM(field, jnp.float32),
            pltpu.VMEM(model.shape, jnp.float32),
            pltpu.SemaphoreType.DMA((NT, 2, 2)),
            pltpu.SemaphoreType.DMA((NT, 2, 2)),
        ],
        compiler_params=pltpu.CompilerParams(collective_id=0, has_side_effects=True),
    )(
        src,
        wave.astype(jnp.float32),
        rrow,
        rcol,
        resid.T,
        model,
        state_fwd.astype(jnp.float32),
        state_adj.astype(jnp.float32),
    )


def body(
    velocity_tiles,
    forward_state,
    adjoint_state,
    wavelet,
    source_cell,
    receiver_cell,
    residual,
    aperture_row,
    aperture_col,
):
    groups = lax.axis_size("shot")
    own_cols = groups // AP_ROWS
    caps = (AP_COLS + own_cols) // own_cols
    assert own_cols == AP_COLS and caps == 2 and forward_state.shape[0] == 1
    n_sub = lax.axis_size("sub")
    assert n_sub == 2 * X_CHIPS and groups % GROUP_ROW == 0
    outbound = [
        (g * n_sub + b, g * n_sub + device_of(g, b)) for g in range(groups) for b in range(n_sub)
    ]
    myself = lax.axis_index("shot")
    shots_here = forward_state.shape[0]
    gradient = jnp.zeros(velocity_tiles.shape, jnp.float32)
    every_shot = list(range(shots_here))
    states_moved = []
    for k in range(shots_here):
        states = jnp.concatenate(
            [forward_state[k].astype(jnp.float32), adjoint_state[k].astype(jnp.float32)]
        )
        states_moved.append(lax.ppermute(states, ("shot", "sub"), outbound))
    sending = outgoing(
        velocity_tiles, aperture_row, aperture_col, every_shot, groups, own_cols, caps
    )
    fetched = lax.all_to_all(sending, "shot", split_axis=0, concat_axis=0, tiled=True)
    images = []
    for k in every_shot:
        shot_id = myself * SHOTS_DEV + k
        row_start = aperture_row[shot_id]
        col_start = aperture_col[shot_id]
        model = assemble(fetched, row_start, col_start, own_cols)
        model = lax.ppermute(model, ("shot", "sub"), outbound)
        states = states_moved[k]
        image = migrate(
            model,
            states[0:2],
            states[2:4],
            wavelet[k],
            source_cell[k],
            receiver_cell[k],
            residual[k],
        )
        image = lax.ppermute(image, ("shot", "sub"), [(b, a) for a, b in outbound])
        images.append(disperse(image, row_start, col_start, groups, own_cols, caps))
    returned = lax.all_to_all(images[0], "shot", split_axis=0, concat_axis=0, tiled=True)
    gradient = accumulate(
        gradient, returned, aperture_row, aperture_col, every_shot, groups, own_cols, caps
    )
    return gradient


def solution(mesh):
    placed = (
        P("shot", "sub", None),
        P("shot", None, "sub", None, None),
        P("shot", None, "sub", None, None),
        P("shot", None),
        P("shot"),
        P("shot", None),
        P("shot", None, None),
        P(),
        P(),
    )
    return jax.shard_map(
        body, mesh=mesh, in_specs=placed, out_specs=P("shot", "sub", None), check_vma=False
    )
```

```python
import functools

import jax
import jax.numpy as jnp
from jax import lax
from jax.sharding import PartitionSpec as P
from jax.experimental import pallas as pl
from jax.experimental.pallas import tpu as pltpu

TILE = 16
RY = 3
SHOTS_DEV = 1
NT = 4
RADIUS = 4
AP_ROWS = 4
AP_COLS = 8
TILE_DEV = 12
AX = 64
AY = 128


COEFFS = (-205.0 / 72.0, 8.0 / 5.0, -1.0 / 5.0, 8.0 / 315.0, -1.0 / 560.0)
IMAGE_SCALE = 1.0 / 64.0


def padded_2(array, sides, width):
    for axis, dim in sides:
        size, length = (lax.axis_size(axis), array.shape[dim])
        up = [(i, (i + 1) % size) for i in range(size - 1)]
        down = [(j, i) for i, j in up]
        last = lax.slice_in_dim(array, length - width, length, axis=dim)
        first = lax.slice_in_dim(array, 0, width, axis=dim)
        before = lax.ppermute(last, axis, up)
        after = lax.ppermute(first, axis, down)
        array = jnp.concatenate([before, array, after], axis=dim)
    return array


def laplace(padded, depth_cells, row_cells, column_cells):
    r = 4
    center = padded[r : r + depth_cells, r : r + row_cells, r : r + column_cells]
    summed = 3.0 * COEFFS[0] * center
    for k in range(1, 5):
        nearby = padded[r + k : r + k + depth_cells, r : r + row_cells, r : r + column_cells]
        nearby = (
            nearby + padded[r - k : r - k + depth_cells, r : r + row_cells, r : r + column_cells]
        )
        nearby = (
            nearby + padded[r : r + depth_cells, r + k : r + k + row_cells, r : r + column_cells]
        )
        nearby = (
            nearby + padded[r : r + depth_cells, r - k : r - k + row_cells, r : r + column_cells]
        )
        nearby = (
            nearby + padded[r : r + depth_cells, r : r + row_cells, r + k : r + k + column_cells]
        )
        nearby = (
            nearby + padded[r : r + depth_cells, r : r + row_cells, r - k : r - k + column_cells]
        )
        summed = summed + COEFFS[k] * nearby
    return summed


def wave_operator(field):
    padded = padded_2(field, (("sub", 0),), RADIUS)
    padded = jnp.pad(padded, ((0, 0), (4, 4), (4, 4)))
    return laplace(padded, field.shape[0], AX, AY)


def adjoint_operator(field):
    padded = padded_2(field, (("sub", 0),), RADIUS)
    padded = jnp.pad(padded, ((0, 0), (4, 4), (4, 4)))
    return laplace(padded, field.shape[0], AX, AY)


def slot_layout(row_start, col_start, owner_row, owner_col, own_cols, caps):
    block_row = (owner_row - row_start) % AP_ROWS
    first_col = (owner_col - col_start // TILE) % own_cols
    block_col = first_col + own_cols * jnp.arange(caps, dtype=jnp.int32)
    usable = block_col <= AP_COLS
    return (block_row, block_col, usable)


def owner_slots(row_table, col_table, shot_list, groups, own_cols, caps):
    myself = lax.axis_index("shot")
    owner_row = myself // own_cols
    owner_col = myself % own_cols
    senders = jnp.arange(groups, dtype=jnp.int32)[:, None]
    if SHOTS_DEV == 1 and list(shot_list) == [0]:
        row_start = row_table[:groups].reshape(groups, 1, 1)
        col_start = col_table[:groups].reshape(groups, 1, 1)
    else:
        picked = senders * SHOTS_DEV + jnp.asarray(shot_list, dtype=jnp.int32)[None, :]
        row_start = row_table[picked][..., None]
        col_start = col_table[picked][..., None]
    block_row, block_col, usable = slot_layout(
        row_start, col_start, owner_row, owner_col, own_cols, caps
    )
    tile_row = row_start + block_row
    tile_col = col_start // TILE + block_col
    local = tile_row // AP_ROWS * RY + tile_col // own_cols
    local = jnp.clip(local, 0, TILE_DEV - 1)
    return (local.reshape(-1), usable.reshape(-1))


def lane_column():
    return jnp.arange(TILE * TILE, dtype=jnp.int32) % TILE


def merge_slots(pair, spare_ok, offset):
    lower = spare_ok & (lane_column() < offset)
    return jnp.where(lower, pair[:, 1], pair[:, 0])


def outgoing(velocity_tiles, row_table, col_table, shot_list, groups, own_cols, caps):
    local, usable = owner_slots(row_table, col_table, shot_list, groups, own_cols, caps)
    chosen = velocity_tiles[local]
    chosen = jnp.where(usable[:, None, None], chosen, 0.0)
    chosen = chosen.reshape(groups, caps, velocity_tiles.shape[1], velocity_tiles.shape[2])
    usable = usable.reshape(groups, caps)
    offset = (col_table[:groups] % TILE).reshape(groups, 1, 1)
    merged = merge_slots(chosen, usable[:, 1, None, None], offset)
    return merged.reshape(groups, 1, velocity_tiles.shape[1], velocity_tiles.shape[2])


def accumulate(gradient, returned, row_table, col_table, shot_list, groups, own_cols, caps):
    local, usable = owner_slots(row_table, col_table, shot_list, groups, own_cols, caps)
    usable = usable.reshape(groups, caps)
    offset = (col_table[:groups] % TILE).reshape(groups, 1, 1)
    lower = lane_column() < offset
    piece = returned.reshape(groups, gradient.shape[1], gradient.shape[2])
    spare = usable[:, 1, None, None]
    first = jnp.where(spare & lower, 0.0, piece)
    second = jnp.where(spare & lower, piece, 0.0)
    pieces = jnp.stack([first, second], axis=1).reshape(groups * caps, -1)
    hot = (local[:, None] == jnp.arange(gradient.shape[0], dtype=jnp.int32)[None, :]) & usable.reshape(-1)[:, None]
    summed = jnp.einsum(
        "st,sf->tf", hot.astype(jnp.float32), pieces, precision=lax.Precision.HIGHEST
    )
    return gradient + summed.reshape(gradient.shape)


def assemble(received, row_start, col_start, own_cols):
    depth_cells = received.shape[2]
    rel_row = jnp.arange(AP_ROWS, dtype=jnp.int32)[:, None]
    rel_col = jnp.arange(AP_COLS + 1, dtype=jnp.int32)[None, :]
    source_owner = (row_start + rel_row) % AP_ROWS * own_cols + (
        col_start // TILE + rel_col
    ) % own_cols
    flat_index = source_owner.reshape(-1)
    pieces = received.reshape(-1, depth_cells, TILE * TILE)[flat_index]
    block = pieces.reshape(AP_ROWS, AP_COLS + 1, depth_cells, TILE, TILE)
    block = block.transpose(2, 0, 3, 1, 4).reshape(depth_cells, AX, (AP_COLS + 1) * TILE)
    return lax.dynamic_slice_in_dim(block, col_start % TILE, AY, 2)


def disperse(image, row_start, col_start, groups, own_cols, caps):
    depth_cells = image.shape[0]
    wide = jnp.zeros((depth_cells, AX, (AP_COLS + 1) * TILE), jnp.float32)
    wide = lax.dynamic_update_slice_in_dim(wide, image, col_start % TILE, 2)
    pieces = wide.reshape(depth_cells, AP_ROWS, TILE, AP_COLS + 1, TILE)
    pieces = pieces.transpose(1, 3, 0, 2, 4).reshape(
        AP_ROWS * (AP_COLS + 1), depth_cells, TILE * TILE
    )
    owners = jnp.arange(groups, dtype=jnp.int32)[:, None]
    block_row, block_col, usable = slot_layout(
        row_start, col_start, owners // own_cols, owners % own_cols, own_cols, caps
    )
    position = jnp.clip(block_row * (AP_COLS + 1) + block_col, 0, AP_ROWS * (AP_COLS + 1) - 1)
    chosen = jnp.where(usable[..., None, None], pieces[position], 0.0)
    merged = merge_slots(chosen, usable[:, 1, None, None], col_start % TILE)
    return merged.reshape(groups, 1, depth_cells, TILE * TILE)


X_CHIPS = 4
GROUP_ROW = 8


def crossing(group):
    return (group // GROUP_ROW * 2 + group % 2) % X_CHIPS


def block_of(group, sub):
    cross = crossing(group)
    x, half = sub // 2, sub % 2
    low = (x - cross + 2 * X_CHIPS - 1) % X_CHIPS
    high = X_CHIPS + (cross - x + X_CHIPS) % X_CHIPS
    return (1 - half) * low + half * high


def device_of(group, block):
    cross = crossing(group)
    half = block // X_CHIPS
    low = (cross + 1 + block) % X_CHIPS
    high = (cross - block + 2 * X_CHIPS) % X_CHIPS
    return ((1 - half) * low + half * high) * 2 + half


def shift_rows(c, k, rows):
    if k > 0:
        moved = pltpu.roll(c, AX - k, 0)
        return jnp.where(rows < AX - k, moved, 0.0)
    moved = pltpu.roll(c, -k, 0)
    return jnp.where(rows >= -k, moved, 0.0)


def shift_lanes(c, k, lanes):
    if k > 0:
        moved = pltpu.roll(c, AY - k, 1)
        return jnp.where(lanes < AY - k, moved, 0.0)
    moved = pltpu.roll(c, -k, 1)
    return jnp.where(lanes >= -k, moved, 0.0)


def plane_stencil(buf, r, p, rows, lanes):
    c = buf[r, p]
    summed = (3.0 * COEFFS[0]) * c
    for k in range(1, 5):
        nearby = buf[r, p + k] + buf[r, p - k]
        nearby = nearby + shift_rows(c, k, rows)
        nearby = nearby + shift_rows(c, -k, rows)
        nearby = nearby + shift_lanes(c, k, lanes)
        nearby = nearby + shift_lanes(c, -k, lanes)
        summed = summed + COEFFS[k] * nearby
    return summed


def split_bf16(values):
    high = values.astype(jnp.bfloat16)
    rest = values - high.astype(jnp.float32)
    middle = rest.astype(jnp.bfloat16)
    low = (rest - middle.astype(jnp.float32)).astype(jnp.bfloat16)
    return (high, middle, low)


def halo_exchange(buf, r, f, me, n_sub, up_dev, down_dev, send_sem, recv_sem):
    depth = buf.shape[1] - 2 * RADIUS
    down = pltpu.make_async_remote_copy(
        src_ref=buf.at[r, RADIUS : 2 * RADIUS],
        dst_ref=buf.at[r, RADIUS + depth : 2 * RADIUS + depth],
        send_sem=send_sem.at[r, f, 0],
        recv_sem=recv_sem.at[r, f, 0],
        device_id={"sub": down_dev},
        device_id_type=pl.DeviceIdType.MESH,
    )
    up = pltpu.make_async_remote_copy(
        src_ref=buf.at[r, depth : RADIUS + depth],
        dst_ref=buf.at[r, 0:RADIUS],
        send_sem=send_sem.at[r, f, 1],
        recv_sem=recv_sem.at[r, f, 1],
        device_id={"sub": up_dev},
        device_id_type=pl.DeviceIdType.MESH,
    )

    @pl.when(me > 0)
    def _():
        down.start()

    @pl.when(me < n_sub - 1)
    def _():
        up.start()

    def finish():
        @pl.when(me > 0)
        def _():
            down.wait_send()
            up.wait_recv()

        @pl.when(me < n_sub - 1)
        def _():
            up.wait_send()
            down.wait_recv()

    return finish


def chain_setup(pad, first, depth):
    group = lax.axis_index("shot")
    me = block_of(group, lax.axis_index("sub"))
    n_sub = lax.axis_size("sub")
    halo = jnp.zeros((RADIUS, AX, AY), jnp.float32)
    for r in range(NT):
        pad[r, 0:RADIUS] = halo
        pad[r, RADIUS + depth : 2 * RADIUS + depth] = halo
    pad[0, RADIUS : RADIUS + depth] = first
    up_dev = device_of(group, (me + 1) % n_sub)
    down_dev = device_of(group, (me + n_sub - 1) % n_sub)
    barrier = pltpu.get_barrier_semaphore()
    pl.semaphore_signal(barrier, 1, device_id={"sub": up_dev}, device_id_type=pl.DeviceIdType.MESH)
    pl.semaphore_signal(barrier, 1, device_id={"sub": down_dev}, device_id_type=pl.DeviceIdType.MESH)
    pl.semaphore_wait(barrier, 2)
    return me, n_sub, up_dev, down_dev


def forward_kernel(src_ref, wave_ref, model_ref, pf_ref, lap, pad_p, send_sem, recv_sem):
    depth = model_ref.shape[0]
    me, n_sub, up_dev, down_dev = chain_setup(pad_p, pf_ref[0], depth)
    rows = lax.broadcasted_iota(jnp.int32, (AX, AY), 0)
    lanes = lax.broadcasted_iota(jnp.int32, (AX, AY), 1)
    src_level = src_ref[0]
    src_spot = (rows == src_ref[1]) & (lanes == src_ref[2])
    for r in range(NT):
        finish = halo_exchange(pad_p, r, 0, me, n_sub, up_dev, down_dev, send_sem, recv_sem)
        finish()

        def plane(j, carry, r=r):
            p = j + RADIUS
            lp = plane_stencil(pad_p, r, p, rows, lanes)
            lap[r, j] = lp
            if r < NT - 1:
                before = pf_ref[1, j] if r == 0 else pad_p[r - 1, p]
                following = 2.0 * pad_p[r, p] - before + model_ref[j] * lp
                source = jnp.where(src_spot & (src_level == j), wave_ref[r], 0.0)
                pad_p[r + 1, p] = following + source
            return carry

        lax.fori_loop(0, depth, plane, 0)


def adjoint_kernel(
    rrow_ref, rcol_ref, resid_ref, model_ref, qa_ref, lap, img_ref,
    pad_q, qs, inject, send_sem, recv_sem,
):
    depth = model_ref.shape[0]
    me, n_sub, up_dev, down_dev = chain_setup(pad_q, model_ref[...] * qa_ref[0], depth)
    n_rec = rcol_ref.shape[0]

    def build_injection(step):
        hit_y = lax.broadcasted_iota(jnp.int32, (n_rec, AY), 1) == rcol_ref[...]
        spread = jnp.where(hit_y, resid_ref[:, step : step + 1], 0.0)
        parts = split_bf16(spread)
        rec_level = rrow_ref[0:1, :]
        hit_x = lax.broadcasted_iota(jnp.int32, (AX, n_rec), 0) == rrow_ref[1:2, :]

        def plane(j, carry):
            picks = (hit_x & (rec_level == j)).astype(jnp.bfloat16)
            total = jnp.dot(picks, parts[0], preferred_element_type=jnp.float32)
            total = total + jnp.dot(picks, parts[1], preferred_element_type=jnp.float32)
            total = total + jnp.dot(picks, parts[2], preferred_element_type=jnp.float32)
            inject[j] = total
            return carry

        lax.fori_loop(0, depth, plane, 0)

    rows = lax.broadcasted_iota(jnp.int32, (AX, AY), 0)
    lanes = lax.broadcasted_iota(jnp.int32, (AX, AY), 1)
    for r in range(NT):
        finish = halo_exchange(pad_q, r, 0, me, n_sub, up_dev, down_dev, send_sem, recv_sem)
        build_injection(NT - 1 - r)
        finish()

        def plane(j, carry, r=r):
            p = j + RADIUS
            lq = plane_stencil(pad_q, r, p, rows, lanes)
            now = qa_ref[0, j] if r == 0 else qs[r - 1, j]
            if r == 0:
                later = qa_ref[1, j]
            elif r == 1:
                later = qa_ref[0, j]
            else:
                later = qs[r - 2, j]
            result = 2.0 * now - later + lq
            result = result + inject[j]
            if r < NT - 1:
                qs[r, j] = result
                pad_q[r + 1, p] = model_ref[j] * result
            else:
                image = jnp.zeros((AX, AY), jnp.float32)
                for s in range(NT - 1):
                    image = image + qs[s, j] * lap[NT - 1 - s, j]
                image = image + result * lap[0, j]
                img_ref[j] = IMAGE_SCALE * image
            return carry

        lax.fori_loop(0, depth, plane, 0)


def migrate(model, state_fwd, state_adj, wave, source, receivers, resid):
    depth_cells = model.shape[0]
    plane = AX * AY
    offset = block_of(lax.axis_index("shot"), lax.axis_index("sub")) * depth_cells

    def level_of(cells):
        level = cells // plane - offset
        inside = (level >= 0) & (level < depth_cells)
        return jnp.where(inside, level, -1)

    src = jnp.stack([level_of(source), source % plane // AY, source % AY]).astype(jnp.int32)
    rrow = jnp.stack([level_of(receivers), receivers % plane // AY]).astype(jnp.int32)
    rcol = (receivers % AY).astype(jnp.int32).reshape(-1, 1)
    vmem = pl.BlockSpec(memory_space=pltpu.VMEM)
    smem = pl.BlockSpec(memory_space=pltpu.SMEM)
    padded = (NT, depth_cells + 2 * RADIUS, AX, AY)
    field = (NT, depth_cells, AX, AY)
    lap = pl.pallas_call(
        forward_kernel,
        out_shape=jax.ShapeDtypeStruct(field, jnp.float32),
        in_specs=[smem, smem, vmem, vmem],
        out_specs=vmem,
        scratch_shapes=[
            pltpu.VMEM(padded, jnp.float32),
            pltpu.SemaphoreType.DMA((NT, 1, 2)),
            pltpu.SemaphoreType.DMA((NT, 1, 2)),
        ],
        compiler_params=pltpu.CompilerParams(collective_id=0, has_side_effects=True),
    )(src, wave.astype(jnp.float32), model, state_fwd.astype(jnp.float32))
    state_adj = state_adj()
    return pl.pallas_call(
        adjoint_kernel,
        out_shape=jax.ShapeDtypeStruct(model.shape, jnp.float32),
        in_specs=[vmem] * 6,
        out_specs=vmem,
        scratch_shapes=[
            pltpu.VMEM(padded, jnp.float32),
            pltpu.VMEM((NT - 1, depth_cells, AX, AY), jnp.float32),
            pltpu.VMEM(model.shape, jnp.float32),
            pltpu.SemaphoreType.DMA((NT, 1, 2)),
            pltpu.SemaphoreType.DMA((NT, 1, 2)),
        ],
        compiler_params=pltpu.CompilerParams(collective_id=1, has_side_effects=True),
    )(rrow, rcol, resid.T, model, state_adj.astype(jnp.float32), lap)


def body(
    velocity_tiles,
    forward_state,
    adjoint_state,
    wavelet,
    source_cell,
    receiver_cell,
    residual,
    aperture_row,
    aperture_col,
):
    groups = lax.axis_size("shot")
    own_cols = groups // AP_ROWS
    caps = (AP_COLS + own_cols) // own_cols
    assert own_cols == AP_COLS and caps == 2 and forward_state.shape[0] == 1
    n_sub = lax.axis_size("sub")
    assert n_sub == 2 * X_CHIPS and groups % GROUP_ROW == 0
    outbound = [
        (g * n_sub + b, g * n_sub + device_of(g, b)) for g in range(groups) for b in range(n_sub)
    ]
    myself = lax.axis_index("shot")
    shots_here = forward_state.shape[0]
    gradient = jnp.zeros(velocity_tiles.shape, jnp.float32)
    every_shot = list(range(shots_here))
    forward_moved = []
    for k in range(shots_here):
        states = forward_state[k].astype(jnp.float32)
        forward_moved.append(lax.ppermute(states, ("shot", "sub"), outbound))
    sending = outgoing(
        velocity_tiles, aperture_row, aperture_col, every_shot, groups, own_cols, caps
    )
    fetched = lax.all_to_all(sending, "shot", split_axis=0, concat_axis=0, tiled=True)
    images = []
    for k in every_shot:
        shot_id = myself * SHOTS_DEV + k
        row_start = aperture_row[shot_id]
        col_start = aperture_col[shot_id]
        model = assemble(fetched, row_start, col_start, own_cols)
        model = lax.ppermute(model, ("shot", "sub"), outbound)
        adjoint_moved = functools.partial(
            lax.ppermute, adjoint_state[k].astype(jnp.float32), ("shot", "sub"), outbound
        )
        image = migrate(
            model,
            forward_moved[k],
            adjoint_moved,
            wavelet[k],
            source_cell[k],
            receiver_cell[k],
            residual[k],
        )
        image = lax.ppermute(image, ("shot", "sub"), [(b, a) for a, b in outbound])
        images.append(disperse(image, row_start, col_start, groups, own_cols, caps))
    returned = lax.all_to_all(images[0], "shot", split_axis=0, concat_axis=0, tiled=True)
    gradient = accumulate(
        gradient, returned, aperture_row, aperture_col, every_shot, groups, own_cols, caps
    )
    return gradient


def solution(mesh):
    placed = (
        P("shot", "sub", None),
        P("shot", None, "sub", None, None),
        P("shot", None, "sub", None, None),
        P("shot", None),
        P("shot"),
        P("shot", None),
        P("shot", None, None),
        P(),
        P(),
    )
    return jax.shard_map(
        body, mesh=mesh, in_specs=placed, out_specs=P("shot", "sub", None), check_vma=False
    )
```

```python
import jax
import jax.numpy as jnp
from jax import lax
from jax.sharding import PartitionSpec as P
from jax.experimental import pallas as pl
from jax.experimental.pallas import tpu as pltpu

TILE = 16
RY = 3
SHOTS_DEV = 1
NT = 4
RADIUS = 4
AP_ROWS = 4
AP_COLS = 8
TILE_DEV = 12
AX = 64
AY = 128


COEFFS = (-205.0 / 72.0, 8.0 / 5.0, -1.0 / 5.0, 8.0 / 315.0, -1.0 / 560.0)
IMAGE_SCALE = 1.0 / 64.0


def padded_2(array, sides, width):
    for axis, dim in sides:
        size, length = (lax.axis_size(axis), array.shape[dim])
        up = [(i, (i + 1) % size) for i in range(size - 1)]
        down = [(j, i) for i, j in up]
        last = lax.slice_in_dim(array, length - width, length, axis=dim)
        first = lax.slice_in_dim(array, 0, width, axis=dim)
        before = lax.ppermute(last, axis, up)
        after = lax.ppermute(first, axis, down)
        array = jnp.concatenate([before, array, after], axis=dim)
    return array


def laplace(padded, depth_cells, row_cells, column_cells):
    r = 4
    center = padded[r : r + depth_cells, r : r + row_cells, r : r + column_cells]
    summed = 3.0 * COEFFS[0] * center
    for k in range(1, 5):
        nearby = padded[r + k : r + k + depth_cells, r : r + row_cells, r : r + column_cells]
        nearby = (
            nearby + padded[r - k : r - k + depth_cells, r : r + row_cells, r : r + column_cells]
        )
        nearby = (
            nearby + padded[r : r + depth_cells, r + k : r + k + row_cells, r : r + column_cells]
        )
        nearby = (
            nearby + padded[r : r + depth_cells, r - k : r - k + row_cells, r : r + column_cells]
        )
        nearby = (
            nearby + padded[r : r + depth_cells, r : r + row_cells, r + k : r + k + column_cells]
        )
        nearby = (
            nearby + padded[r : r + depth_cells, r : r + row_cells, r - k : r - k + column_cells]
        )
        summed = summed + COEFFS[k] * nearby
    return summed


def wave_operator(field):
    padded = padded_2(field, (("sub", 0),), RADIUS)
    padded = jnp.pad(padded, ((0, 0), (4, 4), (4, 4)))
    return laplace(padded, field.shape[0], AX, AY)


def adjoint_operator(field):
    padded = padded_2(field, (("sub", 0),), RADIUS)
    padded = jnp.pad(padded, ((0, 0), (4, 4), (4, 4)))
    return laplace(padded, field.shape[0], AX, AY)


def slot_layout(row_start, col_start, owner_row, owner_col, own_cols, caps):
    block_row = (owner_row - row_start) % AP_ROWS
    first_col = (owner_col - col_start // TILE) % own_cols
    block_col = first_col + own_cols * jnp.arange(caps, dtype=jnp.int32)
    usable = block_col <= AP_COLS
    return (block_row, block_col, usable)


def owner_slots(row_table, col_table, shot_list, groups, own_cols, caps):
    myself = lax.axis_index("shot")
    owner_row = myself // own_cols
    owner_col = myself % own_cols
    senders = jnp.arange(groups, dtype=jnp.int32)[:, None]
    if SHOTS_DEV == 1 and list(shot_list) == [0]:
        row_start = row_table[:groups].reshape(groups, 1, 1)
        col_start = col_table[:groups].reshape(groups, 1, 1)
    else:
        picked = senders * SHOTS_DEV + jnp.asarray(shot_list, dtype=jnp.int32)[None, :]
        row_start = row_table[picked][..., None]
        col_start = col_table[picked][..., None]
    block_row, block_col, usable = slot_layout(
        row_start, col_start, owner_row, owner_col, own_cols, caps
    )
    tile_row = row_start + block_row
    tile_col = col_start // TILE + block_col
    local = tile_row // AP_ROWS * RY + tile_col // own_cols
    local = jnp.clip(local, 0, TILE_DEV - 1)
    return (local.reshape(-1), usable.reshape(-1))


def lane_column():
    return jnp.arange(TILE * TILE, dtype=jnp.int32) % TILE


def merge_slots(pair, spare_ok, offset):
    lower = spare_ok & (lane_column() < offset)
    return jnp.where(lower, pair[:, 1], pair[:, 0])


def outgoing(velocity_tiles, row_table, col_table, shot_list, groups, own_cols, caps):
    local, usable = owner_slots(row_table, col_table, shot_list, groups, own_cols, caps)
    chosen = velocity_tiles[local]
    chosen = jnp.where(usable[:, None, None], chosen, 0.0)
    chosen = chosen.reshape(groups, caps, velocity_tiles.shape[1], velocity_tiles.shape[2])
    usable = usable.reshape(groups, caps)
    offset = (col_table[:groups] % TILE).reshape(groups, 1, 1)
    merged = merge_slots(chosen, usable[:, 1, None, None], offset)
    return merged.reshape(groups, 1, velocity_tiles.shape[1], velocity_tiles.shape[2])


def accumulate(gradient, returned, row_table, col_table, shot_list, groups, own_cols, caps):
    local, usable = owner_slots(row_table, col_table, shot_list, groups, own_cols, caps)
    usable = usable.reshape(groups, caps)
    offset = (col_table[:groups] % TILE).reshape(groups, 1, 1)
    lower = lane_column() < offset
    piece = returned.reshape(groups, gradient.shape[1], gradient.shape[2])
    spare = usable[:, 1, None, None]
    first = jnp.where(spare & lower, 0.0, piece)
    second = jnp.where(spare & lower, piece, 0.0)
    pieces = jnp.stack([first, second], axis=1).reshape(groups * caps, -1)
    hot = (local[:, None] == jnp.arange(gradient.shape[0], dtype=jnp.int32)[None, :]) & usable.reshape(-1)[:, None]
    summed = jnp.einsum(
        "st,sf->tf", hot.astype(jnp.float32), pieces, precision=lax.Precision.HIGHEST
    )
    return gradient + summed.reshape(gradient.shape)


def assemble(received, row_start, col_start, own_cols):
    depth_cells = received.shape[2]
    rel_row = jnp.arange(AP_ROWS, dtype=jnp.int32)[:, None]
    rel_col = jnp.arange(AP_COLS + 1, dtype=jnp.int32)[None, :]
    source_owner = (row_start + rel_row) % AP_ROWS * own_cols + (
        col_start // TILE + rel_col
    ) % own_cols
    flat_index = source_owner.reshape(-1)
    pieces = received.reshape(-1, depth_cells, TILE * TILE)[flat_index]
    block = pieces.reshape(AP_ROWS, AP_COLS + 1, depth_cells, TILE, TILE)
    block = block.transpose(2, 0, 3, 1, 4).reshape(depth_cells, AX, (AP_COLS + 1) * TILE)
    return lax.dynamic_slice_in_dim(block, col_start % TILE, AY, 2)


def disperse(image, row_start, col_start, groups, own_cols, caps):
    depth_cells = image.shape[0]
    wide = jnp.zeros((depth_cells, AX, (AP_COLS + 1) * TILE), jnp.float32)
    wide = lax.dynamic_update_slice_in_dim(wide, image, col_start % TILE, 2)
    pieces = wide.reshape(depth_cells, AP_ROWS, TILE, AP_COLS + 1, TILE)
    pieces = pieces.transpose(1, 3, 0, 2, 4).reshape(
        AP_ROWS * (AP_COLS + 1), depth_cells, TILE * TILE
    )
    owners = jnp.arange(groups, dtype=jnp.int32)[:, None]
    block_row, block_col, usable = slot_layout(
        row_start, col_start, owners // own_cols, owners % own_cols, own_cols, caps
    )
    position = jnp.clip(block_row * (AP_COLS + 1) + block_col, 0, AP_ROWS * (AP_COLS + 1) - 1)
    chosen = jnp.where(usable[..., None, None], pieces[position], 0.0)
    merged = merge_slots(chosen, usable[:, 1, None, None], col_start % TILE)
    return merged.reshape(groups, 1, depth_cells, TILE * TILE)


X_CHIPS = 4
GROUP_ROW = 8


def crossing(group):
    return (group // GROUP_ROW * 2 + group % 2) % X_CHIPS


def mirror(group):
    return group % 2


def block_of(group, sub):
    cross = crossing(group)
    x, side = sub // 2, sub % 2
    flip = mirror(group)
    half = side + flip - 2 * side * flip
    low = (x - cross + 2 * X_CHIPS - 1) % X_CHIPS
    high = X_CHIPS + (cross - x + X_CHIPS) % X_CHIPS
    return (1 - half) * low + half * high


def device_of(group, block):
    cross = crossing(group)
    half = block // X_CHIPS
    low = (cross + 1 + block) % X_CHIPS
    high = (cross - block + 2 * X_CHIPS) % X_CHIPS
    flip = mirror(group)
    side = half + flip - 2 * half * flip
    return ((1 - half) * low + half * high) * 2 + side


def shift_rows(c, k, rows):
    if k > 0:
        moved = pltpu.roll(c, AX - k, 0)
        return jnp.where(rows < AX - k, moved, 0.0)
    moved = pltpu.roll(c, -k, 0)
    return jnp.where(rows >= -k, moved, 0.0)


def shift_lanes(c, k, lanes):
    if k > 0:
        moved = pltpu.roll(c, AY - k, 1)
        return jnp.where(lanes < AY - k, moved, 0.0)
    moved = pltpu.roll(c, -k, 1)
    return jnp.where(lanes >= -k, moved, 0.0)


def plane_stencil(buf, r, p, rows, lanes):
    c = buf[r, p]
    summed = (3.0 * COEFFS[0]) * c
    for k in range(1, 5):
        nearby = buf[r, p + k] + buf[r, p - k]
        nearby = nearby + shift_rows(c, k, rows)
        nearby = nearby + shift_rows(c, -k, rows)
        nearby = nearby + shift_lanes(c, k, lanes)
        nearby = nearby + shift_lanes(c, -k, lanes)
        summed = summed + COEFFS[k] * nearby
    return summed


def split_bf16(values):
    high = values.astype(jnp.bfloat16)
    rest = values - high.astype(jnp.float32)
    middle = rest.astype(jnp.bfloat16)
    low = (rest - middle.astype(jnp.float32)).astype(jnp.bfloat16)
    return (high, middle, low)


def migrate_kernel(
    src_ref, wave_ref, rrow_ref, rcol_ref, resid_ref, model_ref, pf_ref, qa_ref,
    img_ref, pad_p, pad_q, lap, qs, inject, send_sem, recv_sem,
):
    group = lax.axis_index("shot")
    me = block_of(group, lax.axis_index("sub"))
    n_sub = lax.axis_size("sub")
    depth = model_ref.shape[0]
    halo = jnp.zeros((RADIUS, AX, AY), jnp.float32)
    for r in range(NT):
        for buf in (pad_p, pad_q):
            buf[r, 0:RADIUS] = halo
            buf[r, RADIUS + depth : 2 * RADIUS + depth] = halo
    pad_p[0, RADIUS : RADIUS + depth] = pf_ref[0]
    pad_q[0, RADIUS : RADIUS + depth] = model_ref[...] * qa_ref[0]
    up_dev = device_of(group, (me + 1) % n_sub)
    down_dev = device_of(group, (me + n_sub - 1) % n_sub)
    barrier = pltpu.get_barrier_semaphore()
    pl.semaphore_signal(barrier, 1, device_id={"sub": up_dev}, device_id_type=pl.DeviceIdType.MESH)
    pl.semaphore_signal(barrier, 1, device_id={"sub": down_dev}, device_id_type=pl.DeviceIdType.MESH)
    pl.semaphore_wait(barrier, 2)
    rows = lax.broadcasted_iota(jnp.int32, (AX, AY), 0)
    lanes = lax.broadcasted_iota(jnp.int32, (AX, AY), 1)
    n_rec = rcol_ref.shape[0]
    src_level = src_ref[0]
    src_spot = (rows == src_ref[1]) & (lanes == src_ref[2])

    def build_injection(step):
        hit_y = lax.broadcasted_iota(jnp.int32, (n_rec, AY), 1) == rcol_ref[...]
        spread = jnp.where(hit_y, resid_ref[:, step : step + 1], 0.0)
        parts = split_bf16(spread)
        rec_level = rrow_ref[0:1, :]
        hit_x = lax.broadcasted_iota(jnp.int32, (AX, n_rec), 0) == rrow_ref[1:2, :]

        def plane(j, carry):
            picks = (hit_x & (rec_level == j)).astype(jnp.bfloat16)
            total = jnp.dot(picks, parts[0], preferred_element_type=jnp.float32)
            total = total + jnp.dot(picks, parts[1], preferred_element_type=jnp.float32)
            total = total + jnp.dot(picks, parts[2], preferred_element_type=jnp.float32)
            inject[j] = total
            return carry

        lax.fori_loop(0, depth, plane, 0)

    def exchange(r, f):
        buf = (pad_p, pad_q)[f]
        down = pltpu.make_async_remote_copy(
            src_ref=buf.at[r, RADIUS : 2 * RADIUS],
            dst_ref=buf.at[r, RADIUS + depth : 2 * RADIUS + depth],
            send_sem=send_sem.at[r, f, 0],
            recv_sem=recv_sem.at[r, f, 0],
            device_id={"sub": down_dev},
            device_id_type=pl.DeviceIdType.MESH,
        )
        up = pltpu.make_async_remote_copy(
            src_ref=buf.at[r, depth : RADIUS + depth],
            dst_ref=buf.at[r, 0:RADIUS],
            send_sem=send_sem.at[r, f, 1],
            recv_sem=recv_sem.at[r, f, 1],
            device_id={"sub": up_dev},
            device_id_type=pl.DeviceIdType.MESH,
        )

        @pl.when(me > 0)
        def _():
            down.start()

        @pl.when(me < n_sub - 1)
        def _():
            up.start()

        return (down, up)

    def finish(pair):
        down, up = pair

        @pl.when(me > 0)
        def _():
            down.wait_send()
            up.wait_recv()

        @pl.when(me < n_sub - 1)
        def _():
            up.wait_send()
            down.wait_recv()

    def forward_round(r):
        def plane(j, carry):
            p = j + RADIUS
            lp = plane_stencil(pad_p, r, p, rows, lanes)
            lap[r, j] = lp
            if r < NT - 1:
                before = pf_ref[1, j] if r == 0 else pad_p[r - 1, p]
                following = 2.0 * pad_p[r, p] - before + model_ref[j] * lp
                source = jnp.where(src_spot & (src_level == j), wave_ref[r], 0.0)
                pad_p[r + 1, p] = following + source
            return carry

        lax.fori_loop(0, depth, plane, 0)

    def adjoint_round(r):
        def plane(j, carry):
            p = j + RADIUS
            lq = plane_stencil(pad_q, r, p, rows, lanes)
            now = qa_ref[0, j] if r == 0 else qs[r - 1, j]
            if r == 0:
                later = qa_ref[1, j]
            elif r == 1:
                later = qa_ref[0, j]
            else:
                later = qs[r - 2, j]
            result = 2.0 * now - later + lq
            result = result + inject[j]
            if r < NT - 1:
                qs[r, j] = result
                pad_q[r + 1, p] = model_ref[j] * result
            else:
                image = jnp.zeros((AX, AY), jnp.float32)
                for s in range(NT - 1):
                    image = image + qs[s, j] * lap[NT - 1 - s, j]
                image = image + result * lap[0, j]
                img_ref[j] = IMAGE_SCALE * image
            return carry

        lax.fori_loop(0, depth, plane, 0)

    fwd = exchange(0, 0)
    adj = exchange(0, 1)
    build_injection(NT - 1)
    for r in range(NT):
        finish(fwd)
        forward_round(r)
        if r < NT - 1:
            fwd = exchange(r + 1, 0)
        finish(adj)
        adjoint_round(r)
        if r < NT - 1:
            adj = exchange(r + 1, 1)
            build_injection(NT - 2 - r)


def migrate(model, state_fwd, state_adj, wave, source, receivers, resid):
    depth_cells = model.shape[0]
    plane = AX * AY
    offset = block_of(lax.axis_index("shot"), lax.axis_index("sub")) * depth_cells

    def level_of(cells):
        level = cells // plane - offset
        inside = (level >= 0) & (level < depth_cells)
        return jnp.where(inside, level, -1)

    src = jnp.stack([level_of(source), source % plane // AY, source % AY]).astype(jnp.int32)
    rrow = jnp.stack([level_of(receivers), receivers % plane // AY]).astype(jnp.int32)
    rcol = (receivers % AY).astype(jnp.int32).reshape(-1, 1)
    vmem = pl.BlockSpec(memory_space=pltpu.VMEM)
    smem = pl.BlockSpec(memory_space=pltpu.SMEM)
    padded = (NT, depth_cells + 2 * RADIUS, AX, AY)
    field = (NT, depth_cells, AX, AY)
    return pl.pallas_call(
        migrate_kernel,
        out_shape=jax.ShapeDtypeStruct(model.shape, jnp.float32),
        in_specs=[smem, smem] + [vmem] * 6,
        out_specs=vmem,
        scratch_shapes=[
            pltpu.VMEM(padded, jnp.float32),
            pltpu.VMEM(padded, jnp.float32),
            pltpu.VMEM(field, jnp.float32),
            pltpu.VMEM(field, jnp.float32),
            pltpu.VMEM(model.shape, jnp.float32),
            pltpu.SemaphoreType.DMA((NT, 2, 2)),
            pltpu.SemaphoreType.DMA((NT, 2, 2)),
        ],
        compiler_params=pltpu.CompilerParams(collective_id=0, has_side_effects=True),
    )(
        src,
        wave.astype(jnp.float32),
        rrow,
        rcol,
        resid.T,
        model,
        state_fwd.astype(jnp.float32),
        state_adj.astype(jnp.float32),
    )


def body(
    velocity_tiles,
    forward_state,
    adjoint_state,
    wavelet,
    source_cell,
    receiver_cell,
    residual,
    aperture_row,
    aperture_col,
):
    groups = lax.axis_size("shot")
    own_cols = groups // AP_ROWS
    caps = (AP_COLS + own_cols) // own_cols
    assert own_cols == AP_COLS and caps == 2 and forward_state.shape[0] == 1
    n_sub = lax.axis_size("sub")
    assert n_sub == 2 * X_CHIPS and groups % GROUP_ROW == 0
    outbound = [
        (g * n_sub + b, g * n_sub + device_of(g, b)) for g in range(groups) for b in range(n_sub)
    ]
    myself = lax.axis_index("shot")
    shots_here = forward_state.shape[0]
    gradient = jnp.zeros(velocity_tiles.shape, jnp.float32)
    every_shot = list(range(shots_here))
    states_moved = []
    for k in range(shots_here):
        states = jnp.concatenate(
            [forward_state[k].astype(jnp.float32), adjoint_state[k].astype(jnp.float32)]
        )
        states_moved.append(lax.ppermute(states, ("shot", "sub"), outbound))
    sending = outgoing(
        velocity_tiles, aperture_row, aperture_col, every_shot, groups, own_cols, caps
    )
    fetched = lax.all_to_all(sending, "shot", split_axis=0, concat_axis=0, tiled=True)
    images = []
    for k in every_shot:
        shot_id = myself * SHOTS_DEV + k
        row_start = aperture_row[shot_id]
        col_start = aperture_col[shot_id]
        model = assemble(fetched, row_start, col_start, own_cols)
        model = lax.ppermute(model, ("shot", "sub"), outbound)
        states = states_moved[k]
        image = migrate(
            model,
            states[0:2],
            states[2:4],
            wavelet[k],
            source_cell[k],
            receiver_cell[k],
            residual[k],
        )
        image = lax.ppermute(image, ("shot", "sub"), [(b, a) for a, b in outbound])
        images.append(disperse(image, row_start, col_start, groups, own_cols, caps))
    returned = lax.all_to_all(images[0], "shot", split_axis=0, concat_axis=0, tiled=True)
    gradient = accumulate(
        gradient, returned, aperture_row, aperture_col, every_shot, groups, own_cols, caps
    )
    return gradient


def solution(mesh):
    placed = (
        P("shot", "sub", None),
        P("shot", None, "sub", None, None),
        P("shot", None, "sub", None, None),
        P("shot", None),
        P("shot"),
        P("shot", None),
        P("shot", None, None),
        P(),
        P(),
    )
    return jax.shard_map(
        body, mesh=mesh, in_specs=placed, out_specs=P("shot", "sub", None), check_vma=False
    )
```

```python
import jax
import jax.numpy as jnp
from jax import lax
from jax.sharding import PartitionSpec as P
from jax.experimental import pallas as pl
from jax.experimental.pallas import tpu as pltpu

TILE = 16
RY = 3
SHOTS_DEV = 1
NT = 4
RADIUS = 4
AP_ROWS = 4
AP_COLS = 8
TILE_DEV = 12
AX = 64
AY = 128


COEFFS = (-205.0 / 72.0, 8.0 / 5.0, -1.0 / 5.0, 8.0 / 315.0, -1.0 / 560.0)
IMAGE_SCALE = 1.0 / 64.0


def padded_2(array, sides, width):
    for axis, dim in sides:
        size, length = (lax.axis_size(axis), array.shape[dim])
        up = [(i, (i + 1) % size) for i in range(size - 1)]
        down = [(j, i) for i, j in up]
        last = lax.slice_in_dim(array, length - width, length, axis=dim)
        first = lax.slice_in_dim(array, 0, width, axis=dim)
        before = lax.ppermute(last, axis, up)
        after = lax.ppermute(first, axis, down)
        array = jnp.concatenate([before, array, after], axis=dim)
    return array


def laplace(padded, depth_cells, row_cells, column_cells):
    r = 4
    center = padded[r : r + depth_cells, r : r + row_cells, r : r + column_cells]
    summed = 3.0 * COEFFS[0] * center
    for k in range(1, 5):
        nearby = padded[r + k : r + k + depth_cells, r : r + row_cells, r : r + column_cells]
        nearby = (
            nearby + padded[r - k : r - k + depth_cells, r : r + row_cells, r : r + column_cells]
        )
        nearby = (
            nearby + padded[r : r + depth_cells, r + k : r + k + row_cells, r : r + column_cells]
        )
        nearby = (
            nearby + padded[r : r + depth_cells, r - k : r - k + row_cells, r : r + column_cells]
        )
        nearby = (
            nearby + padded[r : r + depth_cells, r : r + row_cells, r + k : r + k + column_cells]
        )
        nearby = (
            nearby + padded[r : r + depth_cells, r : r + row_cells, r - k : r - k + column_cells]
        )
        summed = summed + COEFFS[k] * nearby
    return summed


def wave_operator(field):
    padded = padded_2(field, (("sub", 0),), RADIUS)
    padded = jnp.pad(padded, ((0, 0), (4, 4), (4, 4)))
    return laplace(padded, field.shape[0], AX, AY)


def adjoint_operator(field):
    padded = padded_2(field, (("sub", 0),), RADIUS)
    padded = jnp.pad(padded, ((0, 0), (4, 4), (4, 4)))
    return laplace(padded, field.shape[0], AX, AY)


def slot_layout(row_start, col_start, owner_row, owner_col, own_cols, caps):
    block_row = (owner_row - row_start) % AP_ROWS
    first_col = (owner_col - col_start // TILE) % own_cols
    block_col = first_col + own_cols * jnp.arange(caps, dtype=jnp.int32)
    usable = block_col <= AP_COLS
    return (block_row, block_col, usable)


def owner_slots(row_table, col_table, shot_list, groups, own_cols, caps):
    myself = lax.axis_index("shot")
    owner_row = myself // own_cols
    owner_col = myself % own_cols
    senders = jnp.arange(groups, dtype=jnp.int32)[:, None]
    if SHOTS_DEV == 1 and list(shot_list) == [0]:
        row_start = row_table[:groups].reshape(groups, 1, 1)
        col_start = col_table[:groups].reshape(groups, 1, 1)
    else:
        picked = senders * SHOTS_DEV + jnp.asarray(shot_list, dtype=jnp.int32)[None, :]
        row_start = row_table[picked][..., None]
        col_start = col_table[picked][..., None]
    block_row, block_col, usable = slot_layout(
        row_start, col_start, owner_row, owner_col, own_cols, caps
    )
    tile_row = row_start + block_row
    tile_col = col_start // TILE + block_col
    local = tile_row // AP_ROWS * RY + tile_col // own_cols
    local = jnp.clip(local, 0, TILE_DEV - 1)
    return (local.reshape(-1), usable.reshape(-1))


def lane_column():
    return jnp.arange(TILE * TILE, dtype=jnp.int32) % TILE


def merge_slots(pair, spare_ok, offset):
    lower = spare_ok & (lane_column() < offset)
    return jnp.where(lower, pair[:, 1], pair[:, 0])


def outgoing(velocity_tiles, row_table, col_table, shot_list, groups, own_cols, caps):
    local, usable = owner_slots(row_table, col_table, shot_list, groups, own_cols, caps)
    chosen = velocity_tiles[local]
    chosen = jnp.where(usable[:, None, None], chosen, 0.0)
    chosen = chosen.reshape(groups, caps, velocity_tiles.shape[1], velocity_tiles.shape[2])
    usable = usable.reshape(groups, caps)
    offset = (col_table[:groups] % TILE).reshape(groups, 1, 1)
    merged = merge_slots(chosen, usable[:, 1, None, None], offset)
    return merged.reshape(groups, 1, velocity_tiles.shape[1], velocity_tiles.shape[2])


def accumulate(gradient, returned, row_table, col_table, shot_list, groups, own_cols, caps):
    local, usable = owner_slots(row_table, col_table, shot_list, groups, own_cols, caps)
    usable = usable.reshape(groups, caps)
    offset = (col_table[:groups] % TILE).reshape(groups, 1, 1)
    lower = lane_column() < offset
    piece = returned.reshape(groups, gradient.shape[1], gradient.shape[2])
    spare = usable[:, 1, None, None]
    first = jnp.where(spare & lower, 0.0, piece)
    second = jnp.where(spare & lower, piece, 0.0)
    pieces = jnp.stack([first, second], axis=1).reshape(groups * caps, -1)
    hot = (local[:, None] == jnp.arange(gradient.shape[0], dtype=jnp.int32)[None, :]) & usable.reshape(-1)[:, None]
    summed = jnp.einsum(
        "st,sf->tf", hot.astype(jnp.float32), pieces, precision=lax.Precision.HIGHEST
    )
    return gradient + summed.reshape(gradient.shape)


def assemble(received, row_start, col_start, own_cols):
    depth_cells = received.shape[2]
    rel_row = jnp.arange(AP_ROWS, dtype=jnp.int32)[:, None]
    rel_col = jnp.arange(AP_COLS + 1, dtype=jnp.int32)[None, :]
    source_owner = (row_start + rel_row) % AP_ROWS * own_cols + (
        col_start // TILE + rel_col
    ) % own_cols
    flat_index = source_owner.reshape(-1)
    pieces = received.reshape(-1, depth_cells, TILE * TILE)[flat_index]
    block = pieces.reshape(AP_ROWS, AP_COLS + 1, depth_cells, TILE, TILE)
    block = block.transpose(2, 0, 3, 1, 4).reshape(depth_cells, AX, (AP_COLS + 1) * TILE)
    return lax.dynamic_slice_in_dim(block, col_start % TILE, AY, 2)


def disperse(image, row_start, col_start, groups, own_cols, caps):
    depth_cells = image.shape[0]
    wide = jnp.zeros((depth_cells, AX, (AP_COLS + 1) * TILE), jnp.float32)
    wide = lax.dynamic_update_slice_in_dim(wide, image, col_start % TILE, 2)
    pieces = wide.reshape(depth_cells, AP_ROWS, TILE, AP_COLS + 1, TILE)
    pieces = pieces.transpose(1, 3, 0, 2, 4).reshape(
        AP_ROWS * (AP_COLS + 1), depth_cells, TILE * TILE
    )
    owners = jnp.arange(groups, dtype=jnp.int32)[:, None]
    block_row, block_col, usable = slot_layout(
        row_start, col_start, owners // own_cols, owners % own_cols, own_cols, caps
    )
    position = jnp.clip(block_row * (AP_COLS + 1) + block_col, 0, AP_ROWS * (AP_COLS + 1) - 1)
    chosen = jnp.where(usable[..., None, None], pieces[position], 0.0)
    merged = merge_slots(chosen, usable[:, 1, None, None], col_start % TILE)
    return merged.reshape(groups, 1, depth_cells, TILE * TILE)


X_CHIPS = 4
GROUP_ROW = 8


def crossing(group):
    return (group // GROUP_ROW * 2 + group % 2) % X_CHIPS


def mirror(group):
    return group % 2


def block_of(group, sub):
    cross = crossing(group)
    x, side = sub // 2, sub % 2
    flip = mirror(group)
    half = side + flip - 2 * side * flip
    low = (x - cross + 2 * X_CHIPS - 1) % X_CHIPS
    high = X_CHIPS + (cross - x + X_CHIPS) % X_CHIPS
    return (1 - half) * low + half * high


def device_of(group, block):
    cross = crossing(group)
    half = block // X_CHIPS
    low = (cross + 1 + block) % X_CHIPS
    high = (cross - block + 2 * X_CHIPS) % X_CHIPS
    flip = mirror(group)
    side = half + flip - 2 * half * flip
    return ((1 - half) * low + half * high) * 2 + side


def shift_rows(c, k, rows):
    if k > 0:
        moved = pltpu.roll(c, AX - k, 0)
        return jnp.where(rows < AX - k, moved, 0.0)
    moved = pltpu.roll(c, -k, 0)
    return jnp.where(rows >= -k, moved, 0.0)


def shift_lanes(c, k, lanes):
    if k > 0:
        moved = pltpu.roll(c, AY - k, 1)
        return jnp.where(lanes < AY - k, moved, 0.0)
    moved = pltpu.roll(c, -k, 1)
    return jnp.where(lanes >= -k, moved, 0.0)


def plane_stencil(buf, r, p, rows, lanes):
    c = buf[r, p]
    summed = (3.0 * COEFFS[0]) * c
    for k in range(1, 5):
        nearby = buf[r, p + k] + buf[r, p - k]
        nearby = nearby + shift_rows(c, k, rows)
        nearby = nearby + shift_rows(c, -k, rows)
        nearby = nearby + shift_lanes(c, k, lanes)
        nearby = nearby + shift_lanes(c, -k, lanes)
        summed = summed + COEFFS[k] * nearby
    return summed


def split_bf16(values):
    high = values.astype(jnp.bfloat16)
    rest = values - high.astype(jnp.float32)
    middle = rest.astype(jnp.bfloat16)
    low = (rest - middle.astype(jnp.float32)).astype(jnp.bfloat16)
    return (high, middle, low)


def migrate_kernel(
    src_ref, wave_ref, rrow_ref, rcol_ref, resid_ref, model_ref, pf_ref, qa_ref,
    img_ref, pad_p, pad_q, lap, qs, inject, model_scr, send_sem, recv_sem, model_sem,
):
    group = lax.axis_index("shot")
    sub = lax.axis_index("sub")
    me = block_of(group, sub)
    n_sub = lax.axis_size("sub")
    depth = model_ref.shape[0]
    halo = jnp.zeros((RADIUS, AX, AY), jnp.float32)
    for r in range(NT):
        for buf in (pad_p, pad_q):
            buf[r, 0:RADIUS] = halo
            buf[r, RADIUS + depth : 2 * RADIUS + depth] = halo
    pad_p[0, RADIUS : RADIUS + depth] = pf_ref[0]
    up_dev = device_of(group, (me + 1) % n_sub)
    down_dev = device_of(group, (me + n_sub - 1) % n_sub)
    target = device_of(group, sub)
    moved = target != sub
    mesh_id = pl.DeviceIdType.MESH
    barrier = pltpu.get_barrier_semaphore()
    pl.semaphore_signal(barrier, 1, device_id={"sub": up_dev}, device_id_type=mesh_id)
    pl.semaphore_signal(barrier, 1, device_id={"sub": down_dev}, device_id_type=mesh_id)

    @pl.when(moved)
    def _():
        pl.semaphore_signal(barrier, 1, device_id={"sub": target}, device_id_type=mesh_id)
        pl.semaphore_signal(barrier, 1, device_id={"sub": me}, device_id_type=mesh_id)
        pl.semaphore_wait(barrier, 4)

    @pl.when(jnp.logical_not(moved))
    def _():
        pl.semaphore_wait(barrier, 2)

    model_copy = pltpu.make_async_remote_copy(
        src_ref=model_ref,
        dst_ref=model_scr,
        send_sem=model_sem.at[0],
        recv_sem=model_sem.at[1],
        device_id={"sub": target},
        device_id_type=mesh_id,
    )
    model_local = pltpu.make_async_copy(model_ref, model_scr, model_sem.at[2])

    @pl.when(moved)
    def _():
        model_copy.start()

    @pl.when(jnp.logical_not(moved))
    def _():
        model_local.start()
    rows = lax.broadcasted_iota(jnp.int32, (AX, AY), 0)
    lanes = lax.broadcasted_iota(jnp.int32, (AX, AY), 1)
    n_rec = rcol_ref.shape[0]
    src_level = src_ref[0]
    src_spot = (rows == src_ref[1]) & (lanes == src_ref[2])

    def build_injection(step):
        hit_y = lax.broadcasted_iota(jnp.int32, (n_rec, AY), 1) == rcol_ref[...]
        spread = jnp.where(hit_y, resid_ref[:, step : step + 1], 0.0)
        parts = split_bf16(spread)
        rec_level = rrow_ref[0:1, :]
        hit_x = lax.broadcasted_iota(jnp.int32, (AX, n_rec), 0) == rrow_ref[1:2, :]

        def plane(j, carry):
            picks = (hit_x & (rec_level == j)).astype(jnp.bfloat16)
            total = jnp.dot(picks, parts[0], preferred_element_type=jnp.float32)
            total = total + jnp.dot(picks, parts[1], preferred_element_type=jnp.float32)
            total = total + jnp.dot(picks, parts[2], preferred_element_type=jnp.float32)
            inject[j] = total
            return carry

        lax.fori_loop(0, depth, plane, 0)

    def exchange(r, f):
        buf = (pad_p, pad_q)[f]
        down = pltpu.make_async_remote_copy(
            src_ref=buf.at[r, RADIUS : 2 * RADIUS],
            dst_ref=buf.at[r, RADIUS + depth : 2 * RADIUS + depth],
            send_sem=send_sem.at[r, f, 0],
            recv_sem=recv_sem.at[r, f, 0],
            device_id={"sub": down_dev},
            device_id_type=pl.DeviceIdType.MESH,
        )
        up = pltpu.make_async_remote_copy(
            src_ref=buf.at[r, depth : RADIUS + depth],
            dst_ref=buf.at[r, 0:RADIUS],
            send_sem=send_sem.at[r, f, 1],
            recv_sem=recv_sem.at[r, f, 1],
            device_id={"sub": up_dev},
            device_id_type=pl.DeviceIdType.MESH,
        )

        @pl.when(me > 0)
        def _():
            down.start()

        @pl.when(me < n_sub - 1)
        def _():
            up.start()

        return (down, up)

    def finish(pair):
        down, up = pair

        @pl.when(me > 0)
        def _():
            down.wait_send()
            up.wait_recv()

        @pl.when(me < n_sub - 1)
        def _():
            up.wait_send()
            down.wait_recv()

    def forward_round(r):
        def plane(j, carry):
            p = j + RADIUS
            lp = plane_stencil(pad_p, r, p, rows, lanes)
            lap[r, j] = lp
            if r < NT - 1:
                before = pf_ref[1, j] if r == 0 else pad_p[r - 1, p]
                following = 2.0 * pad_p[r, p] - before + model_scr[j] * lp
                source = jnp.where(src_spot & (src_level == j), wave_ref[r], 0.0)
                pad_p[r + 1, p] = following + source
            return carry

        lax.fori_loop(0, depth, plane, 0)

    def adjoint_round(r):
        def plane(j, carry):
            p = j + RADIUS
            lq = plane_stencil(pad_q, r, p, rows, lanes)
            now = qa_ref[0, j] if r == 0 else qs[r - 1, j]
            if r == 0:
                later = qa_ref[1, j]
            elif r == 1:
                later = qa_ref[0, j]
            else:
                later = qs[r - 2, j]
            result = 2.0 * now - later + lq
            result = result + inject[j]
            if r < NT - 1:
                qs[r, j] = result
                pad_q[r + 1, p] = model_scr[j] * result
            else:
                image = jnp.zeros((AX, AY), jnp.float32)
                for s in range(NT - 1):
                    image = image + qs[s, j] * lap[NT - 1 - s, j]
                image = image + result * lap[0, j]
                img_ref[j] = IMAGE_SCALE * image
            return carry

        lax.fori_loop(0, depth, plane, 0)

    fwd = exchange(0, 0)

    @pl.when(moved)
    def _():
        model_copy.wait_send()
        model_copy.wait_recv()

    @pl.when(jnp.logical_not(moved))
    def _():
        model_local.wait()

    pad_q[0, RADIUS : RADIUS + depth] = model_scr[...] * qa_ref[0]
    adj = exchange(0, 1)
    build_injection(NT - 1)
    for r in range(NT):
        finish(fwd)
        forward_round(r)
        if r < NT - 1:
            fwd = exchange(r + 1, 0)
        finish(adj)
        adjoint_round(r)
        if r < NT - 1:
            adj = exchange(r + 1, 1)
            build_injection(NT - 2 - r)


def migrate(model, state_fwd, state_adj, wave, source, receivers, resid):
    depth_cells = model.shape[0]
    plane = AX * AY
    offset = block_of(lax.axis_index("shot"), lax.axis_index("sub")) * depth_cells

    def level_of(cells):
        level = cells // plane - offset
        inside = (level >= 0) & (level < depth_cells)
        return jnp.where(inside, level, -1)

    src = jnp.stack([level_of(source), source % plane // AY, source % AY]).astype(jnp.int32)
    rrow = jnp.stack([level_of(receivers), receivers % plane // AY]).astype(jnp.int32)
    rcol = (receivers % AY).astype(jnp.int32).reshape(-1, 1)
    vmem = pl.BlockSpec(memory_space=pltpu.VMEM)
    smem = pl.BlockSpec(memory_space=pltpu.SMEM)
    padded = (NT, depth_cells + 2 * RADIUS, AX, AY)
    field = (NT, depth_cells, AX, AY)
    return pl.pallas_call(
        migrate_kernel,
        out_shape=jax.ShapeDtypeStruct(model.shape, jnp.float32),
        in_specs=[smem, smem] + [vmem] * 6,
        out_specs=vmem,
        scratch_shapes=[
            pltpu.VMEM(padded, jnp.float32),
            pltpu.VMEM(padded, jnp.float32),
            pltpu.VMEM(field, jnp.float32),
            pltpu.VMEM(field, jnp.float32),
            pltpu.VMEM(model.shape, jnp.float32),
            pltpu.VMEM(model.shape, jnp.float32),
            pltpu.SemaphoreType.DMA((NT, 2, 2)),
            pltpu.SemaphoreType.DMA((NT, 2, 2)),
            pltpu.SemaphoreType.DMA((3,)),
        ],
        compiler_params=pltpu.CompilerParams(collective_id=0, has_side_effects=True),
    )(
        src,
        wave.astype(jnp.float32),
        rrow,
        rcol,
        resid.T,
        model,
        state_fwd.astype(jnp.float32),
        state_adj.astype(jnp.float32),
    )


def body(
    velocity_tiles,
    forward_state,
    adjoint_state,
    wavelet,
    source_cell,
    receiver_cell,
    residual,
    aperture_row,
    aperture_col,
):
    groups = lax.axis_size("shot")
    own_cols = groups // AP_ROWS
    caps = (AP_COLS + own_cols) // own_cols
    assert own_cols == AP_COLS and caps == 2 and forward_state.shape[0] == 1
    n_sub = lax.axis_size("sub")
    assert n_sub == 2 * X_CHIPS and groups % GROUP_ROW == 0
    outbound = [
        (g * n_sub + b, g * n_sub + device_of(g, b)) for g in range(groups) for b in range(n_sub)
    ]
    myself = lax.axis_index("shot")
    shots_here = forward_state.shape[0]
    gradient = jnp.zeros(velocity_tiles.shape, jnp.float32)
    every_shot = list(range(shots_here))
    states_moved = []
    for k in range(shots_here):
        states = jnp.concatenate(
            [forward_state[k].astype(jnp.float32), adjoint_state[k].astype(jnp.float32)]
        )
        states_moved.append(lax.ppermute(states, ("shot", "sub"), outbound))
    sending = outgoing(
        velocity_tiles, aperture_row, aperture_col, every_shot, groups, own_cols, caps
    )
    fetched = lax.all_to_all(sending, "shot", split_axis=0, concat_axis=0, tiled=True)
    images = []
    for k in every_shot:
        shot_id = myself * SHOTS_DEV + k
        row_start = aperture_row[shot_id]
        col_start = aperture_col[shot_id]
        model = assemble(fetched, row_start, col_start, own_cols)
        states = states_moved[k]
        image = migrate(
            model,
            states[0:2],
            states[2:4],
            wavelet[k],
            source_cell[k],
            receiver_cell[k],
            residual[k],
        )
        image = lax.ppermute(image, ("shot", "sub"), [(b, a) for a, b in outbound])
        images.append(disperse(image, row_start, col_start, groups, own_cols, caps))
    returned = lax.all_to_all(images[0], "shot", split_axis=0, concat_axis=0, tiled=True)
    gradient = accumulate(
        gradient, returned, aperture_row, aperture_col, every_shot, groups, own_cols, caps
    )
    return gradient


def solution(mesh):
    placed = (
        P("shot", "sub", None),
        P("shot", None, "sub", None, None),
        P("shot", None, "sub", None, None),
        P("shot", None),
        P("shot"),
        P("shot", None),
        P("shot", None, None),
        P(),
        P(),
    )
    return jax.shard_map(
        body, mesh=mesh, in_specs=placed, out_specs=P("shot", "sub", None), check_vma=False
    )
```

```python
import jax
import jax.numpy as jnp
from jax import lax
from jax.sharding import PartitionSpec as P
from jax.experimental import pallas as pl
from jax.experimental.pallas import tpu as pltpu

TILE = 16
RY = 3
SHOTS_DEV = 1
NT = 4
RADIUS = 4
AP_ROWS = 4
AP_COLS = 8
TILE_DEV = 12
AX = 64
AY = 128


COEFFS = (-205.0 / 72.0, 8.0 / 5.0, -1.0 / 5.0, 8.0 / 315.0, -1.0 / 560.0)
IMAGE_SCALE = 1.0 / 64.0


def padded_2(array, sides, width):
    for axis, dim in sides:
        size, length = (lax.axis_size(axis), array.shape[dim])
        up = [(i, (i + 1) % size) for i in range(size - 1)]
        down = [(j, i) for i, j in up]
        last = lax.slice_in_dim(array, length - width, length, axis=dim)
        first = lax.slice_in_dim(array, 0, width, axis=dim)
        before = lax.ppermute(last, axis, up)
        after = lax.ppermute(first, axis, down)
        array = jnp.concatenate([before, array, after], axis=dim)
    return array


def laplace(padded, depth_cells, row_cells, column_cells):
    r = 4
    center = padded[r : r + depth_cells, r : r + row_cells, r : r + column_cells]
    summed = 3.0 * COEFFS[0] * center
    for k in range(1, 5):
        nearby = padded[r + k : r + k + depth_cells, r : r + row_cells, r : r + column_cells]
        nearby = (
            nearby + padded[r - k : r - k + depth_cells, r : r + row_cells, r : r + column_cells]
        )
        nearby = (
            nearby + padded[r : r + depth_cells, r + k : r + k + row_cells, r : r + column_cells]
        )
        nearby = (
            nearby + padded[r : r + depth_cells, r - k : r - k + row_cells, r : r + column_cells]
        )
        nearby = (
            nearby + padded[r : r + depth_cells, r : r + row_cells, r + k : r + k + column_cells]
        )
        nearby = (
            nearby + padded[r : r + depth_cells, r : r + row_cells, r - k : r - k + column_cells]
        )
        summed = summed + COEFFS[k] * nearby
    return summed


def wave_operator(field):
    padded = padded_2(field, (("sub", 0),), RADIUS)
    padded = jnp.pad(padded, ((0, 0), (4, 4), (4, 4)))
    return laplace(padded, field.shape[0], AX, AY)


def adjoint_operator(field):
    padded = padded_2(field, (("sub", 0),), RADIUS)
    padded = jnp.pad(padded, ((0, 0), (4, 4), (4, 4)))
    return laplace(padded, field.shape[0], AX, AY)


def slot_layout(row_start, col_start, owner_row, owner_col, own_cols, caps):
    block_row = (owner_row - row_start) % AP_ROWS
    first_col = (owner_col - col_start // TILE) % own_cols
    block_col = first_col + own_cols * jnp.arange(caps, dtype=jnp.int32)
    usable = block_col <= AP_COLS
    return (block_row, block_col, usable)


def owner_slots(row_table, col_table, shot_list, groups, own_cols, caps):
    myself = lax.axis_index("shot")
    owner_row = myself // own_cols
    owner_col = myself % own_cols
    senders = jnp.arange(groups, dtype=jnp.int32)[:, None]
    if SHOTS_DEV == 1 and list(shot_list) == [0]:
        row_start = row_table[:groups].reshape(groups, 1, 1)
        col_start = col_table[:groups].reshape(groups, 1, 1)
    else:
        picked = senders * SHOTS_DEV + jnp.asarray(shot_list, dtype=jnp.int32)[None, :]
        row_start = row_table[picked][..., None]
        col_start = col_table[picked][..., None]
    block_row, block_col, usable = slot_layout(
        row_start, col_start, owner_row, owner_col, own_cols, caps
    )
    tile_row = row_start + block_row
    tile_col = col_start // TILE + block_col
    local = tile_row // AP_ROWS * RY + tile_col // own_cols
    local = jnp.clip(local, 0, TILE_DEV - 1)
    return (local.reshape(-1), usable.reshape(-1))


def lane_column():
    return jnp.arange(TILE * TILE, dtype=jnp.int32) % TILE


def merge_slots(pair, spare_ok, offset):
    lower = spare_ok & (lane_column() < offset)
    return jnp.where(lower, pair[:, 1], pair[:, 0])


def outgoing(velocity_tiles, row_table, col_table, shot_list, groups, own_cols, caps):
    local, usable = owner_slots(row_table, col_table, shot_list, groups, own_cols, caps)
    chosen = velocity_tiles[local]
    chosen = jnp.where(usable[:, None, None], chosen, 0.0)
    chosen = chosen.reshape(groups, caps, velocity_tiles.shape[1], velocity_tiles.shape[2])
    usable = usable.reshape(groups, caps)
    offset = (col_table[:groups] % TILE).reshape(groups, 1, 1)
    merged = merge_slots(chosen, usable[:, 1, None, None], offset)
    return merged.reshape(groups, 1, velocity_tiles.shape[1], velocity_tiles.shape[2])


def accumulate(gradient, returned, row_table, col_table, shot_list, groups, own_cols, caps):
    local, usable = owner_slots(row_table, col_table, shot_list, groups, own_cols, caps)
    usable = usable.reshape(groups, caps)
    offset = (col_table[:groups] % TILE).reshape(groups, 1, 1)
    lower = lane_column() < offset
    piece = returned.reshape(groups, gradient.shape[1], gradient.shape[2])
    spare = usable[:, 1, None, None]
    first = jnp.where(spare & lower, 0.0, piece)
    second = jnp.where(spare & lower, piece, 0.0)
    pieces = jnp.stack([first, second], axis=1).reshape(groups * caps, -1)
    hot = (local[:, None] == jnp.arange(gradient.shape[0], dtype=jnp.int32)[None, :]) & usable.reshape(-1)[:, None]
    summed = jnp.einsum(
        "st,sf->tf", hot.astype(jnp.float32), pieces, precision=lax.Precision.HIGHEST
    )
    return gradient + summed.reshape(gradient.shape)


def assemble(received, row_start, col_start, own_cols):
    depth_cells = received.shape[2]
    rel_row = jnp.arange(AP_ROWS, dtype=jnp.int32)[:, None]
    rel_col = jnp.arange(AP_COLS + 1, dtype=jnp.int32)[None, :]
    source_owner = (row_start + rel_row) % AP_ROWS * own_cols + (
        col_start // TILE + rel_col
    ) % own_cols
    flat_index = source_owner.reshape(-1)
    pieces = received.reshape(-1, depth_cells, TILE * TILE)[flat_index]
    block = pieces.reshape(AP_ROWS, AP_COLS + 1, depth_cells, TILE, TILE)
    block = block.transpose(2, 0, 3, 1, 4).reshape(depth_cells, AX, (AP_COLS + 1) * TILE)
    return lax.dynamic_slice_in_dim(block, col_start % TILE, AY, 2)


def disperse(image, row_start, col_start, groups, own_cols, caps):
    depth_cells = image.shape[0]
    wide = jnp.zeros((depth_cells, AX, (AP_COLS + 1) * TILE), jnp.float32)
    wide = lax.dynamic_update_slice_in_dim(wide, image, col_start % TILE, 2)
    pieces = wide.reshape(depth_cells, AP_ROWS, TILE, AP_COLS + 1, TILE)
    pieces = pieces.transpose(1, 3, 0, 2, 4).reshape(
        AP_ROWS * (AP_COLS + 1), depth_cells, TILE * TILE
    )
    owners = jnp.arange(groups, dtype=jnp.int32)[:, None]
    block_row, block_col, usable = slot_layout(
        row_start, col_start, owners // own_cols, owners % own_cols, own_cols, caps
    )
    position = jnp.clip(block_row * (AP_COLS + 1) + block_col, 0, AP_ROWS * (AP_COLS + 1) - 1)
    chosen = jnp.where(usable[..., None, None], pieces[position], 0.0)
    merged = merge_slots(chosen, usable[:, 1, None, None], col_start % TILE)
    return merged.reshape(groups, 1, depth_cells, TILE * TILE)


X_CHIPS = 4
GROUP_ROW = 8


def crossing(group):
    return (group // GROUP_ROW * 2 + group % 2) % X_CHIPS


def mirror(group):
    return group % 2


def block_of(group, sub):
    cross = crossing(group)
    x, side = sub // 2, sub % 2
    flip = mirror(group)
    half = side + flip - 2 * side * flip
    low = (x - cross + 2 * X_CHIPS - 1) % X_CHIPS
    high = X_CHIPS + (cross - x + X_CHIPS) % X_CHIPS
    return (1 - half) * low + half * high


def device_of(group, block):
    cross = crossing(group)
    half = block // X_CHIPS
    low = (cross + 1 + block) % X_CHIPS
    high = (cross - block + 2 * X_CHIPS) % X_CHIPS
    flip = mirror(group)
    side = half + flip - 2 * half * flip
    return ((1 - half) * low + half * high) * 2 + side


def shift_rows(c, k, rows):
    if k > 0:
        moved = pltpu.roll(c, AX - k, 0)
        return jnp.where(rows < AX - k, moved, 0.0)
    moved = pltpu.roll(c, -k, 0)
    return jnp.where(rows >= -k, moved, 0.0)


def shift_lanes(c, k, lanes):
    if k > 0:
        moved = pltpu.roll(c, AY - k, 1)
        return jnp.where(lanes < AY - k, moved, 0.0)
    moved = pltpu.roll(c, -k, 1)
    return jnp.where(lanes >= -k, moved, 0.0)


def plane_stencil(buf, r, p, rows, lanes):
    c = buf[r, p]
    summed = (3.0 * COEFFS[0]) * c
    for k in range(1, 5):
        nearby = buf[r, p + k] + buf[r, p - k]
        nearby = nearby + shift_rows(c, k, rows)
        nearby = nearby + shift_rows(c, -k, rows)
        nearby = nearby + shift_lanes(c, k, lanes)
        nearby = nearby + shift_lanes(c, -k, lanes)
        summed = summed + COEFFS[k] * nearby
    return summed


def split_bf16(values):
    high = values.astype(jnp.bfloat16)
    rest = values - high.astype(jnp.float32)
    middle = rest.astype(jnp.bfloat16)
    low = (rest - middle.astype(jnp.float32)).astype(jnp.bfloat16)
    return (high, middle, low)


def migrate_kernel(
    src_ref, wave_ref, rrow_ref, rcol_ref, resid_ref, model_ref, pf_ref, qa_ref,
    img_ref, pad_p, pad_q, lap, qs, inject, send_sem, recv_sem,
):
    group = lax.axis_index("shot")
    me = block_of(group, lax.axis_index("sub"))
    n_sub = lax.axis_size("sub")
    depth = model_ref.shape[0]
    halo = jnp.zeros((RADIUS, AX, AY), jnp.float32)
    for r in range(NT):
        for buf in (pad_p, pad_q):
            buf[r, 0:RADIUS] = halo
            buf[r, RADIUS + depth : 2 * RADIUS + depth] = halo
    pad_p[0, RADIUS : RADIUS + depth] = pf_ref[0]
    pad_q[0, RADIUS : RADIUS + depth] = model_ref[...] * qa_ref[0]
    up_dev = device_of(group, (me + 1) % n_sub)
    down_dev = device_of(group, (me + n_sub - 1) % n_sub)
    barrier = pltpu.get_barrier_semaphore()
    pl.semaphore_signal(barrier, 1, device_id={"sub": up_dev}, device_id_type=pl.DeviceIdType.MESH)
    pl.semaphore_signal(barrier, 1, device_id={"sub": down_dev}, device_id_type=pl.DeviceIdType.MESH)
    pl.semaphore_wait(barrier, 2)
    rows = lax.broadcasted_iota(jnp.int32, (AX, AY), 0)
    lanes = lax.broadcasted_iota(jnp.int32, (AX, AY), 1)
    n_rec = rcol_ref.shape[0]
    src_level = src_ref[0]
    src_spot = (rows == src_ref[1]) & (lanes == src_ref[2])

    def build_injection(step):
        hit_y = lax.broadcasted_iota(jnp.int32, (n_rec, AY), 1) == rcol_ref[...]
        spread = jnp.where(hit_y, resid_ref[:, step : step + 1], 0.0)
        parts = split_bf16(spread)
        rec_level = rrow_ref[0:1, :]
        hit_x = lax.broadcasted_iota(jnp.int32, (AX, n_rec), 0) == rrow_ref[1:2, :]

        def plane(j, carry):
            picks = (hit_x & (rec_level == j)).astype(jnp.bfloat16)
            total = jnp.dot(picks, parts[0], preferred_element_type=jnp.float32)
            total = total + jnp.dot(picks, parts[1], preferred_element_type=jnp.float32)
            total = total + jnp.dot(picks, parts[2], preferred_element_type=jnp.float32)
            inject[j] = total
            return carry

        lax.fori_loop(0, depth, plane, 0)

    def exchange(r, f):
        buf = (pad_p, pad_q)[f]
        down = pltpu.make_async_remote_copy(
            src_ref=buf.at[r, RADIUS : 2 * RADIUS],
            dst_ref=buf.at[r, RADIUS + depth : 2 * RADIUS + depth],
            send_sem=send_sem.at[r, f, 0],
            recv_sem=recv_sem.at[r, f, 0],
            device_id={"sub": down_dev},
            device_id_type=pl.DeviceIdType.MESH,
        )
        up = pltpu.make_async_remote_copy(
            src_ref=buf.at[r, depth : RADIUS + depth],
            dst_ref=buf.at[r, 0:RADIUS],
            send_sem=send_sem.at[r, f, 1],
            recv_sem=recv_sem.at[r, f, 1],
            device_id={"sub": up_dev},
            device_id_type=pl.DeviceIdType.MESH,
        )

        @pl.when(me > 0)
        def _():
            down.start()

        @pl.when(me < n_sub - 1)
        def _():
            up.start()

        return (down, up)

    def finish(pair):
        down, up = pair

        @pl.when(me > 0)
        def _():
            down.wait_send()
            up.wait_recv()

        @pl.when(me < n_sub - 1)
        def _():
            up.wait_send()
            down.wait_recv()

    def forward_round(r):
        def plane(j, carry):
            p = j + RADIUS
            lp = plane_stencil(pad_p, r, p, rows, lanes)
            lap[r, j] = lp
            if r < NT - 1:
                before = pf_ref[1, j] if r == 0 else pad_p[r - 1, p]
                following = 2.0 * pad_p[r, p] - before + model_ref[j] * lp
                source = jnp.where(src_spot & (src_level == j), wave_ref[r], 0.0)
                pad_p[r + 1, p] = following + source
            return carry

        lax.fori_loop(0, depth, plane, 0)

    def adjoint_round(r):
        def plane(j, carry):
            p = j + RADIUS
            lq = plane_stencil(pad_q, r, p, rows, lanes)
            now = qa_ref[0, j] if r == 0 else qs[r - 1, j]
            if r == 0:
                later = qa_ref[1, j]
            elif r == 1:
                later = qa_ref[0, j]
            else:
                later = qs[r - 2, j]
            result = 2.0 * now - later + lq
            result = result + inject[j]
            if r < NT - 1:
                qs[r, j] = result
                pad_q[r + 1, p] = model_ref[j] * result
            else:
                image = jnp.zeros((AX, AY), jnp.float32)
                for s in range(NT - 1):
                    image = image + qs[s, j] * lap[NT - 1 - s, j]
                image = image + result * lap[0, j]
                img_ref[j] = IMAGE_SCALE * image
            return carry

        lax.fori_loop(0, depth, plane, 0)

    fwd = exchange(0, 0)
    adj = exchange(0, 1)
    build_injection(NT - 1)
    for r in range(NT):
        finish(fwd)
        forward_round(r)
        if r < NT - 1:
            fwd = exchange(r + 1, 0)
        finish(adj)
        adjoint_round(r)
        if r < NT - 1:
            adj = exchange(r + 1, 1)
            build_injection(NT - 2 - r)


def migrate(model, state_fwd, state_adj, wave, source, receivers, resid):
    depth_cells = model.shape[0]
    plane = AX * AY
    offset = block_of(lax.axis_index("shot"), lax.axis_index("sub")) * depth_cells

    def level_of(cells):
        level = cells // plane - offset
        inside = (level >= 0) & (level < depth_cells)
        return jnp.where(inside, level, -1)

    src = jnp.stack([level_of(source), source % plane // AY, source % AY]).astype(jnp.int32)
    rrow = jnp.stack([level_of(receivers), receivers % plane // AY]).astype(jnp.int32)
    rcol = (receivers % AY).astype(jnp.int32).reshape(-1, 1)
    vmem = pl.BlockSpec(memory_space=pltpu.VMEM)
    smem = pl.BlockSpec(memory_space=pltpu.SMEM)
    padded = (NT, depth_cells + 2 * RADIUS, AX, AY)
    field = (NT, depth_cells, AX, AY)
    return pl.pallas_call(
        migrate_kernel,
        out_shape=jax.ShapeDtypeStruct(model.shape, jnp.float32),
        in_specs=[smem, smem] + [vmem] * 6,
        out_specs=vmem,
        scratch_shapes=[
            pltpu.VMEM(padded, jnp.float32),
            pltpu.VMEM(padded, jnp.float32),
            pltpu.VMEM(field, jnp.float32),
            pltpu.VMEM(field, jnp.float32),
            pltpu.VMEM(model.shape, jnp.float32),
            pltpu.SemaphoreType.DMA((NT, 2, 2)),
            pltpu.SemaphoreType.DMA((NT, 2, 2)),
        ],
        compiler_params=pltpu.CompilerParams(collective_id=0, has_side_effects=True),
    )(
        src,
        wave.astype(jnp.float32),
        rrow,
        rcol,
        resid.T,
        model,
        state_fwd.astype(jnp.float32),
        state_adj.astype(jnp.float32),
    )


def body(
    velocity_tiles,
    forward_state,
    adjoint_state,
    wavelet,
    source_cell,
    receiver_cell,
    residual,
    aperture_row,
    aperture_col,
):
    groups = lax.axis_size("shot")
    own_cols = groups // AP_ROWS
    caps = (AP_COLS + own_cols) // own_cols
    assert own_cols == AP_COLS and caps == 2 and forward_state.shape[0] == 1
    n_sub = lax.axis_size("sub")
    assert n_sub == 2 * X_CHIPS and groups % GROUP_ROW == 0
    outbound = [
        (g * n_sub + b, g * n_sub + device_of(g, b)) for g in range(groups) for b in range(n_sub)
    ]
    myself = lax.axis_index("shot")
    shots_here = forward_state.shape[0]
    gradient = jnp.zeros(velocity_tiles.shape, jnp.float32)
    every_shot = list(range(shots_here))
    states = [
        jnp.concatenate(
            [forward_state[k].astype(jnp.float32), adjoint_state[k].astype(jnp.float32)]
        )
        for k in range(shots_here)
    ]
    velocity_tiles, states = lax.optimization_barrier((velocity_tiles, states))
    states_moved = [lax.ppermute(s, ("shot", "sub"), outbound) for s in states]
    sending = outgoing(
        velocity_tiles, aperture_row, aperture_col, every_shot, groups, own_cols, caps
    )
    fetched = lax.all_to_all(sending, "shot", split_axis=0, concat_axis=0, tiled=True)
    images = []
    for k in every_shot:
        shot_id = myself * SHOTS_DEV + k
        row_start = aperture_row[shot_id]
        col_start = aperture_col[shot_id]
        model = assemble(fetched, row_start, col_start, own_cols)
        model = lax.ppermute(model, ("shot", "sub"), outbound)
        states = states_moved[k]
        image = migrate(
            model,
            states[0:2],
            states[2:4],
            wavelet[k],
            source_cell[k],
            receiver_cell[k],
            residual[k],
        )
        image = lax.ppermute(image, ("shot", "sub"), [(b, a) for a, b in outbound])
        images.append(disperse(image, row_start, col_start, groups, own_cols, caps))
    returned = lax.all_to_all(images[0], "shot", split_axis=0, concat_axis=0, tiled=True)
    gradient = accumulate(
        gradient, returned, aperture_row, aperture_col, every_shot, groups, own_cols, caps
    )
    return gradient


def solution(mesh):
    placed = (
        P("shot", "sub", None),
        P("shot", None, "sub", None, None),
        P("shot", None, "sub", None, None),
        P("shot", None),
        P("shot"),
        P("shot", None),
        P("shot", None, None),
        P(),
        P(),
    )
    return jax.shard_map(
        body, mesh=mesh, in_specs=placed, out_specs=P("shot", "sub", None), check_vma=False
    )
```

```python
import jax
import jax.numpy as jnp
from jax import lax
from jax.sharding import PartitionSpec as P
from jax.experimental import pallas as pl
from jax.experimental.pallas import tpu as pltpu

TILE = 16
RY = 3
SHOTS_DEV = 1
NT = 4
RADIUS = 4
AP_ROWS = 4
AP_COLS = 8
TILE_DEV = 12
AX = 64
AY = 128


COEFFS = (-205.0 / 72.0, 8.0 / 5.0, -1.0 / 5.0, 8.0 / 315.0, -1.0 / 560.0)
IMAGE_SCALE = 1.0 / 64.0


def padded_2(array, sides, width):
    for axis, dim in sides:
        size, length = (lax.axis_size(axis), array.shape[dim])
        up = [(i, (i + 1) % size) for i in range(size - 1)]
        down = [(j, i) for i, j in up]
        last = lax.slice_in_dim(array, length - width, length, axis=dim)
        first = lax.slice_in_dim(array, 0, width, axis=dim)
        before = lax.ppermute(last, axis, up)
        after = lax.ppermute(first, axis, down)
        array = jnp.concatenate([before, array, after], axis=dim)
    return array


def laplace(padded, depth_cells, row_cells, column_cells):
    r = 4
    center = padded[r : r + depth_cells, r : r + row_cells, r : r + column_cells]
    summed = 3.0 * COEFFS[0] * center
    for k in range(1, 5):
        nearby = padded[r + k : r + k + depth_cells, r : r + row_cells, r : r + column_cells]
        nearby = (
            nearby + padded[r - k : r - k + depth_cells, r : r + row_cells, r : r + column_cells]
        )
        nearby = (
            nearby + padded[r : r + depth_cells, r + k : r + k + row_cells, r : r + column_cells]
        )
        nearby = (
            nearby + padded[r : r + depth_cells, r - k : r - k + row_cells, r : r + column_cells]
        )
        nearby = (
            nearby + padded[r : r + depth_cells, r : r + row_cells, r + k : r + k + column_cells]
        )
        nearby = (
            nearby + padded[r : r + depth_cells, r : r + row_cells, r - k : r - k + column_cells]
        )
        summed = summed + COEFFS[k] * nearby
    return summed


def wave_operator(field):
    padded = padded_2(field, (("sub", 0),), RADIUS)
    padded = jnp.pad(padded, ((0, 0), (4, 4), (4, 4)))
    return laplace(padded, field.shape[0], AX, AY)


def adjoint_operator(field):
    padded = padded_2(field, (("sub", 0),), RADIUS)
    padded = jnp.pad(padded, ((0, 0), (4, 4), (4, 4)))
    return laplace(padded, field.shape[0], AX, AY)


def slot_layout(row_start, col_start, owner_row, owner_col, own_cols, caps):
    block_row = (owner_row - row_start) % AP_ROWS
    first_col = (owner_col - col_start // TILE) % own_cols
    block_col = first_col + own_cols * jnp.arange(caps, dtype=jnp.int32)
    usable = block_col <= AP_COLS
    return (block_row, block_col, usable)


def owner_slots(row_table, col_table, shot_list, groups, own_cols, caps):
    myself = lax.axis_index("shot")
    owner_row = myself // own_cols
    owner_col = myself % own_cols
    senders = jnp.arange(groups, dtype=jnp.int32)[:, None]
    if SHOTS_DEV == 1 and list(shot_list) == [0]:
        row_start = row_table[:groups].reshape(groups, 1, 1)
        col_start = col_table[:groups].reshape(groups, 1, 1)
    else:
        picked = senders * SHOTS_DEV + jnp.asarray(shot_list, dtype=jnp.int32)[None, :]
        row_start = row_table[picked][..., None]
        col_start = col_table[picked][..., None]
    block_row, block_col, usable = slot_layout(
        row_start, col_start, owner_row, owner_col, own_cols, caps
    )
    tile_row = row_start + block_row
    tile_col = col_start // TILE + block_col
    local = tile_row // AP_ROWS * RY + tile_col // own_cols
    local = jnp.clip(local, 0, TILE_DEV - 1)
    return (local.reshape(-1), usable.reshape(-1))


def lane_column():
    return jnp.arange(TILE * TILE, dtype=jnp.int32) % TILE


def merge_slots(pair, spare_ok, offset):
    lower = spare_ok & (lane_column() < offset)
    return jnp.where(lower, pair[:, 1], pair[:, 0])


def outgoing(velocity_tiles, row_table, col_table, shot_list, groups, own_cols, caps):
    local, usable = owner_slots(row_table, col_table, shot_list, groups, own_cols, caps)
    chosen = velocity_tiles[local]
    chosen = jnp.where(usable[:, None, None], chosen, 0.0)
    chosen = chosen.reshape(groups, caps, velocity_tiles.shape[1], velocity_tiles.shape[2])
    usable = usable.reshape(groups, caps)
    offset = (col_table[:groups] % TILE).reshape(groups, 1, 1)
    merged = merge_slots(chosen, usable[:, 1, None, None], offset)
    return merged.reshape(groups, 1, velocity_tiles.shape[1], velocity_tiles.shape[2])


def accumulate(gradient, returned, row_table, col_table, shot_list, groups, own_cols, caps):
    local, usable = owner_slots(row_table, col_table, shot_list, groups, own_cols, caps)
    usable = usable.reshape(groups, caps)
    offset = (col_table[:groups] % TILE).reshape(groups, 1, 1)
    lower = lane_column() < offset
    piece = returned.reshape(groups, gradient.shape[1], gradient.shape[2])
    spare = usable[:, 1, None, None]
    first = jnp.where(spare & lower, 0.0, piece)
    second = jnp.where(spare & lower, piece, 0.0)
    pieces = jnp.stack([first, second], axis=1).reshape(groups * caps, -1)
    hot = (local[:, None] == jnp.arange(gradient.shape[0], dtype=jnp.int32)[None, :]) & usable.reshape(-1)[:, None]
    summed = jnp.einsum(
        "st,sf->tf", hot.astype(jnp.float32), pieces, precision=lax.Precision.HIGHEST
    )
    return gradient + summed.reshape(gradient.shape)


def assemble(received, row_start, col_start, own_cols):
    depth_cells = received.shape[2]
    rel_row = jnp.arange(AP_ROWS, dtype=jnp.int32)[:, None]
    rel_col = jnp.arange(AP_COLS + 1, dtype=jnp.int32)[None, :]
    source_owner = (row_start + rel_row) % AP_ROWS * own_cols + (
        col_start // TILE + rel_col
    ) % own_cols
    flat_index = source_owner.reshape(-1)
    pieces = received.reshape(-1, depth_cells, TILE * TILE)[flat_index]
    block = pieces.reshape(AP_ROWS, AP_COLS + 1, depth_cells, TILE, TILE)
    block = block.transpose(2, 0, 3, 1, 4).reshape(depth_cells, AX, (AP_COLS + 1) * TILE)
    return lax.dynamic_slice_in_dim(block, col_start % TILE, AY, 2)


def disperse(image, row_start, col_start, groups, own_cols, caps):
    depth_cells = image.shape[0]
    wide = jnp.zeros((depth_cells, AX, (AP_COLS + 1) * TILE), jnp.float32)
    wide = lax.dynamic_update_slice_in_dim(wide, image, col_start % TILE, 2)
    pieces = wide.reshape(depth_cells, AP_ROWS, TILE, AP_COLS + 1, TILE)
    pieces = pieces.transpose(1, 3, 0, 2, 4).reshape(
        AP_ROWS * (AP_COLS + 1), depth_cells, TILE * TILE
    )
    owners = jnp.arange(groups, dtype=jnp.int32)[:, None]
    block_row, block_col, usable = slot_layout(
        row_start, col_start, owners // own_cols, owners % own_cols, own_cols, caps
    )
    position = jnp.clip(block_row * (AP_COLS + 1) + block_col, 0, AP_ROWS * (AP_COLS + 1) - 1)
    chosen = jnp.where(usable[..., None, None], pieces[position], 0.0)
    merged = merge_slots(chosen, usable[:, 1, None, None], col_start % TILE)
    return merged.reshape(groups, 1, depth_cells, TILE * TILE)


X_CHIPS = 4
GROUP_ROW = 8


def crossing(group):
    return (group // GROUP_ROW * 2 + group % 2) % X_CHIPS


def mirror(group):
    return group % 2


def block_of(group, sub):
    cross = crossing(group)
    x, side = sub // 2, sub % 2
    flip = mirror(group)
    half = side + flip - 2 * side * flip
    low = (x - cross + 2 * X_CHIPS - 1) % X_CHIPS
    high = X_CHIPS + (cross - x + X_CHIPS) % X_CHIPS
    return (1 - half) * low + half * high


def device_of(group, block):
    cross = crossing(group)
    half = block // X_CHIPS
    low = (cross + 1 + block) % X_CHIPS
    high = (cross - block + 2 * X_CHIPS) % X_CHIPS
    flip = mirror(group)
    side = half + flip - 2 * half * flip
    return ((1 - half) * low + half * high) * 2 + side


def shift_rows(c, k, rows):
    if k > 0:
        moved = pltpu.roll(c, AX - k, 0)
        return jnp.where(rows < AX - k, moved, 0.0)
    moved = pltpu.roll(c, -k, 0)
    return jnp.where(rows >= -k, moved, 0.0)


def shift_lanes(c, k, lanes):
    if k > 0:
        moved = pltpu.roll(c, AY - k, 1)
        return jnp.where(lanes < AY - k, moved, 0.0)
    moved = pltpu.roll(c, -k, 1)
    return jnp.where(lanes >= -k, moved, 0.0)


def plane_stencil(buf, r, p, rows, lanes):
    c = buf[r, p]
    summed = (3.0 * COEFFS[0]) * c
    for k in range(1, 5):
        nearby = buf[r, p + k] + buf[r, p - k]
        nearby = nearby + shift_rows(c, k, rows)
        nearby = nearby + shift_rows(c, -k, rows)
        nearby = nearby + shift_lanes(c, k, lanes)
        nearby = nearby + shift_lanes(c, -k, lanes)
        summed = summed + COEFFS[k] * nearby
    return summed


def split_bf16(values):
    high = values.astype(jnp.bfloat16)
    rest = values - high.astype(jnp.float32)
    middle = rest.astype(jnp.bfloat16)
    low = (rest - middle.astype(jnp.float32)).astype(jnp.bfloat16)
    return (high, middle, low)


def migrate_kernel(
    src_ref, wave_ref, rrow_ref, rcol_ref, resid_ref, model_ref, pf_ref, qa_ref,
    img_ref, pad_p, pad_q, lap, qs, inject, img_loc, img_scr, send_sem, recv_sem, image_sem,
):
    group = lax.axis_index("shot")
    sub = lax.axis_index("sub")
    me = block_of(group, sub)
    n_sub = lax.axis_size("sub")
    depth = model_ref.shape[0]
    halo = jnp.zeros((RADIUS, AX, AY), jnp.float32)
    for r in range(NT):
        for buf in (pad_p, pad_q):
            buf[r, 0:RADIUS] = halo
            buf[r, RADIUS + depth : 2 * RADIUS + depth] = halo
    pad_p[0, RADIUS : RADIUS + depth] = pf_ref[0]
    pad_q[0, RADIUS : RADIUS + depth] = model_ref[...] * qa_ref[0]
    up_dev = device_of(group, (me + 1) % n_sub)
    down_dev = device_of(group, (me + n_sub - 1) % n_sub)
    target = device_of(group, sub)
    moved = target != sub
    mesh_id = pl.DeviceIdType.MESH
    barrier = pltpu.get_barrier_semaphore()
    pl.semaphore_signal(barrier, 1, device_id={"sub": up_dev}, device_id_type=mesh_id)
    pl.semaphore_signal(barrier, 1, device_id={"sub": down_dev}, device_id_type=mesh_id)

    @pl.when(moved)
    def _():
        pl.semaphore_signal(barrier, 1, device_id={"sub": target}, device_id_type=mesh_id)
        pl.semaphore_signal(barrier, 1, device_id={"sub": me}, device_id_type=mesh_id)
        pl.semaphore_wait(barrier, 4)

    @pl.when(jnp.logical_not(moved))
    def _():
        pl.semaphore_wait(barrier, 2)
    rows = lax.broadcasted_iota(jnp.int32, (AX, AY), 0)
    lanes = lax.broadcasted_iota(jnp.int32, (AX, AY), 1)
    n_rec = rcol_ref.shape[0]
    src_level = src_ref[0]
    src_spot = (rows == src_ref[1]) & (lanes == src_ref[2])

    def build_injection(step):
        hit_y = lax.broadcasted_iota(jnp.int32, (n_rec, AY), 1) == rcol_ref[...]
        spread = jnp.where(hit_y, resid_ref[:, step : step + 1], 0.0)
        parts = split_bf16(spread)
        rec_level = rrow_ref[0:1, :]
        hit_x = lax.broadcasted_iota(jnp.int32, (AX, n_rec), 0) == rrow_ref[1:2, :]

        def plane(j, carry):
            picks = (hit_x & (rec_level == j)).astype(jnp.bfloat16)
            total = jnp.dot(picks, parts[0], preferred_element_type=jnp.float32)
            total = total + jnp.dot(picks, parts[1], preferred_element_type=jnp.float32)
            total = total + jnp.dot(picks, parts[2], preferred_element_type=jnp.float32)
            inject[j] = total
            return carry

        lax.fori_loop(0, depth, plane, 0)

    def exchange(r, f):
        buf = (pad_p, pad_q)[f]
        down = pltpu.make_async_remote_copy(
            src_ref=buf.at[r, RADIUS : 2 * RADIUS],
            dst_ref=buf.at[r, RADIUS + depth : 2 * RADIUS + depth],
            send_sem=send_sem.at[r, f, 0],
            recv_sem=recv_sem.at[r, f, 0],
            device_id={"sub": down_dev},
            device_id_type=pl.DeviceIdType.MESH,
        )
        up = pltpu.make_async_remote_copy(
            src_ref=buf.at[r, depth : RADIUS + depth],
            dst_ref=buf.at[r, 0:RADIUS],
            send_sem=send_sem.at[r, f, 1],
            recv_sem=recv_sem.at[r, f, 1],
            device_id={"sub": up_dev},
            device_id_type=pl.DeviceIdType.MESH,
        )

        @pl.when(me > 0)
        def _():
            down.start()

        @pl.when(me < n_sub - 1)
        def _():
            up.start()

        return (down, up)

    def finish(pair):
        down, up = pair

        @pl.when(me > 0)
        def _():
            down.wait_send()
            up.wait_recv()

        @pl.when(me < n_sub - 1)
        def _():
            up.wait_send()
            down.wait_recv()

    def forward_round(r):
        def plane(j, carry):
            p = j + RADIUS
            lp = plane_stencil(pad_p, r, p, rows, lanes)
            lap[r, j] = lp
            if r < NT - 1:
                before = pf_ref[1, j] if r == 0 else pad_p[r - 1, p]
                following = 2.0 * pad_p[r, p] - before + model_ref[j] * lp
                source = jnp.where(src_spot & (src_level == j), wave_ref[r], 0.0)
                pad_p[r + 1, p] = following + source
            return carry

        lax.fori_loop(0, depth, plane, 0)

    def adjoint_round(r):
        def plane(j, carry):
            p = j + RADIUS
            lq = plane_stencil(pad_q, r, p, rows, lanes)
            now = qa_ref[0, j] if r == 0 else qs[r - 1, j]
            if r == 0:
                later = qa_ref[1, j]
            elif r == 1:
                later = qa_ref[0, j]
            else:
                later = qs[r - 2, j]
            result = 2.0 * now - later + lq
            result = result + inject[j]
            if r < NT - 1:
                qs[r, j] = result
                pad_q[r + 1, p] = model_ref[j] * result
            else:
                image = jnp.zeros((AX, AY), jnp.float32)
                for s in range(NT - 1):
                    image = image + qs[s, j] * lap[NT - 1 - s, j]
                image = image + result * lap[0, j]
                img_loc[j] = IMAGE_SCALE * image
            return carry

        lax.fori_loop(0, depth, plane, 0)

    fwd = exchange(0, 0)
    adj = exchange(0, 1)
    build_injection(NT - 1)
    for r in range(NT):
        finish(fwd)
        forward_round(r)
        if r < NT - 1:
            fwd = exchange(r + 1, 0)
        finish(adj)
        adjoint_round(r)
        if r < NT - 1:
            adj = exchange(r + 1, 1)
            build_injection(NT - 2 - r)
    image_copy = pltpu.make_async_remote_copy(
        src_ref=img_loc,
        dst_ref=img_scr,
        send_sem=image_sem.at[0],
        recv_sem=image_sem.at[1],
        device_id={"sub": me},
        device_id_type=mesh_id,
    )

    @pl.when(moved)
    def _():
        image_copy.start()
        image_copy.wait_send()
        image_copy.wait_recv()
        img_ref[...] = img_scr[...]

    @pl.when(jnp.logical_not(moved))
    def _():
        img_ref[...] = img_loc[...]


def migrate(model, state_fwd, state_adj, wave, source, receivers, resid):
    depth_cells = model.shape[0]
    plane = AX * AY
    offset = block_of(lax.axis_index("shot"), lax.axis_index("sub")) * depth_cells

    def level_of(cells):
        level = cells // plane - offset
        inside = (level >= 0) & (level < depth_cells)
        return jnp.where(inside, level, -1)

    src = jnp.stack([level_of(source), source % plane // AY, source % AY]).astype(jnp.int32)
    rrow = jnp.stack([level_of(receivers), receivers % plane // AY]).astype(jnp.int32)
    rcol = (receivers % AY).astype(jnp.int32).reshape(-1, 1)
    vmem = pl.BlockSpec(memory_space=pltpu.VMEM)
    smem = pl.BlockSpec(memory_space=pltpu.SMEM)
    padded = (NT, depth_cells + 2 * RADIUS, AX, AY)
    field = (NT, depth_cells, AX, AY)
    return pl.pallas_call(
        migrate_kernel,
        out_shape=jax.ShapeDtypeStruct(model.shape, jnp.float32),
        in_specs=[smem, smem] + [vmem] * 6,
        out_specs=vmem,
        scratch_shapes=[
            pltpu.VMEM(padded, jnp.float32),
            pltpu.VMEM(padded, jnp.float32),
            pltpu.VMEM(field, jnp.float32),
            pltpu.VMEM(field, jnp.float32),
            pltpu.VMEM(model.shape, jnp.float32),
            pltpu.VMEM(model.shape, jnp.float32),
            pltpu.VMEM(model.shape, jnp.float32),
            pltpu.SemaphoreType.DMA((NT, 2, 2)),
            pltpu.SemaphoreType.DMA((NT, 2, 2)),
            pltpu.SemaphoreType.DMA((2,)),
        ],
        compiler_params=pltpu.CompilerParams(collective_id=0, has_side_effects=True),
    )(
        src,
        wave.astype(jnp.float32),
        rrow,
        rcol,
        resid.T,
        model,
        state_fwd.astype(jnp.float32),
        state_adj.astype(jnp.float32),
    )


def body(
    velocity_tiles,
    forward_state,
    adjoint_state,
    wavelet,
    source_cell,
    receiver_cell,
    residual,
    aperture_row,
    aperture_col,
):
    groups = lax.axis_size("shot")
    own_cols = groups // AP_ROWS
    caps = (AP_COLS + own_cols) // own_cols
    assert own_cols == AP_COLS and caps == 2 and forward_state.shape[0] == 1
    n_sub = lax.axis_size("sub")
    assert n_sub == 2 * X_CHIPS and groups % GROUP_ROW == 0
    outbound = [
        (g * n_sub + b, g * n_sub + device_of(g, b)) for g in range(groups) for b in range(n_sub)
    ]
    myself = lax.axis_index("shot")
    shots_here = forward_state.shape[0]
    gradient = jnp.zeros(velocity_tiles.shape, jnp.float32)
    every_shot = list(range(shots_here))
    states_moved = []
    for k in range(shots_here):
        states = jnp.concatenate(
            [forward_state[k].astype(jnp.float32), adjoint_state[k].astype(jnp.float32)]
        )
        states_moved.append(lax.ppermute(states, ("shot", "sub"), outbound))
    sending = outgoing(
        velocity_tiles, aperture_row, aperture_col, every_shot, groups, own_cols, caps
    )
    fetched = lax.all_to_all(sending, "shot", split_axis=0, concat_axis=0, tiled=True)
    images = []
    for k in every_shot:
        shot_id = myself * SHOTS_DEV + k
        row_start = aperture_row[shot_id]
        col_start = aperture_col[shot_id]
        model = assemble(fetched, row_start, col_start, own_cols)
        model = lax.ppermute(model, ("shot", "sub"), outbound)
        states = states_moved[k]
        image = migrate(
            model,
            states[0:2],
            states[2:4],
            wavelet[k],
            source_cell[k],
            receiver_cell[k],
            residual[k],
        )
        images.append(disperse(image, row_start, col_start, groups, own_cols, caps))
    returned = lax.all_to_all(images[0], "shot", split_axis=0, concat_axis=0, tiled=True)
    gradient = accumulate(
        gradient, returned, aperture_row, aperture_col, every_shot, groups, own_cols, caps
    )
    return gradient


def solution(mesh):
    placed = (
        P("shot", "sub", None),
        P("shot", None, "sub", None, None),
        P("shot", None, "sub", None, None),
        P("shot", None),
        P("shot"),
        P("shot", None),
        P("shot", None, None),
        P(),
        P(),
    )
    return jax.shard_map(
        body, mesh=mesh, in_specs=placed, out_specs=P("shot", "sub", None), check_vma=False
    )
```

```python
import jax
import jax.numpy as jnp
from jax import lax
from jax.sharding import PartitionSpec as P
from jax.experimental import pallas as pl
from jax.experimental.pallas import tpu as pltpu

TILE = 16
RY = 3
SHOTS_DEV = 1
NT = 4
RADIUS = 4
AP_ROWS = 4
AP_COLS = 8
TILE_DEV = 12
AX = 64
AY = 128


COEFFS = (-205.0 / 72.0, 8.0 / 5.0, -1.0 / 5.0, 8.0 / 315.0, -1.0 / 560.0)
IMAGE_SCALE = 1.0 / 64.0


def padded_2(array, sides, width):
    for axis, dim in sides:
        size, length = (lax.axis_size(axis), array.shape[dim])
        up = [(i, (i + 1) % size) for i in range(size - 1)]
        down = [(j, i) for i, j in up]
        last = lax.slice_in_dim(array, length - width, length, axis=dim)
        first = lax.slice_in_dim(array, 0, width, axis=dim)
        before = lax.ppermute(last, axis, up)
        after = lax.ppermute(first, axis, down)
        array = jnp.concatenate([before, array, after], axis=dim)
    return array


def laplace(padded, depth_cells, row_cells, column_cells):
    r = 4
    center = padded[r : r + depth_cells, r : r + row_cells, r : r + column_cells]
    summed = 3.0 * COEFFS[0] * center
    for k in range(1, 5):
        nearby = padded[r + k : r + k + depth_cells, r : r + row_cells, r : r + column_cells]
        nearby = (
            nearby + padded[r - k : r - k + depth_cells, r : r + row_cells, r : r + column_cells]
        )
        nearby = (
            nearby + padded[r : r + depth_cells, r + k : r + k + row_cells, r : r + column_cells]
        )
        nearby = (
            nearby + padded[r : r + depth_cells, r - k : r - k + row_cells, r : r + column_cells]
        )
        nearby = (
            nearby + padded[r : r + depth_cells, r : r + row_cells, r + k : r + k + column_cells]
        )
        nearby = (
            nearby + padded[r : r + depth_cells, r : r + row_cells, r - k : r - k + column_cells]
        )
        summed = summed + COEFFS[k] * nearby
    return summed


def wave_operator(field):
    padded = padded_2(field, (("sub", 0),), RADIUS)
    padded = jnp.pad(padded, ((0, 0), (4, 4), (4, 4)))
    return laplace(padded, field.shape[0], AX, AY)


def adjoint_operator(field):
    padded = padded_2(field, (("sub", 0),), RADIUS)
    padded = jnp.pad(padded, ((0, 0), (4, 4), (4, 4)))
    return laplace(padded, field.shape[0], AX, AY)


def slot_layout(row_start, col_start, owner_row, owner_col, own_cols, caps):
    block_row = (owner_row - row_start) % AP_ROWS
    first_col = (owner_col - col_start // TILE) % own_cols
    block_col = first_col + own_cols * jnp.arange(caps, dtype=jnp.int32)
    usable = block_col <= AP_COLS
    return (block_row, block_col, usable)


def owner_slots(row_table, col_table, shot_list, groups, own_cols, caps):
    myself = lax.axis_index("shot")
    owner_row = myself // own_cols
    owner_col = myself % own_cols
    senders = jnp.arange(groups, dtype=jnp.int32)[:, None]
    if SHOTS_DEV == 1 and list(shot_list) == [0]:
        row_start = row_table[:groups].reshape(groups, 1, 1)
        col_start = col_table[:groups].reshape(groups, 1, 1)
    else:
        picked = senders * SHOTS_DEV + jnp.asarray(shot_list, dtype=jnp.int32)[None, :]
        row_start = row_table[picked][..., None]
        col_start = col_table[picked][..., None]
    block_row, block_col, usable = slot_layout(
        row_start, col_start, owner_row, owner_col, own_cols, caps
    )
    tile_row = row_start + block_row
    tile_col = col_start // TILE + block_col
    local = tile_row // AP_ROWS * RY + tile_col // own_cols
    local = jnp.clip(local, 0, TILE_DEV - 1)
    return (local.reshape(-1), usable.reshape(-1))


def lane_column():
    return jnp.arange(TILE * TILE, dtype=jnp.int32) % TILE


def merge_slots(pair, spare_ok, offset):
    lower = spare_ok & (lane_column() < offset)
    return jnp.where(lower, pair[:, 1], pair[:, 0])


def outgoing(velocity_tiles, row_table, col_table, shot_list, groups, own_cols, caps):
    local, usable = owner_slots(row_table, col_table, shot_list, groups, own_cols, caps)
    chosen = velocity_tiles[local]
    chosen = jnp.where(usable[:, None, None], chosen, 0.0)
    chosen = chosen.reshape(groups, caps, velocity_tiles.shape[1], velocity_tiles.shape[2])
    usable = usable.reshape(groups, caps)
    offset = (col_table[:groups] % TILE).reshape(groups, 1, 1)
    merged = merge_slots(chosen, usable[:, 1, None, None], offset)
    return merged.reshape(groups, 1, velocity_tiles.shape[1], velocity_tiles.shape[2])


def accumulate(gradient, returned, row_table, col_table, shot_list, groups, own_cols, caps):
    local, usable = owner_slots(row_table, col_table, shot_list, groups, own_cols, caps)
    usable = usable.reshape(groups, caps)
    offset = (col_table[:groups] % TILE).reshape(groups, 1, 1)
    lower = lane_column() < offset
    piece = returned.reshape(groups, gradient.shape[1], gradient.shape[2])
    spare = usable[:, 1, None, None]
    first = jnp.where(spare & lower, 0.0, piece)
    second = jnp.where(spare & lower, piece, 0.0)
    pieces = jnp.stack([first, second], axis=1).reshape(groups * caps, -1)
    hot = (local[:, None] == jnp.arange(gradient.shape[0], dtype=jnp.int32)[None, :]) & usable.reshape(-1)[:, None]
    summed = jnp.einsum(
        "st,sf->tf", hot.astype(jnp.float32), pieces, precision=lax.Precision.HIGHEST
    )
    return gradient + summed.reshape(gradient.shape)


def assemble(received, row_start, col_start, own_cols):
    depth_cells = received.shape[2]
    rel_row = jnp.arange(AP_ROWS, dtype=jnp.int32)[:, None]
    rel_col = jnp.arange(AP_COLS + 1, dtype=jnp.int32)[None, :]
    source_owner = (row_start + rel_row) % AP_ROWS * own_cols + (
        col_start // TILE + rel_col
    ) % own_cols
    flat_index = source_owner.reshape(-1)
    pieces = received.reshape(-1, depth_cells, TILE * TILE)[flat_index]
    block = pieces.reshape(AP_ROWS, AP_COLS + 1, depth_cells, TILE, TILE)
    block = block.transpose(2, 0, 3, 1, 4).reshape(depth_cells, AX, (AP_COLS + 1) * TILE)
    return lax.dynamic_slice_in_dim(block, col_start % TILE, AY, 2)


def disperse(image, row_start, col_start, groups, own_cols, caps):
    depth_cells = image.shape[0]
    wide = jnp.zeros((depth_cells, AX, (AP_COLS + 1) * TILE), jnp.float32)
    wide = lax.dynamic_update_slice_in_dim(wide, image, col_start % TILE, 2)
    pieces = wide.reshape(depth_cells, AP_ROWS, TILE, AP_COLS + 1, TILE)
    pieces = pieces.transpose(1, 3, 0, 2, 4).reshape(
        AP_ROWS * (AP_COLS + 1), depth_cells, TILE * TILE
    )
    owners = jnp.arange(groups, dtype=jnp.int32)[:, None]
    block_row, block_col, usable = slot_layout(
        row_start, col_start, owners // own_cols, owners % own_cols, own_cols, caps
    )
    position = jnp.clip(block_row * (AP_COLS + 1) + block_col, 0, AP_ROWS * (AP_COLS + 1) - 1)
    chosen = jnp.where(usable[..., None, None], pieces[position], 0.0)
    merged = merge_slots(chosen, usable[:, 1, None, None], col_start % TILE)
    return merged.reshape(groups, 1, depth_cells, TILE * TILE)


X_CHIPS = 4
GROUP_ROW = 8


def crossing(group):
    return (group // GROUP_ROW * 2 + group % 2) % X_CHIPS


def mirror(group):
    return group % 2


def block_of(group, sub):
    cross = crossing(group)
    x, side = sub // 2, sub % 2
    flip = mirror(group)
    half = side + flip - 2 * side * flip
    low = (x - cross + 2 * X_CHIPS - 1) % X_CHIPS
    high = X_CHIPS + (cross - x + X_CHIPS) % X_CHIPS
    return (1 - half) * low + half * high


def device_of(group, block):
    cross = crossing(group)
    half = block // X_CHIPS
    low = (cross + 1 + block) % X_CHIPS
    high = (cross - block + 2 * X_CHIPS) % X_CHIPS
    flip = mirror(group)
    side = half + flip - 2 * half * flip
    return ((1 - half) * low + half * high) * 2 + side


def shift_rows(c, k, rows):
    if k > 0:
        moved = pltpu.roll(c, AX - k, 0)
        return jnp.where(rows < AX - k, moved, 0.0)
    moved = pltpu.roll(c, -k, 0)
    return jnp.where(rows >= -k, moved, 0.0)


def shift_lanes(c, k, lanes):
    if k > 0:
        moved = pltpu.roll(c, AY - k, 1)
        return jnp.where(lanes < AY - k, moved, 0.0)
    moved = pltpu.roll(c, -k, 1)
    return jnp.where(lanes >= -k, moved, 0.0)


def plane_stencil(buf, r, p, rows, lanes):
    c = buf[r, p]
    summed = (3.0 * COEFFS[0]) * c
    for k in range(1, 5):
        nearby = buf[r, p + k] + buf[r, p - k]
        nearby = nearby + shift_rows(c, k, rows)
        nearby = nearby + shift_rows(c, -k, rows)
        nearby = nearby + shift_lanes(c, k, lanes)
        nearby = nearby + shift_lanes(c, -k, lanes)
        summed = summed + COEFFS[k] * nearby
    return summed


def split_bf16(values):
    high = values.astype(jnp.bfloat16)
    rest = values - high.astype(jnp.float32)
    middle = rest.astype(jnp.bfloat16)
    low = (rest - middle.astype(jnp.float32)).astype(jnp.bfloat16)
    return (high, middle, low)


def migrate_kernel(
    src_ref, wave_ref, rrow_ref, rcol_ref, resid_ref, model_ref, pf_ref, qa_ref,
    img_ref, pad_p, pad_q, lap, qs, inject, img_loc, img_scr, send_sem, recv_sem, image_sem,
):
    group = lax.axis_index("shot")
    sub = lax.axis_index("sub")
    me = block_of(group, sub)
    n_sub = lax.axis_size("sub")
    depth = model_ref.shape[0]
    halo = jnp.zeros((RADIUS, AX, AY), jnp.float32)
    for r in range(NT):
        for buf in (pad_p, pad_q):
            buf[r, 0:RADIUS] = halo
            buf[r, RADIUS + depth : 2 * RADIUS + depth] = halo
    pad_p[0, RADIUS : RADIUS + depth] = pf_ref[0]
    pad_q[0, RADIUS : RADIUS + depth] = model_ref[...] * qa_ref[0]
    up_dev = device_of(group, (me + 1) % n_sub)
    down_dev = device_of(group, (me + n_sub - 1) % n_sub)
    target = device_of(group, sub)
    moved = target != sub
    mesh_id = pl.DeviceIdType.MESH
    barrier = pltpu.get_barrier_semaphore()
    pl.semaphore_signal(barrier, 1, device_id={"sub": up_dev}, device_id_type=mesh_id)
    pl.semaphore_signal(barrier, 1, device_id={"sub": down_dev}, device_id_type=mesh_id)

    @pl.when(moved)
    def _():
        pl.semaphore_signal(barrier, 1, device_id={"sub": target}, device_id_type=mesh_id)
        pl.semaphore_signal(barrier, 1, device_id={"sub": me}, device_id_type=mesh_id)
        pl.semaphore_wait(barrier, 4)

    @pl.when(jnp.logical_not(moved))
    def _():
        pl.semaphore_wait(barrier, 2)
    rows = lax.broadcasted_iota(jnp.int32, (AX, AY), 0)
    lanes = lax.broadcasted_iota(jnp.int32, (AX, AY), 1)
    n_rec = rcol_ref.shape[0]
    src_level = src_ref[0]
    src_spot = (rows == src_ref[1]) & (lanes == src_ref[2])

    def build_injection(step):
        hit_y = lax.broadcasted_iota(jnp.int32, (n_rec, AY), 1) == rcol_ref[...]
        spread = jnp.where(hit_y, resid_ref[:, step : step + 1], 0.0)
        parts = split_bf16(spread)
        rec_level = rrow_ref[0:1, :]
        hit_x = lax.broadcasted_iota(jnp.int32, (AX, n_rec), 0) == rrow_ref[1:2, :]

        def plane(j, carry):
            picks = (hit_x & (rec_level == j)).astype(jnp.bfloat16)
            total = jnp.dot(picks, parts[0], preferred_element_type=jnp.float32)
            total = total + jnp.dot(picks, parts[1], preferred_element_type=jnp.float32)
            total = total + jnp.dot(picks, parts[2], preferred_element_type=jnp.float32)
            inject[j] = total
            return carry

        lax.fori_loop(0, depth, plane, 0)

    def exchange(r, f):
        buf = (pad_p, pad_q)[f]
        down = pltpu.make_async_remote_copy(
            src_ref=buf.at[r, RADIUS : 2 * RADIUS],
            dst_ref=buf.at[r, RADIUS + depth : 2 * RADIUS + depth],
            send_sem=send_sem.at[r, f, 0],
            recv_sem=recv_sem.at[r, f, 0],
            device_id={"sub": down_dev},
            device_id_type=pl.DeviceIdType.MESH,
        )
        up = pltpu.make_async_remote_copy(
            src_ref=buf.at[r, depth : RADIUS + depth],
            dst_ref=buf.at[r, 0:RADIUS],
            send_sem=send_sem.at[r, f, 1],
            recv_sem=recv_sem.at[r, f, 1],
            device_id={"sub": up_dev},
            device_id_type=pl.DeviceIdType.MESH,
        )

        @pl.when(me > 0)
        def _():
            down.start()

        @pl.when(me < n_sub - 1)
        def _():
            up.start()

        return (down, up)

    def finish(pair):
        down, up = pair

        @pl.when(me > 0)
        def _():
            down.wait_send()
            up.wait_recv()

        @pl.when(me < n_sub - 1)
        def _():
            up.wait_send()
            down.wait_recv()

    def forward_round(r):
        def plane(j, carry):
            p = j + RADIUS
            lp = plane_stencil(pad_p, r, p, rows, lanes)
            lap[r, j] = lp
            if r < NT - 1:
                before = pf_ref[1, j] if r == 0 else pad_p[r - 1, p]
                following = 2.0 * pad_p[r, p] - before + model_ref[j] * lp
                source = jnp.where(src_spot & (src_level == j), wave_ref[r], 0.0)
                pad_p[r + 1, p] = following + source
            return carry

        lax.fori_loop(0, depth, plane, 0)

    def adjoint_round(r):
        def plane(j, carry):
            p = j + RADIUS
            lq = plane_stencil(pad_q, r, p, rows, lanes)
            now = qa_ref[0, j] if r == 0 else qs[r - 1, j]
            if r == 0:
                later = qa_ref[1, j]
            elif r == 1:
                later = qa_ref[0, j]
            else:
                later = qs[r - 2, j]
            result = 2.0 * now - later + lq
            result = result + inject[j]
            if r < NT - 1:
                qs[r, j] = result
                pad_q[r + 1, p] = model_ref[j] * result
            else:
                image = jnp.zeros((AX, AY), jnp.float32)
                for s in range(NT - 1):
                    image = image + qs[s, j] * lap[NT - 1 - s, j]
                image = image + result * lap[0, j]
                img_loc[j] = IMAGE_SCALE * image
            return carry

        lax.fori_loop(0, depth, plane, 0)

    fwd = exchange(0, 0)
    adj = exchange(0, 1)
    build_injection(NT - 1)
    for r in range(NT):
        finish(fwd)
        forward_round(r)
        if r < NT - 1:
            fwd = exchange(r + 1, 0)
        finish(adj)
        adjoint_round(r)
        if r < NT - 1:
            adj = exchange(r + 1, 1)
            build_injection(NT - 2 - r)
    image_copy = pltpu.make_async_remote_copy(
        src_ref=img_loc,
        dst_ref=img_scr,
        send_sem=image_sem.at[0],
        recv_sem=image_sem.at[1],
        device_id={"sub": me},
        device_id_type=mesh_id,
    )

    @pl.when(moved)
    def _():
        image_copy.start()
        image_copy.wait_send()
        image_copy.wait_recv()
        img_ref[...] = img_scr[...]

    @pl.when(jnp.logical_not(moved))
    def _():
        img_ref[...] = img_loc[...]


def migrate(model, state_fwd, state_adj, wave, source, receivers, resid):
    depth_cells = model.shape[0]
    plane = AX * AY
    offset = block_of(lax.axis_index("shot"), lax.axis_index("sub")) * depth_cells

    def level_of(cells):
        level = cells // plane - offset
        inside = (level >= 0) & (level < depth_cells)
        return jnp.where(inside, level, -1)

    src = jnp.stack([level_of(source), source % plane // AY, source % AY]).astype(jnp.int32)
    rrow = jnp.stack([level_of(receivers), receivers % plane // AY]).astype(jnp.int32)
    rcol = (receivers % AY).astype(jnp.int32).reshape(-1, 1)
    vmem = pl.BlockSpec(memory_space=pltpu.VMEM)
    smem = pl.BlockSpec(memory_space=pltpu.SMEM)
    padded = (NT, depth_cells + 2 * RADIUS, AX, AY)
    field = (NT, depth_cells, AX, AY)
    return pl.pallas_call(
        migrate_kernel,
        out_shape=jax.ShapeDtypeStruct(model.shape, jnp.float32),
        in_specs=[smem, smem] + [vmem] * 6,
        out_specs=vmem,
        scratch_shapes=[
            pltpu.VMEM(padded, jnp.float32),
            pltpu.VMEM(padded, jnp.float32),
            pltpu.VMEM(field, jnp.float32),
            pltpu.VMEM(field, jnp.float32),
            pltpu.VMEM(model.shape, jnp.float32),
            pltpu.VMEM(model.shape, jnp.float32),
            pltpu.VMEM(model.shape, jnp.float32),
            pltpu.SemaphoreType.DMA((NT, 2, 2)),
            pltpu.SemaphoreType.DMA((NT, 2, 2)),
            pltpu.SemaphoreType.DMA((2,)),
        ],
        compiler_params=pltpu.CompilerParams(collective_id=0, has_side_effects=True),
    )(
        src,
        wave.astype(jnp.float32),
        rrow,
        rcol,
        resid.T,
        model,
        state_fwd.astype(jnp.float32),
        state_adj.astype(jnp.float32),
    )


def body(
    velocity_tiles,
    forward_state,
    adjoint_state,
    wavelet,
    source_cell,
    receiver_cell,
    residual,
    aperture_row,
    aperture_col,
):
    groups = lax.axis_size("shot")
    own_cols = groups // AP_ROWS
    caps = (AP_COLS + own_cols) // own_cols
    assert own_cols == AP_COLS and caps == 2 and forward_state.shape[0] == 1
    n_sub = lax.axis_size("sub")
    assert n_sub == 2 * X_CHIPS and groups % GROUP_ROW == 0
    outbound = [
        (g * n_sub + b, g * n_sub + device_of(g, b)) for g in range(groups) for b in range(n_sub)
    ]
    myself = lax.axis_index("shot")
    shots_here = forward_state.shape[0]
    gradient = jnp.zeros(velocity_tiles.shape, jnp.float32)
    every_shot = list(range(shots_here))
    states_moved = []
    for k in range(shots_here):
        states = jnp.concatenate(
            [forward_state[k].astype(jnp.float32), adjoint_state[k].astype(jnp.float32)]
        )
        states_moved.append(lax.ppermute(states, ("shot", "sub"), outbound))
    sending = outgoing(
        velocity_tiles, aperture_row, aperture_col, every_shot, groups, own_cols, caps
    )
    fetched = lax.all_to_all(sending, "shot", split_axis=0, concat_axis=0, tiled=True)
    fetched = lax.ppermute(fetched, ("shot", "sub"), outbound)
    images = []
    for k in every_shot:
        shot_id = myself * SHOTS_DEV + k
        row_start = aperture_row[shot_id]
        col_start = aperture_col[shot_id]
        model = assemble(fetched, row_start, col_start, own_cols)
        states = states_moved[k]
        image = migrate(
            model,
            states[0:2],
            states[2:4],
            wavelet[k],
            source_cell[k],
            receiver_cell[k],
            residual[k],
        )
        images.append(disperse(image, row_start, col_start, groups, own_cols, caps))
    returned = lax.all_to_all(images[0], "shot", split_axis=0, concat_axis=0, tiled=True)
    gradient = accumulate(
        gradient, returned, aperture_row, aperture_col, every_shot, groups, own_cols, caps
    )
    return gradient


def solution(mesh):
    placed = (
        P("shot", "sub", None),
        P("shot", None, "sub", None, None),
        P("shot", None, "sub", None, None),
        P("shot", None),
        P("shot"),
        P("shot", None),
        P("shot", None, None),
        P(),
        P(),
    )
    return jax.shard_map(
        body, mesh=mesh, in_specs=placed, out_specs=P("shot", "sub", None), check_vma=False
    )
```

```python
import jax
import jax.numpy as jnp
from jax import lax
from jax.sharding import PartitionSpec as P
from jax.experimental import pallas as pl
from jax.experimental.pallas import tpu as pltpu

TILE = 16
RY = 3
SHOTS_DEV = 1
NT = 4
RADIUS = 4
AP_ROWS = 4
AP_COLS = 8
TILE_DEV = 12
AX = 64
AY = 128


COEFFS = (-205.0 / 72.0, 8.0 / 5.0, -1.0 / 5.0, 8.0 / 315.0, -1.0 / 560.0)
IMAGE_SCALE = 1.0 / 64.0


def padded_2(array, sides, width):
    for axis, dim in sides:
        size, length = (lax.axis_size(axis), array.shape[dim])
        up = [(i, (i + 1) % size) for i in range(size - 1)]
        down = [(j, i) for i, j in up]
        last = lax.slice_in_dim(array, length - width, length, axis=dim)
        first = lax.slice_in_dim(array, 0, width, axis=dim)
        before = lax.ppermute(last, axis, up)
        after = lax.ppermute(first, axis, down)
        array = jnp.concatenate([before, array, after], axis=dim)
    return array


def laplace(padded, depth_cells, row_cells, column_cells):
    r = 4
    center = padded[r : r + depth_cells, r : r + row_cells, r : r + column_cells]
    summed = 3.0 * COEFFS[0] * center
    for k in range(1, 5):
        nearby = padded[r + k : r + k + depth_cells, r : r + row_cells, r : r + column_cells]
        nearby = (
            nearby + padded[r - k : r - k + depth_cells, r : r + row_cells, r : r + column_cells]
        )
        nearby = (
            nearby + padded[r : r + depth_cells, r + k : r + k + row_cells, r : r + column_cells]
        )
        nearby = (
            nearby + padded[r : r + depth_cells, r - k : r - k + row_cells, r : r + column_cells]
        )
        nearby = (
            nearby + padded[r : r + depth_cells, r : r + row_cells, r + k : r + k + column_cells]
        )
        nearby = (
            nearby + padded[r : r + depth_cells, r : r + row_cells, r - k : r - k + column_cells]
        )
        summed = summed + COEFFS[k] * nearby
    return summed


def wave_operator(field):
    padded = padded_2(field, (("sub", 0),), RADIUS)
    padded = jnp.pad(padded, ((0, 0), (4, 4), (4, 4)))
    return laplace(padded, field.shape[0], AX, AY)


def adjoint_operator(field):
    padded = padded_2(field, (("sub", 0),), RADIUS)
    padded = jnp.pad(padded, ((0, 0), (4, 4), (4, 4)))
    return laplace(padded, field.shape[0], AX, AY)


def slot_layout(row_start, col_start, owner_row, owner_col, own_cols, caps):
    block_row = (owner_row - row_start) % AP_ROWS
    first_col = (owner_col - col_start // TILE) % own_cols
    block_col = first_col + own_cols * jnp.arange(caps, dtype=jnp.int32)
    usable = block_col <= AP_COLS
    return (block_row, block_col, usable)


def owner_slots(row_table, col_table, shot_list, groups, own_cols, caps):
    myself = lax.axis_index("shot")
    owner_row = myself // own_cols
    owner_col = myself % own_cols
    senders = jnp.arange(groups, dtype=jnp.int32)[:, None]
    if SHOTS_DEV == 1 and list(shot_list) == [0]:
        row_start = row_table[:groups].reshape(groups, 1, 1)
        col_start = col_table[:groups].reshape(groups, 1, 1)
    else:
        picked = senders * SHOTS_DEV + jnp.asarray(shot_list, dtype=jnp.int32)[None, :]
        row_start = row_table[picked][..., None]
        col_start = col_table[picked][..., None]
    block_row, block_col, usable = slot_layout(
        row_start, col_start, owner_row, owner_col, own_cols, caps
    )
    tile_row = row_start + block_row
    tile_col = col_start // TILE + block_col
    local = tile_row // AP_ROWS * RY + tile_col // own_cols
    local = jnp.clip(local, 0, TILE_DEV - 1)
    return (local.reshape(-1), usable.reshape(-1))


def lane_column():
    return jnp.arange(TILE * TILE, dtype=jnp.int32) % TILE


def merge_slots(pair, spare_ok, offset):
    lower = spare_ok & (lane_column() < offset)
    return jnp.where(lower, pair[:, 1], pair[:, 0])


def outgoing(velocity_tiles, row_table, col_table, shot_list, groups, own_cols, caps):
    local, usable = owner_slots(row_table, col_table, shot_list, groups, own_cols, caps)
    chosen = velocity_tiles[local]
    chosen = jnp.where(usable[:, None, None], chosen, 0.0)
    chosen = chosen.reshape(groups, caps, velocity_tiles.shape[1], velocity_tiles.shape[2])
    usable = usable.reshape(groups, caps)
    offset = (col_table[:groups] % TILE).reshape(groups, 1, 1)
    merged = merge_slots(chosen, usable[:, 1, None, None], offset)
    return merged.reshape(groups, 1, velocity_tiles.shape[1], velocity_tiles.shape[2])


def accumulate(gradient, returned, row_table, col_table, shot_list, groups, own_cols, caps):
    local, usable = owner_slots(row_table, col_table, shot_list, groups, own_cols, caps)
    usable = usable.reshape(groups, caps)
    offset = (col_table[:groups] % TILE).reshape(groups, 1, 1)
    lower = lane_column() < offset
    piece = returned.reshape(groups, gradient.shape[1], gradient.shape[2])
    spare = usable[:, 1, None, None]
    first = jnp.where(spare & lower, 0.0, piece)
    second = jnp.where(spare & lower, piece, 0.0)
    pieces = jnp.stack([first, second], axis=1).reshape(groups * caps, -1)
    hot = (local[:, None] == jnp.arange(gradient.shape[0], dtype=jnp.int32)[None, :]) & usable.reshape(-1)[:, None]
    summed = jnp.einsum(
        "st,sf->tf", hot.astype(jnp.float32), pieces, precision=lax.Precision.HIGHEST
    )
    return gradient + summed.reshape(gradient.shape)


def owner_tiles(row_start, col_start, own_cols):
    owner = jnp.arange(AP_ROWS * own_cols, dtype=jnp.int32)
    rel_row = (owner // own_cols - row_start) % AP_ROWS
    rel_col = (owner % own_cols - col_start // TILE) % own_cols
    return rel_row * own_cols + rel_col


def assemble(received, row_start, col_start, own_cols):
    depth_cells = received.shape[2]
    owner = (
        (row_start + jnp.arange(AP_ROWS, dtype=jnp.int32)[:, None]) % AP_ROWS * own_cols
        + (col_start // TILE + jnp.arange(own_cols, dtype=jnp.int32)[None, :]) % own_cols
    )
    pieces = received.reshape(-1, depth_cells, TILE * TILE)[owner.reshape(-1)]
    block = pieces.reshape(AP_ROWS, own_cols, depth_cells, TILE, TILE)
    block = block.transpose(2, 0, 3, 1, 4).reshape(depth_cells, AX, AY)
    return jnp.roll(block, -(col_start % TILE), axis=2)


def disperse(image, row_start, col_start, groups, own_cols, caps):
    depth_cells = image.shape[0]
    rolled = jnp.roll(image, col_start % TILE, axis=2)
    pieces = rolled.reshape(depth_cells, AP_ROWS, TILE, own_cols, TILE)
    pieces = pieces.transpose(1, 3, 0, 2, 4).reshape(AP_ROWS * own_cols, depth_cells, TILE * TILE)
    chosen = pieces[owner_tiles(row_start, col_start, own_cols)]
    return chosen.reshape(groups, 1, depth_cells, TILE * TILE)


X_CHIPS = 4
GROUP_ROW = 8


def crossing(group):
    return (group // GROUP_ROW * 2 + group % 2) % X_CHIPS


def mirror(group):
    return group % 2


def block_of(group, sub):
    cross = crossing(group)
    x, side = sub // 2, sub % 2
    flip = mirror(group)
    half = side + flip - 2 * side * flip
    low = (x - cross + 2 * X_CHIPS - 1) % X_CHIPS
    high = X_CHIPS + (cross - x + X_CHIPS) % X_CHIPS
    return (1 - half) * low + half * high


def device_of(group, block):
    cross = crossing(group)
    half = block // X_CHIPS
    low = (cross + 1 + block) % X_CHIPS
    high = (cross - block + 2 * X_CHIPS) % X_CHIPS
    flip = mirror(group)
    side = half + flip - 2 * half * flip
    return ((1 - half) * low + half * high) * 2 + side


def shift_rows(c, k, rows):
    if k > 0:
        moved = pltpu.roll(c, AX - k, 0)
        return jnp.where(rows < AX - k, moved, 0.0)
    moved = pltpu.roll(c, -k, 0)
    return jnp.where(rows >= -k, moved, 0.0)


def shift_lanes(c, k, lanes):
    if k > 0:
        moved = pltpu.roll(c, AY - k, 1)
        return jnp.where(lanes < AY - k, moved, 0.0)
    moved = pltpu.roll(c, -k, 1)
    return jnp.where(lanes >= -k, moved, 0.0)


def plane_stencil(buf, r, p, rows, lanes):
    c = buf[r, p]
    summed = (3.0 * COEFFS[0]) * c
    for k in range(1, 5):
        nearby = buf[r, p + k] + buf[r, p - k]
        nearby = nearby + shift_rows(c, k, rows)
        nearby = nearby + shift_rows(c, -k, rows)
        nearby = nearby + shift_lanes(c, k, lanes)
        nearby = nearby + shift_lanes(c, -k, lanes)
        summed = summed + COEFFS[k] * nearby
    return summed


def split_bf16(values):
    high = values.astype(jnp.bfloat16)
    rest = values - high.astype(jnp.float32)
    middle = rest.astype(jnp.bfloat16)
    low = (rest - middle.astype(jnp.float32)).astype(jnp.bfloat16)
    return (high, middle, low)


def migrate_kernel(
    src_ref, wave_ref, rrow_ref, rcol_ref, resid_ref, model_ref, pf_ref, qa_ref,
    img_ref, pad_p, pad_q, lap, qs, inject, img_loc, img_scr, send_sem, recv_sem, image_sem,
):
    group = lax.axis_index("shot")
    sub = lax.axis_index("sub")
    me = block_of(group, sub)
    n_sub = lax.axis_size("sub")
    depth = model_ref.shape[0]
    halo = jnp.zeros((RADIUS, AX, AY), jnp.float32)
    for r in range(NT):
        for buf in (pad_p, pad_q):
            buf[r, 0:RADIUS] = halo
            buf[r, RADIUS + depth : 2 * RADIUS + depth] = halo
    pad_p[0, RADIUS : RADIUS + depth] = pf_ref[0]
    pad_q[0, RADIUS : RADIUS + depth] = model_ref[...] * qa_ref[0]
    up_dev = device_of(group, (me + 1) % n_sub)
    down_dev = device_of(group, (me + n_sub - 1) % n_sub)
    target = device_of(group, sub)
    moved = target != sub
    mesh_id = pl.DeviceIdType.MESH
    barrier = pltpu.get_barrier_semaphore()
    pl.semaphore_signal(barrier, 1, device_id={"sub": up_dev}, device_id_type=mesh_id)
    pl.semaphore_signal(barrier, 1, device_id={"sub": down_dev}, device_id_type=mesh_id)

    @pl.when(moved)
    def _():
        pl.semaphore_signal(barrier, 1, device_id={"sub": target}, device_id_type=mesh_id)
        pl.semaphore_signal(barrier, 1, device_id={"sub": me}, device_id_type=mesh_id)
        pl.semaphore_wait(barrier, 4)

    @pl.when(jnp.logical_not(moved))
    def _():
        pl.semaphore_wait(barrier, 2)
    rows = lax.broadcasted_iota(jnp.int32, (AX, AY), 0)
    lanes = lax.broadcasted_iota(jnp.int32, (AX, AY), 1)
    n_rec = rcol_ref.shape[0]
    src_level = src_ref[0]
    src_spot = (rows == src_ref[1]) & (lanes == src_ref[2])

    def build_injection(step):
        hit_y = lax.broadcasted_iota(jnp.int32, (n_rec, AY), 1) == rcol_ref[...]
        spread = jnp.where(hit_y, resid_ref[:, step : step + 1], 0.0)
        parts = split_bf16(spread)
        rec_level = rrow_ref[0:1, :]
        hit_x = lax.broadcasted_iota(jnp.int32, (AX, n_rec), 0) == rrow_ref[1:2, :]

        def plane(j, carry):
            picks = (hit_x & (rec_level == j)).astype(jnp.bfloat16)
            total = jnp.dot(picks, parts[0], preferred_element_type=jnp.float32)
            total = total + jnp.dot(picks, parts[1], preferred_element_type=jnp.float32)
            total = total + jnp.dot(picks, parts[2], preferred_element_type=jnp.float32)
            inject[j] = total
            return carry

        lax.fori_loop(0, depth, plane, 0)

    def exchange(r, f):
        buf = (pad_p, pad_q)[f]
        down = pltpu.make_async_remote_copy(
            src_ref=buf.at[r, RADIUS : 2 * RADIUS],
            dst_ref=buf.at[r, RADIUS + depth : 2 * RADIUS + depth],
            send_sem=send_sem.at[r, f, 0],
            recv_sem=recv_sem.at[r, f, 0],
            device_id={"sub": down_dev},
            device_id_type=pl.DeviceIdType.MESH,
        )
        up = pltpu.make_async_remote_copy(
            src_ref=buf.at[r, depth : RADIUS + depth],
            dst_ref=buf.at[r, 0:RADIUS],
            send_sem=send_sem.at[r, f, 1],
            recv_sem=recv_sem.at[r, f, 1],
            device_id={"sub": up_dev},
            device_id_type=pl.DeviceIdType.MESH,
        )

        @pl.when(me > 0)
        def _():
            down.start()

        @pl.when(me < n_sub - 1)
        def _():
            up.start()

        return (down, up)

    def finish(pair):
        down, up = pair

        @pl.when(me > 0)
        def _():
            down.wait_send()
            up.wait_recv()

        @pl.when(me < n_sub - 1)
        def _():
            up.wait_send()
            down.wait_recv()

    def forward_round(r):
        def plane(j, carry):
            p = j + RADIUS
            lp = plane_stencil(pad_p, r, p, rows, lanes)
            lap[r, j] = lp
            if r < NT - 1:
                before = pf_ref[1, j] if r == 0 else pad_p[r - 1, p]
                following = 2.0 * pad_p[r, p] - before + model_ref[j] * lp
                source = jnp.where(src_spot & (src_level == j), wave_ref[r], 0.0)
                pad_p[r + 1, p] = following + source
            return carry

        lax.fori_loop(0, depth, plane, 0)

    def adjoint_round(r):
        def plane(j, carry):
            p = j + RADIUS
            lq = plane_stencil(pad_q, r, p, rows, lanes)
            now = qa_ref[0, j] if r == 0 else qs[r - 1, j]
            if r == 0:
                later = qa_ref[1, j]
            elif r == 1:
                later = qa_ref[0, j]
            else:
                later = qs[r - 2, j]
            result = 2.0 * now - later + lq
            result = result + inject[j]
            if r < NT - 1:
                qs[r, j] = result
                pad_q[r + 1, p] = model_ref[j] * result
            else:
                image = jnp.zeros((AX, AY), jnp.float32)
                for s in range(NT - 1):
                    image = image + qs[s, j] * lap[NT - 1 - s, j]
                image = image + result * lap[0, j]
                img_loc[j] = IMAGE_SCALE * image
            return carry

        lax.fori_loop(0, depth, plane, 0)

    fwd = exchange(0, 0)
    adj = exchange(0, 1)
    build_injection(NT - 1)
    for r in range(NT):
        finish(fwd)
        forward_round(r)
        if r < NT - 1:
            fwd = exchange(r + 1, 0)
        finish(adj)
        adjoint_round(r)
        if r < NT - 1:
            adj = exchange(r + 1, 1)
            build_injection(NT - 2 - r)
    image_copy = pltpu.make_async_remote_copy(
        src_ref=img_loc,
        dst_ref=img_scr,
        send_sem=image_sem.at[0],
        recv_sem=image_sem.at[1],
        device_id={"sub": me},
        device_id_type=mesh_id,
    )

    @pl.when(moved)
    def _():
        image_copy.start()
        image_copy.wait_send()
        image_copy.wait_recv()
        img_ref[...] = img_scr[...]

    @pl.when(jnp.logical_not(moved))
    def _():
        img_ref[...] = img_loc[...]


def migrate(model, state_fwd, state_adj, wave, source, receivers, resid):
    depth_cells = model.shape[0]
    plane = AX * AY
    offset = block_of(lax.axis_index("shot"), lax.axis_index("sub")) * depth_cells

    def level_of(cells):
        level = cells // plane - offset
        inside = (level >= 0) & (level < depth_cells)
        return jnp.where(inside, level, -1)

    src = jnp.stack([level_of(source), source % plane // AY, source % AY]).astype(jnp.int32)
    rrow = jnp.stack([level_of(receivers), receivers % plane // AY]).astype(jnp.int32)
    rcol = (receivers % AY).astype(jnp.int32).reshape(-1, 1)
    vmem = pl.BlockSpec(memory_space=pltpu.VMEM)
    smem = pl.BlockSpec(memory_space=pltpu.SMEM)
    padded = (NT, depth_cells + 2 * RADIUS, AX, AY)
    field = (NT, depth_cells, AX, AY)
    return pl.pallas_call(
        migrate_kernel,
        out_shape=jax.ShapeDtypeStruct(model.shape, jnp.float32),
        in_specs=[smem, smem] + [vmem] * 6,
        out_specs=vmem,
        scratch_shapes=[
            pltpu.VMEM(padded, jnp.float32),
            pltpu.VMEM(padded, jnp.float32),
            pltpu.VMEM(field, jnp.float32),
            pltpu.VMEM(field, jnp.float32),
            pltpu.VMEM(model.shape, jnp.float32),
            pltpu.VMEM(model.shape, jnp.float32),
            pltpu.VMEM(model.shape, jnp.float32),
            pltpu.SemaphoreType.DMA((NT, 2, 2)),
            pltpu.SemaphoreType.DMA((NT, 2, 2)),
            pltpu.SemaphoreType.DMA((2,)),
        ],
        compiler_params=pltpu.CompilerParams(collective_id=0, has_side_effects=True),
    )(
        src,
        wave.astype(jnp.float32),
        rrow,
        rcol,
        resid.T,
        model,
        state_fwd.astype(jnp.float32),
        state_adj.astype(jnp.float32),
    )


def body(
    velocity_tiles,
    forward_state,
    adjoint_state,
    wavelet,
    source_cell,
    receiver_cell,
    residual,
    aperture_row,
    aperture_col,
):
    groups = lax.axis_size("shot")
    own_cols = groups // AP_ROWS
    caps = (AP_COLS + own_cols) // own_cols
    assert own_cols == AP_COLS and caps == 2 and forward_state.shape[0] == 1
    n_sub = lax.axis_size("sub")
    assert n_sub == 2 * X_CHIPS and groups % GROUP_ROW == 0
    outbound = [
        (g * n_sub + b, g * n_sub + device_of(g, b)) for g in range(groups) for b in range(n_sub)
    ]
    myself = lax.axis_index("shot")
    shots_here = forward_state.shape[0]
    gradient = jnp.zeros(velocity_tiles.shape, jnp.float32)
    every_shot = list(range(shots_here))
    states_moved = []
    for k in range(shots_here):
        states = jnp.concatenate(
            [forward_state[k].astype(jnp.float32), adjoint_state[k].astype(jnp.float32)]
        )
        states_moved.append(lax.ppermute(states, ("shot", "sub"), outbound))
    sending = outgoing(
        velocity_tiles, aperture_row, aperture_col, every_shot, groups, own_cols, caps
    )
    fetched = lax.all_to_all(sending, "shot", split_axis=0, concat_axis=0, tiled=True)
    images = []
    for k in every_shot:
        shot_id = myself * SHOTS_DEV + k
        row_start = aperture_row[shot_id]
        col_start = aperture_col[shot_id]
        model = assemble(fetched, row_start, col_start, own_cols)
        model = lax.ppermute(model, ("shot", "sub"), outbound)
        states = states_moved[k]
        image = migrate(
            model,
            states[0:2],
            states[2:4],
            wavelet[k],
            source_cell[k],
            receiver_cell[k],
            residual[k],
        )
        images.append(disperse(image, row_start, col_start, groups, own_cols, caps))
    returned = lax.all_to_all(images[0], "shot", split_axis=0, concat_axis=0, tiled=True)
    gradient = accumulate(
        gradient, returned, aperture_row, aperture_col, every_shot, groups, own_cols, caps
    )
    return gradient


def solution(mesh):
    placed = (
        P("shot", "sub", None),
        P("shot", None, "sub", None, None),
        P("shot", None, "sub", None, None),
        P("shot", None),
        P("shot"),
        P("shot", None),
        P("shot", None, None),
        P(),
        P(),
    )
    return jax.shard_map(
        body, mesh=mesh, in_specs=placed, out_specs=P("shot", "sub", None), check_vma=False
    )
```

```python
import jax
import jax.numpy as jnp
from jax import lax
from jax.sharding import PartitionSpec as P
from jax.experimental import pallas as pl
from jax.experimental.pallas import tpu as pltpu

TILE = 16
RY = 3
SHOTS_DEV = 1
NT = 4
RADIUS = 4
AP_ROWS = 4
AP_COLS = 8
TILE_DEV = 12
AX = 64
AY = 128


COEFFS = (-205.0 / 72.0, 8.0 / 5.0, -1.0 / 5.0, 8.0 / 315.0, -1.0 / 560.0)
IMAGE_SCALE = 1.0 / 64.0


def padded_2(array, sides, width):
    for axis, dim in sides:
        size, length = (lax.axis_size(axis), array.shape[dim])
        up = [(i, (i + 1) % size) for i in range(size - 1)]
        down = [(j, i) for i, j in up]
        last = lax.slice_in_dim(array, length - width, length, axis=dim)
        first = lax.slice_in_dim(array, 0, width, axis=dim)
        before = lax.ppermute(last, axis, up)
        after = lax.ppermute(first, axis, down)
        array = jnp.concatenate([before, array, after], axis=dim)
    return array


def laplace(padded, depth_cells, row_cells, column_cells):
    r = 4
    center = padded[r : r + depth_cells, r : r + row_cells, r : r + column_cells]
    summed = 3.0 * COEFFS[0] * center
    for k in range(1, 5):
        nearby = padded[r + k : r + k + depth_cells, r : r + row_cells, r : r + column_cells]
        nearby = (
            nearby + padded[r - k : r - k + depth_cells, r : r + row_cells, r : r + column_cells]
        )
        nearby = (
            nearby + padded[r : r + depth_cells, r + k : r + k + row_cells, r : r + column_cells]
        )
        nearby = (
            nearby + padded[r : r + depth_cells, r - k : r - k + row_cells, r : r + column_cells]
        )
        nearby = (
            nearby + padded[r : r + depth_cells, r : r + row_cells, r + k : r + k + column_cells]
        )
        nearby = (
            nearby + padded[r : r + depth_cells, r : r + row_cells, r - k : r - k + column_cells]
        )
        summed = summed + COEFFS[k] * nearby
    return summed


def wave_operator(field):
    padded = padded_2(field, (("sub", 0),), RADIUS)
    padded = jnp.pad(padded, ((0, 0), (4, 4), (4, 4)))
    return laplace(padded, field.shape[0], AX, AY)


def adjoint_operator(field):
    padded = padded_2(field, (("sub", 0),), RADIUS)
    padded = jnp.pad(padded, ((0, 0), (4, 4), (4, 4)))
    return laplace(padded, field.shape[0], AX, AY)


def slot_layout(row_start, col_start, owner_row, owner_col, own_cols, caps):
    block_row = (owner_row - row_start) % AP_ROWS
    first_col = (owner_col - col_start // TILE) % own_cols
    block_col = first_col + own_cols * jnp.arange(caps, dtype=jnp.int32)
    usable = block_col <= AP_COLS
    return (block_row, block_col, usable)


def owner_slots(row_table, col_table, shot_list, groups, own_cols, caps):
    myself = lax.axis_index("shot")
    owner_row = myself // own_cols
    owner_col = myself % own_cols
    senders = jnp.arange(groups, dtype=jnp.int32)[:, None]
    if SHOTS_DEV == 1 and list(shot_list) == [0]:
        row_start = row_table[:groups].reshape(groups, 1, 1)
        col_start = col_table[:groups].reshape(groups, 1, 1)
    else:
        picked = senders * SHOTS_DEV + jnp.asarray(shot_list, dtype=jnp.int32)[None, :]
        row_start = row_table[picked][..., None]
        col_start = col_table[picked][..., None]
    block_row, block_col, usable = slot_layout(
        row_start, col_start, owner_row, owner_col, own_cols, caps
    )
    tile_row = row_start + block_row
    tile_col = col_start // TILE + block_col
    local = tile_row // AP_ROWS * RY + tile_col // own_cols
    local = jnp.clip(local, 0, TILE_DEV - 1)
    return (local.reshape(-1), usable.reshape(-1))


def lane_column():
    return jnp.arange(TILE * TILE, dtype=jnp.int32) % TILE


def merge_slots(pair, spare_ok, offset):
    lower = spare_ok & (lane_column() < offset)
    return jnp.where(lower, pair[:, 1], pair[:, 0])


def outgoing(velocity_tiles, row_table, col_table, shot_list, groups, own_cols, caps):
    local, usable = owner_slots(row_table, col_table, shot_list, groups, own_cols, caps)
    chosen = velocity_tiles[local]
    chosen = jnp.where(usable[:, None, None], chosen, 0.0)
    chosen = chosen.reshape(groups, caps, velocity_tiles.shape[1], velocity_tiles.shape[2])
    usable = usable.reshape(groups, caps)
    offset = (col_table[:groups] % TILE).reshape(groups, 1, 1)
    merged = merge_slots(chosen, usable[:, 1, None, None], offset)
    return merged.reshape(groups, 1, velocity_tiles.shape[1], velocity_tiles.shape[2])


def accumulate(gradient, returned, row_table, col_table, shot_list, groups, own_cols, caps):
    local, usable = owner_slots(row_table, col_table, shot_list, groups, own_cols, caps)
    usable = usable.reshape(groups, caps)
    offset = (col_table[:groups] % TILE).reshape(groups, 1, 1)
    lower = lane_column() < offset
    piece = returned.reshape(groups, gradient.shape[1], gradient.shape[2])
    spare = usable[:, 1, None, None]
    first = jnp.where(spare & lower, 0.0, piece)
    second = jnp.where(spare & lower, piece, 0.0)
    pieces = jnp.stack([first, second], axis=1).reshape(groups * caps, -1)
    hot = (local[:, None] == jnp.arange(gradient.shape[0], dtype=jnp.int32)[None, :]) & usable.reshape(-1)[:, None]
    summed = jnp.einsum(
        "st,sf->tf", hot.astype(jnp.float32), pieces, precision=lax.Precision.HIGHEST
    )
    return gradient + summed.reshape(gradient.shape)


def assemble(received, row_start, col_start, own_cols):
    depth_cells = received.shape[2]
    block = received.reshape(AP_ROWS, own_cols, depth_cells, TILE, TILE)
    block = block.transpose(2, 0, 3, 1, 4).reshape(depth_cells, AX, AY)
    block = jnp.roll(block, -(row_start * TILE), axis=1)
    return jnp.roll(block, -col_start, axis=2)


def disperse(image, row_start, col_start, groups, own_cols, caps):
    depth_cells = image.shape[0]
    rolled = jnp.roll(image, row_start * TILE, axis=1)
    rolled = jnp.roll(rolled, col_start, axis=2)
    pieces = rolled.reshape(depth_cells, AP_ROWS, TILE, own_cols, TILE)
    pieces = pieces.transpose(1, 3, 0, 2, 4)
    return pieces.reshape(groups, 1, depth_cells, TILE * TILE)


X_CHIPS = 4
GROUP_ROW = 8


def crossing(group):
    return (group // GROUP_ROW * 2 + group % 2) % X_CHIPS


def mirror(group):
    return group % 2


def block_of(group, sub):
    cross = crossing(group)
    x, side = sub // 2, sub % 2
    flip = mirror(group)
    half = side + flip - 2 * side * flip
    low = (x - cross + 2 * X_CHIPS - 1) % X_CHIPS
    high = X_CHIPS + (cross - x + X_CHIPS) % X_CHIPS
    return (1 - half) * low + half * high


def device_of(group, block):
    cross = crossing(group)
    half = block // X_CHIPS
    low = (cross + 1 + block) % X_CHIPS
    high = (cross - block + 2 * X_CHIPS) % X_CHIPS
    flip = mirror(group)
    side = half + flip - 2 * half * flip
    return ((1 - half) * low + half * high) * 2 + side


def shift_rows(c, k, rows):
    if k > 0:
        moved = pltpu.roll(c, AX - k, 0)
        return jnp.where(rows < AX - k, moved, 0.0)
    moved = pltpu.roll(c, -k, 0)
    return jnp.where(rows >= -k, moved, 0.0)


def shift_lanes(c, k, lanes):
    if k > 0:
        moved = pltpu.roll(c, AY - k, 1)
        return jnp.where(lanes < AY - k, moved, 0.0)
    moved = pltpu.roll(c, -k, 1)
    return jnp.where(lanes >= -k, moved, 0.0)


def plane_stencil(buf, r, p, rows, lanes):
    c = buf[r, p]
    summed = (3.0 * COEFFS[0]) * c
    for k in range(1, 5):
        nearby = buf[r, p + k] + buf[r, p - k]
        nearby = nearby + shift_rows(c, k, rows)
        nearby = nearby + shift_rows(c, -k, rows)
        nearby = nearby + shift_lanes(c, k, lanes)
        nearby = nearby + shift_lanes(c, -k, lanes)
        summed = summed + COEFFS[k] * nearby
    return summed


def split_bf16(values):
    high = values.astype(jnp.bfloat16)
    rest = values - high.astype(jnp.float32)
    middle = rest.astype(jnp.bfloat16)
    low = (rest - middle.astype(jnp.float32)).astype(jnp.bfloat16)
    return (high, middle, low)


def migrate_kernel(
    src_ref, wave_ref, rrow_ref, rcol_ref, resid_ref, model_ref, pf_ref, qa_ref,
    img_ref, pad_p, pad_q, lap, qs, inject, img_loc, img_scr, send_sem, recv_sem, image_sem,
):
    group = lax.axis_index("shot")
    sub = lax.axis_index("sub")
    me = block_of(group, sub)
    n_sub = lax.axis_size("sub")
    depth = model_ref.shape[0]
    halo = jnp.zeros((RADIUS, AX, AY), jnp.float32)
    for r in range(NT):
        for buf in (pad_p, pad_q):
            buf[r, 0:RADIUS] = halo
            buf[r, RADIUS + depth : 2 * RADIUS + depth] = halo
    pad_p[0, RADIUS : RADIUS + depth] = pf_ref[0]
    pad_q[0, RADIUS : RADIUS + depth] = model_ref[...] * qa_ref[0]
    up_dev = device_of(group, (me + 1) % n_sub)
    down_dev = device_of(group, (me + n_sub - 1) % n_sub)
    target = device_of(group, sub)
    moved = target != sub
    mesh_id = pl.DeviceIdType.MESH
    barrier = pltpu.get_barrier_semaphore()
    pl.semaphore_signal(barrier, 1, device_id={"sub": up_dev}, device_id_type=mesh_id)
    pl.semaphore_signal(barrier, 1, device_id={"sub": down_dev}, device_id_type=mesh_id)

    @pl.when(moved)
    def _():
        pl.semaphore_signal(barrier, 1, device_id={"sub": target}, device_id_type=mesh_id)
        pl.semaphore_signal(barrier, 1, device_id={"sub": me}, device_id_type=mesh_id)
        pl.semaphore_wait(barrier, 4)

    @pl.when(jnp.logical_not(moved))
    def _():
        pl.semaphore_wait(barrier, 2)
    rows = lax.broadcasted_iota(jnp.int32, (AX, AY), 0)
    lanes = lax.broadcasted_iota(jnp.int32, (AX, AY), 1)
    n_rec = rcol_ref.shape[0]
    src_level = src_ref[0]
    src_spot = (rows == src_ref[1]) & (lanes == src_ref[2])

    def build_injection(step):
        hit_y = lax.broadcasted_iota(jnp.int32, (n_rec, AY), 1) == rcol_ref[...]
        spread = jnp.where(hit_y, resid_ref[:, step : step + 1], 0.0)
        parts = split_bf16(spread)
        rec_level = rrow_ref[0:1, :]
        hit_x = lax.broadcasted_iota(jnp.int32, (AX, n_rec), 0) == rrow_ref[1:2, :]

        def plane(j, carry):
            picks = (hit_x & (rec_level == j)).astype(jnp.bfloat16)
            total = jnp.dot(picks, parts[0], preferred_element_type=jnp.float32)
            total = total + jnp.dot(picks, parts[1], preferred_element_type=jnp.float32)
            total = total + jnp.dot(picks, parts[2], preferred_element_type=jnp.float32)
            inject[j] = total
            return carry

        lax.fori_loop(0, depth, plane, 0)

    def exchange(r, f):
        buf = (pad_p, pad_q)[f]
        down = pltpu.make_async_remote_copy(
            src_ref=buf.at[r, RADIUS : 2 * RADIUS],
            dst_ref=buf.at[r, RADIUS + depth : 2 * RADIUS + depth],
            send_sem=send_sem.at[r, f, 0],
            recv_sem=recv_sem.at[r, f, 0],
            device_id={"sub": down_dev},
            device_id_type=pl.DeviceIdType.MESH,
        )
        up = pltpu.make_async_remote_copy(
            src_ref=buf.at[r, depth : RADIUS + depth],
            dst_ref=buf.at[r, 0:RADIUS],
            send_sem=send_sem.at[r, f, 1],
            recv_sem=recv_sem.at[r, f, 1],
            device_id={"sub": up_dev},
            device_id_type=pl.DeviceIdType.MESH,
        )

        @pl.when(me > 0)
        def _():
            down.start()

        @pl.when(me < n_sub - 1)
        def _():
            up.start()

        return (down, up)

    def finish(pair):
        down, up = pair

        @pl.when(me > 0)
        def _():
            down.wait_send()
            up.wait_recv()

        @pl.when(me < n_sub - 1)
        def _():
            up.wait_send()
            down.wait_recv()

    def forward_round(r):
        def plane(j, carry):
            p = j + RADIUS
            lp = plane_stencil(pad_p, r, p, rows, lanes)
            lap[r, j] = lp
            if r < NT - 1:
                before = pf_ref[1, j] if r == 0 else pad_p[r - 1, p]
                following = 2.0 * pad_p[r, p] - before + model_ref[j] * lp
                source = jnp.where(src_spot & (src_level == j), wave_ref[r], 0.0)
                pad_p[r + 1, p] = following + source
            return carry

        lax.fori_loop(0, depth, plane, 0)

    def adjoint_round(r):
        def plane(j, carry):
            p = j + RADIUS
            lq = plane_stencil(pad_q, r, p, rows, lanes)
            now = qa_ref[0, j] if r == 0 else qs[r - 1, j]
            if r == 0:
                later = qa_ref[1, j]
            elif r == 1:
                later = qa_ref[0, j]
            else:
                later = qs[r - 2, j]
            result = 2.0 * now - later + lq
            result = result + inject[j]
            if r < NT - 1:
                qs[r, j] = result
                pad_q[r + 1, p] = model_ref[j] * result
            else:
                image = jnp.zeros((AX, AY), jnp.float32)
                for s in range(NT - 1):
                    image = image + qs[s, j] * lap[NT - 1 - s, j]
                image = image + result * lap[0, j]
                img_loc[j] = IMAGE_SCALE * image
            return carry

        lax.fori_loop(0, depth, plane, 0)

    fwd = exchange(0, 0)
    adj = exchange(0, 1)
    build_injection(NT - 1)
    for r in range(NT):
        finish(fwd)
        forward_round(r)
        if r < NT - 1:
            fwd = exchange(r + 1, 0)
        finish(adj)
        adjoint_round(r)
        if r < NT - 1:
            adj = exchange(r + 1, 1)
            build_injection(NT - 2 - r)
    image_copy = pltpu.make_async_remote_copy(
        src_ref=img_loc,
        dst_ref=img_scr,
        send_sem=image_sem.at[0],
        recv_sem=image_sem.at[1],
        device_id={"sub": me},
        device_id_type=mesh_id,
    )

    @pl.when(moved)
    def _():
        image_copy.start()
        image_copy.wait_send()
        image_copy.wait_recv()
        img_ref[...] = img_scr[...]

    @pl.when(jnp.logical_not(moved))
    def _():
        img_ref[...] = img_loc[...]


def migrate(model, state_fwd, state_adj, wave, source, receivers, resid):
    depth_cells = model.shape[0]
    plane = AX * AY
    offset = block_of(lax.axis_index("shot"), lax.axis_index("sub")) * depth_cells

    def level_of(cells):
        level = cells // plane - offset
        inside = (level >= 0) & (level < depth_cells)
        return jnp.where(inside, level, -1)

    src = jnp.stack([level_of(source), source % plane // AY, source % AY]).astype(jnp.int32)
    rrow = jnp.stack([level_of(receivers), receivers % plane // AY]).astype(jnp.int32)
    rcol = (receivers % AY).astype(jnp.int32).reshape(-1, 1)
    vmem = pl.BlockSpec(memory_space=pltpu.VMEM)
    smem = pl.BlockSpec(memory_space=pltpu.SMEM)
    padded = (NT, depth_cells + 2 * RADIUS, AX, AY)
    field = (NT, depth_cells, AX, AY)
    return pl.pallas_call(
        migrate_kernel,
        out_shape=jax.ShapeDtypeStruct(model.shape, jnp.float32),
        in_specs=[smem, smem] + [vmem] * 6,
        out_specs=vmem,
        scratch_shapes=[
            pltpu.VMEM(padded, jnp.float32),
            pltpu.VMEM(padded, jnp.float32),
            pltpu.VMEM(field, jnp.float32),
            pltpu.VMEM(field, jnp.float32),
            pltpu.VMEM(model.shape, jnp.float32),
            pltpu.VMEM(model.shape, jnp.float32),
            pltpu.VMEM(model.shape, jnp.float32),
            pltpu.SemaphoreType.DMA((NT, 2, 2)),
            pltpu.SemaphoreType.DMA((NT, 2, 2)),
            pltpu.SemaphoreType.DMA((2,)),
        ],
        compiler_params=pltpu.CompilerParams(collective_id=0, has_side_effects=True),
    )(
        src,
        wave.astype(jnp.float32),
        rrow,
        rcol,
        resid.T,
        model,
        state_fwd.astype(jnp.float32),
        state_adj.astype(jnp.float32),
    )


def body(
    velocity_tiles,
    forward_state,
    adjoint_state,
    wavelet,
    source_cell,
    receiver_cell,
    residual,
    aperture_row,
    aperture_col,
):
    groups = lax.axis_size("shot")
    own_cols = groups // AP_ROWS
    caps = (AP_COLS + own_cols) // own_cols
    assert own_cols == AP_COLS and caps == 2 and forward_state.shape[0] == 1
    n_sub = lax.axis_size("sub")
    assert n_sub == 2 * X_CHIPS and groups % GROUP_ROW == 0
    outbound = [
        (g * n_sub + b, g * n_sub + device_of(g, b)) for g in range(groups) for b in range(n_sub)
    ]
    myself = lax.axis_index("shot")
    shots_here = forward_state.shape[0]
    gradient = jnp.zeros(velocity_tiles.shape, jnp.float32)
    every_shot = list(range(shots_here))
    states_moved = []
    for k in range(shots_here):
        states = jnp.concatenate(
            [forward_state[k].astype(jnp.float32), adjoint_state[k].astype(jnp.float32)]
        )
        states_moved.append(lax.ppermute(states, ("shot", "sub"), outbound))
    sending = outgoing(
        velocity_tiles, aperture_row, aperture_col, every_shot, groups, own_cols, caps
    )
    fetched = lax.all_to_all(sending, "shot", split_axis=0, concat_axis=0, tiled=True)
    images = []
    for k in every_shot:
        shot_id = myself * SHOTS_DEV + k
        row_start = aperture_row[shot_id]
        col_start = aperture_col[shot_id]
        model = assemble(fetched, row_start, col_start, own_cols)
        model = lax.ppermute(model, ("shot", "sub"), outbound)
        states = states_moved[k]
        image = migrate(
            model,
            states[0:2],
            states[2:4],
            wavelet[k],
            source_cell[k],
            receiver_cell[k],
            residual[k],
        )
        images.append(disperse(image, row_start, col_start, groups, own_cols, caps))
    returned = lax.all_to_all(images[0], "shot", split_axis=0, concat_axis=0, tiled=True)
    gradient = accumulate(
        gradient, returned, aperture_row, aperture_col, every_shot, groups, own_cols, caps
    )
    return gradient


def solution(mesh):
    placed = (
        P("shot", "sub", None),
        P("shot", None, "sub", None, None),
        P("shot", None, "sub", None, None),
        P("shot", None),
        P("shot"),
        P("shot", None),
        P("shot", None, None),
        P(),
        P(),
    )
    return jax.shard_map(
        body, mesh=mesh, in_specs=placed, out_specs=P("shot", "sub", None), check_vma=False
    )
```

```python
import functools

import jax
import jax.numpy as jnp
from jax import lax
from jax.sharding import PartitionSpec as P
from jax.experimental import pallas as pl
from jax.experimental.pallas import tpu as pltpu

TILE = 16
RY = 3
SHOTS_DEV = 1
NT = 4
RADIUS = 4
AP_ROWS = 4
AP_COLS = 8
TILE_DEV = 12
AX = 64
AY = 128


COEFFS = (-205.0 / 72.0, 8.0 / 5.0, -1.0 / 5.0, 8.0 / 315.0, -1.0 / 560.0)
IMAGE_SCALE = 1.0 / 64.0


def padded_2(array, sides, width):
    for axis, dim in sides:
        size, length = (lax.axis_size(axis), array.shape[dim])
        up = [(i, (i + 1) % size) for i in range(size - 1)]
        down = [(j, i) for i, j in up]
        last = lax.slice_in_dim(array, length - width, length, axis=dim)
        first = lax.slice_in_dim(array, 0, width, axis=dim)
        before = lax.ppermute(last, axis, up)
        after = lax.ppermute(first, axis, down)
        array = jnp.concatenate([before, array, after], axis=dim)
    return array


def laplace(padded, depth_cells, row_cells, column_cells):
    r = 4
    center = padded[r : r + depth_cells, r : r + row_cells, r : r + column_cells]
    summed = 3.0 * COEFFS[0] * center
    for k in range(1, 5):
        nearby = padded[r + k : r + k + depth_cells, r : r + row_cells, r : r + column_cells]
        nearby = (
            nearby + padded[r - k : r - k + depth_cells, r : r + row_cells, r : r + column_cells]
        )
        nearby = (
            nearby + padded[r : r + depth_cells, r + k : r + k + row_cells, r : r + column_cells]
        )
        nearby = (
            nearby + padded[r : r + depth_cells, r - k : r - k + row_cells, r : r + column_cells]
        )
        nearby = (
            nearby + padded[r : r + depth_cells, r : r + row_cells, r + k : r + k + column_cells]
        )
        nearby = (
            nearby + padded[r : r + depth_cells, r : r + row_cells, r - k : r - k + column_cells]
        )
        summed = summed + COEFFS[k] * nearby
    return summed


def wave_operator(field):
    padded = padded_2(field, (("sub", 0),), RADIUS)
    padded = jnp.pad(padded, ((0, 0), (4, 4), (4, 4)))
    return laplace(padded, field.shape[0], AX, AY)


def adjoint_operator(field):
    padded = padded_2(field, (("sub", 0),), RADIUS)
    padded = jnp.pad(padded, ((0, 0), (4, 4), (4, 4)))
    return laplace(padded, field.shape[0], AX, AY)


def slot_layout(row_start, col_start, owner_row, owner_col, own_cols, caps):
    block_row = (owner_row - row_start) % AP_ROWS
    first_col = (owner_col - col_start // TILE) % own_cols
    block_col = first_col + own_cols * jnp.arange(caps, dtype=jnp.int32)
    usable = block_col <= AP_COLS
    return (block_row, block_col, usable)


def owner_slots(row_table, col_table, shot_list, groups, own_cols, caps):
    myself = lax.axis_index("shot")
    owner_row = myself // own_cols
    owner_col = myself % own_cols
    senders = jnp.arange(groups, dtype=jnp.int32)[:, None]
    if SHOTS_DEV == 1 and list(shot_list) == [0]:
        row_start = row_table[:groups].reshape(groups, 1, 1)
        col_start = col_table[:groups].reshape(groups, 1, 1)
    else:
        picked = senders * SHOTS_DEV + jnp.asarray(shot_list, dtype=jnp.int32)[None, :]
        row_start = row_table[picked][..., None]
        col_start = col_table[picked][..., None]
    block_row, block_col, usable = slot_layout(
        row_start, col_start, owner_row, owner_col, own_cols, caps
    )
    tile_row = row_start + block_row
    tile_col = col_start // TILE + block_col
    local = tile_row // AP_ROWS * RY + tile_col // own_cols
    local = jnp.clip(local, 0, TILE_DEV - 1)
    return (local.reshape(-1), usable.reshape(-1))


def lane_column():
    return jnp.arange(TILE * TILE, dtype=jnp.int32) % TILE


def merge_slots(pair, spare_ok, offset):
    lower = spare_ok & (lane_column() < offset)
    return jnp.where(lower, pair[:, 1], pair[:, 0])


def outgoing(velocity_tiles, row_table, col_table, shot_list, groups, own_cols, caps):
    local, usable = owner_slots(row_table, col_table, shot_list, groups, own_cols, caps)
    chosen = velocity_tiles[local]
    chosen = jnp.where(usable[:, None, None], chosen, 0.0)
    chosen = chosen.reshape(groups, caps, velocity_tiles.shape[1], velocity_tiles.shape[2])
    usable = usable.reshape(groups, caps)
    offset = (col_table[:groups] % TILE).reshape(groups, 1, 1)
    merged = merge_slots(chosen, usable[:, 1, None, None], offset)
    return merged.reshape(groups, 1, velocity_tiles.shape[1], velocity_tiles.shape[2])


def accumulate(gradient, returned, row_table, col_table, shot_list, groups, own_cols, caps):
    local, usable = owner_slots(row_table, col_table, shot_list, groups, own_cols, caps)
    usable = usable.reshape(groups, caps)
    offset = (col_table[:groups] % TILE).reshape(groups, 1, 1)
    lower = lane_column() < offset
    piece = returned.reshape(groups, gradient.shape[1], gradient.shape[2])
    spare = usable[:, 1, None, None]
    first = jnp.where(spare & lower, 0.0, piece)
    second = jnp.where(spare & lower, piece, 0.0)
    pieces = jnp.stack([first, second], axis=1).reshape(groups * caps, -1)
    hot = (local[:, None] == jnp.arange(gradient.shape[0], dtype=jnp.int32)[None, :]) & usable.reshape(-1)[:, None]
    summed = jnp.einsum(
        "st,sf->tf", hot.astype(jnp.float32), pieces, precision=lax.Precision.HIGHEST
    )
    return gradient + summed.reshape(gradient.shape)


def assemble(received, row_start, col_start, own_cols):
    depth_cells = received.shape[2]
    block = received.reshape(AP_ROWS, own_cols, depth_cells, TILE, TILE)
    block = block.transpose(2, 0, 3, 1, 4).reshape(depth_cells, AX, AY)
    block = jnp.roll(block, -(row_start * TILE), axis=1)
    return jnp.roll(block, -col_start, axis=2)


def disperse(image, row_start, col_start, groups, own_cols, caps):
    depth_cells = image.shape[0]
    rolled = jnp.roll(image, row_start * TILE, axis=1)
    rolled = jnp.roll(rolled, col_start, axis=2)
    pieces = rolled.reshape(depth_cells, AP_ROWS, TILE, own_cols, TILE)
    pieces = pieces.transpose(1, 3, 0, 2, 4)
    return pieces.reshape(groups, 1, depth_cells, TILE * TILE)


X_CHIPS = 4
GROUP_ROW = 8


def crossing(group):
    return (group // GROUP_ROW * 2 + group % 2) % X_CHIPS


def mirror(group):
    return group % 2


def block_of(group, sub):
    cross = crossing(group)
    x, side = sub // 2, sub % 2
    flip = mirror(group)
    half = side + flip - 2 * side * flip
    low = (x - cross + 2 * X_CHIPS - 1) % X_CHIPS
    high = X_CHIPS + (cross - x + X_CHIPS) % X_CHIPS
    return (1 - half) * low + half * high


def device_of(group, block):
    cross = crossing(group)
    half = block // X_CHIPS
    low = (cross + 1 + block) % X_CHIPS
    high = (cross - block + 2 * X_CHIPS) % X_CHIPS
    flip = mirror(group)
    side = half + flip - 2 * half * flip
    return ((1 - half) * low + half * high) * 2 + side


def shift_rows(c, k, rows):
    if k > 0:
        moved = pltpu.roll(c, AX - k, 0)
        return jnp.where(rows < AX - k, moved, 0.0)
    moved = pltpu.roll(c, -k, 0)
    return jnp.where(rows >= -k, moved, 0.0)


def shift_lanes(c, k, lanes):
    if k > 0:
        moved = pltpu.roll(c, AY - k, 1)
        return jnp.where(lanes < AY - k, moved, 0.0)
    moved = pltpu.roll(c, -k, 1)
    return jnp.where(lanes >= -k, moved, 0.0)


def plane_stencil(buf, r, p, rows, lanes):
    c = buf[r, p]
    summed = (3.0 * COEFFS[0]) * c
    for k in range(1, 5):
        nearby = buf[r, p + k] + buf[r, p - k]
        nearby = nearby + shift_rows(c, k, rows)
        nearby = nearby + shift_rows(c, -k, rows)
        nearby = nearby + shift_lanes(c, k, lanes)
        nearby = nearby + shift_lanes(c, -k, lanes)
        summed = summed + COEFFS[k] * nearby
    return summed


def split_bf16(values):
    high = values.astype(jnp.bfloat16)
    rest = values - high.astype(jnp.float32)
    middle = rest.astype(jnp.bfloat16)
    low = (rest - middle.astype(jnp.float32)).astype(jnp.bfloat16)
    return (high, middle, low)


def migrate_kernel(
    src_ref, wave_ref, rrow_ref, rcol_ref, resid_ref, model_ref, pf_ref, qa_ref,
    img_ref, pad_p, pad_q, lap, qs, inject, img_loc, img_scr, send_sem, recv_sem, image_sem,
):
    group = lax.axis_index("shot")
    sub = lax.axis_index("sub")
    me = block_of(group, sub)
    n_sub = lax.axis_size("sub")
    depth = model_ref.shape[0]
    halo = jnp.zeros((RADIUS, AX, AY), jnp.float32)
    for r in range(NT):
        for buf in (pad_p, pad_q):
            buf[r, 0:RADIUS] = halo
            buf[r, RADIUS + depth : 2 * RADIUS + depth] = halo
    pad_p[0, RADIUS : RADIUS + depth] = pf_ref[0]
    pad_q[0, RADIUS : RADIUS + depth] = model_ref[...] * qa_ref[0]
    up_dev = device_of(group, (me + 1) % n_sub)
    down_dev = device_of(group, (me + n_sub - 1) % n_sub)
    target = device_of(group, sub)
    moved = target != sub
    mesh_id = pl.DeviceIdType.MESH
    barrier = pltpu.get_barrier_semaphore()
    pl.semaphore_signal(barrier, 1, device_id={"sub": up_dev}, device_id_type=mesh_id)
    pl.semaphore_signal(barrier, 1, device_id={"sub": down_dev}, device_id_type=mesh_id)

    @pl.when(moved)
    def _():
        pl.semaphore_signal(barrier, 1, device_id={"sub": target}, device_id_type=mesh_id)
        pl.semaphore_signal(barrier, 1, device_id={"sub": me}, device_id_type=mesh_id)
        pl.semaphore_wait(barrier, 4)

    @pl.when(jnp.logical_not(moved))
    def _():
        pl.semaphore_wait(barrier, 2)
    rows = lax.broadcasted_iota(jnp.int32, (AX, AY), 0)
    lanes = lax.broadcasted_iota(jnp.int32, (AX, AY), 1)
    n_rec = rcol_ref.shape[0]
    src_level = src_ref[0]
    src_spot = (rows == src_ref[1]) & (lanes == src_ref[2])

    def build_injection(step):
        hit_y = lax.broadcasted_iota(jnp.int32, (n_rec, AY), 1) == rcol_ref[...]
        spread = jnp.where(hit_y, resid_ref[:, step : step + 1], 0.0)
        parts = split_bf16(spread)
        rec_level = rrow_ref[0:1, :]
        hit_x = lax.broadcasted_iota(jnp.int32, (AX, n_rec), 0) == rrow_ref[1:2, :]

        def plane(j, carry):
            picks = (hit_x & (rec_level == j)).astype(jnp.bfloat16)
            total = jnp.dot(picks, parts[0], preferred_element_type=jnp.float32)
            total = total + jnp.dot(picks, parts[1], preferred_element_type=jnp.float32)
            total = total + jnp.dot(picks, parts[2], preferred_element_type=jnp.float32)
            inject[j] = total
            return carry

        lax.fori_loop(0, depth, plane, 0)

    def exchange(r, f, halves=(True, True)):
        buf = (pad_p, pad_q)[f]
        down = pltpu.make_async_remote_copy(
            src_ref=buf.at[r, RADIUS : 2 * RADIUS],
            dst_ref=buf.at[r, RADIUS + depth : 2 * RADIUS + depth],
            send_sem=send_sem.at[r, f, 0],
            recv_sem=recv_sem.at[r, f, 0],
            device_id={"sub": down_dev},
            device_id_type=pl.DeviceIdType.MESH,
        )
        up = pltpu.make_async_remote_copy(
            src_ref=buf.at[r, depth : RADIUS + depth],
            dst_ref=buf.at[r, 0:RADIUS],
            send_sem=send_sem.at[r, f, 1],
            recv_sem=recv_sem.at[r, f, 1],
            device_id={"sub": up_dev},
            device_id_type=pl.DeviceIdType.MESH,
        )

        if halves[0]:
            start_down(down)
        if halves[1]:
            start_up(up)
        return (down, up)

    def start_down(down):
        @pl.when(me > 0)
        def _():
            down.start()

    def start_up(up):
        @pl.when(me < n_sub - 1)
        def _():
            up.start()

    def finish(pair):
        down, up = pair

        @pl.when(me > 0)
        def _():
            down.wait_send()
            up.wait_recv()

        @pl.when(me < n_sub - 1)
        def _():
            up.wait_send()
            down.wait_recv()

    def forward_round(r, midway=None):
        def plane(j, carry):
            p = j + RADIUS
            lp = plane_stencil(pad_p, r, p, rows, lanes)
            lap[r, j] = lp
            if r < NT - 1:
                before = pf_ref[1, j] if r == 0 else pad_p[r - 1, p]
                following = 2.0 * pad_p[r, p] - before + model_ref[j] * lp
                source = jnp.where(src_spot & (src_level == j), wave_ref[r], 0.0)
                pad_p[r + 1, p] = following + source
            return carry

        half = depth // 2
        lax.fori_loop(0, half, plane, 0)
        if midway is not None:
            midway()
        lax.fori_loop(half, depth, plane, 0)

    def adjoint_round(r, midway=None):
        def plane(j, carry):
            p = j + RADIUS
            lq = plane_stencil(pad_q, r, p, rows, lanes)
            now = qa_ref[0, j] if r == 0 else qs[r - 1, j]
            if r == 0:
                later = qa_ref[1, j]
            elif r == 1:
                later = qa_ref[0, j]
            else:
                later = qs[r - 2, j]
            result = 2.0 * now - later + lq
            result = result + inject[j]
            if r < NT - 1:
                qs[r, j] = result
                pad_q[r + 1, p] = model_ref[j] * result
            else:
                image = jnp.zeros((AX, AY), jnp.float32)
                for s in range(NT - 1):
                    image = image + qs[s, j] * lap[NT - 1 - s, j]
                image = image + result * lap[0, j]
                img_loc[j] = IMAGE_SCALE * image
            return carry

        half = depth // 2
        lax.fori_loop(0, half, plane, 0)
        if midway is not None:
            midway()
        lax.fori_loop(half, depth, plane, 0)

    fwd = exchange(0, 0)
    adj = exchange(0, 1)
    build_injection(NT - 1)
    for r in range(NT):
        finish(fwd)
        if r < NT - 1:
            fwd = exchange(r + 1, 0, (False, False))
            forward_round(r, functools.partial(start_down, fwd[0]))
            start_up(fwd[1])
        else:
            forward_round(r)
        finish(adj)
        if r < NT - 1:
            adj = exchange(r + 1, 1, (False, False))
            adjoint_round(r, functools.partial(start_down, adj[0]))
            start_up(adj[1])
            build_injection(NT - 2 - r)
        else:
            adjoint_round(r)
    image_copy = pltpu.make_async_remote_copy(
        src_ref=img_loc,
        dst_ref=img_scr,
        send_sem=image_sem.at[0],
        recv_sem=image_sem.at[1],
        device_id={"sub": me},
        device_id_type=mesh_id,
    )

    @pl.when(moved)
    def _():
        image_copy.start()
        image_copy.wait_send()
        image_copy.wait_recv()
        img_ref[...] = img_scr[...]

    @pl.when(jnp.logical_not(moved))
    def _():
        img_ref[...] = img_loc[...]


def migrate(model, state_fwd, state_adj, wave, source, receivers, resid):
    depth_cells = model.shape[0]
    plane = AX * AY
    offset = block_of(lax.axis_index("shot"), lax.axis_index("sub")) * depth_cells

    def level_of(cells):
        level = cells // plane - offset
        inside = (level >= 0) & (level < depth_cells)
        return jnp.where(inside, level, -1)

    src = jnp.stack([level_of(source), source % plane // AY, source % AY]).astype(jnp.int32)
    rrow = jnp.stack([level_of(receivers), receivers % plane // AY]).astype(jnp.int32)
    rcol = (receivers % AY).astype(jnp.int32).reshape(-1, 1)
    vmem = pl.BlockSpec(memory_space=pltpu.VMEM)
    smem = pl.BlockSpec(memory_space=pltpu.SMEM)
    padded = (NT, depth_cells + 2 * RADIUS, AX, AY)
    field = (NT, depth_cells, AX, AY)
    return pl.pallas_call(
        migrate_kernel,
        out_shape=jax.ShapeDtypeStruct(model.shape, jnp.float32),
        in_specs=[smem, smem] + [vmem] * 6,
        out_specs=vmem,
        scratch_shapes=[
            pltpu.VMEM(padded, jnp.float32),
            pltpu.VMEM(padded, jnp.float32),
            pltpu.VMEM(field, jnp.float32),
            pltpu.VMEM(field, jnp.float32),
            pltpu.VMEM(model.shape, jnp.float32),
            pltpu.VMEM(model.shape, jnp.float32),
            pltpu.VMEM(model.shape, jnp.float32),
            pltpu.SemaphoreType.DMA((NT, 2, 2)),
            pltpu.SemaphoreType.DMA((NT, 2, 2)),
            pltpu.SemaphoreType.DMA((2,)),
        ],
        compiler_params=pltpu.CompilerParams(collective_id=0, has_side_effects=True),
    )(
        src,
        wave.astype(jnp.float32),
        rrow,
        rcol,
        resid.T,
        model,
        state_fwd.astype(jnp.float32),
        state_adj.astype(jnp.float32),
    )


def body(
    velocity_tiles,
    forward_state,
    adjoint_state,
    wavelet,
    source_cell,
    receiver_cell,
    residual,
    aperture_row,
    aperture_col,
):
    groups = lax.axis_size("shot")
    own_cols = groups // AP_ROWS
    caps = (AP_COLS + own_cols) // own_cols
    assert own_cols == AP_COLS and caps == 2 and forward_state.shape[0] == 1
    n_sub = lax.axis_size("sub")
    assert n_sub == 2 * X_CHIPS and groups % GROUP_ROW == 0
    outbound = [
        (g * n_sub + b, g * n_sub + device_of(g, b)) for g in range(groups) for b in range(n_sub)
    ]
    myself = lax.axis_index("shot")
    shots_here = forward_state.shape[0]
    gradient = jnp.zeros(velocity_tiles.shape, jnp.float32)
    every_shot = list(range(shots_here))
    states_moved = []
    for k in range(shots_here):
        states = jnp.concatenate(
            [forward_state[k].astype(jnp.float32), adjoint_state[k].astype(jnp.float32)]
        )
        states_moved.append(lax.ppermute(states, ("shot", "sub"), outbound))
    sending = outgoing(
        velocity_tiles, aperture_row, aperture_col, every_shot, groups, own_cols, caps
    )
    fetched = lax.all_to_all(sending, "shot", split_axis=0, concat_axis=0, tiled=True)
    images = []
    for k in every_shot:
        shot_id = myself * SHOTS_DEV + k
        row_start = aperture_row[shot_id]
        col_start = aperture_col[shot_id]
        model = assemble(fetched, row_start, col_start, own_cols)
        model = lax.ppermute(model, ("shot", "sub"), outbound)
        states = states_moved[k]
        image = migrate(
            model,
            states[0:2],
            states[2:4],
            wavelet[k],
            source_cell[k],
            receiver_cell[k],
            residual[k],
        )
        images.append(disperse(image, row_start, col_start, groups, own_cols, caps))
    returned = lax.all_to_all(images[0], "shot", split_axis=0, concat_axis=0, tiled=True)
    gradient = accumulate(
        gradient, returned, aperture_row, aperture_col, every_shot, groups, own_cols, caps
    )
    return gradient


def solution(mesh):
    placed = (
        P("shot", "sub", None),
        P("shot", None, "sub", None, None),
        P("shot", None, "sub", None, None),
        P("shot", None),
        P("shot"),
        P("shot", None),
        P("shot", None, None),
        P(),
        P(),
    )
    return jax.shard_map(
        body, mesh=mesh, in_specs=placed, out_specs=P("shot", "sub", None), check_vma=False
    )
```

```python
import jax
import jax.numpy as jnp
from jax import lax
from jax.sharding import PartitionSpec as P
from jax.experimental import pallas as pl
from jax.experimental.pallas import tpu as pltpu

TILE = 16
RY = 3
SHOTS_DEV = 1
NT = 4
RADIUS = 4
AP_ROWS = 4
AP_COLS = 8
TILE_DEV = 12
AX = 64
AY = 128


COEFFS = (-205.0 / 72.0, 8.0 / 5.0, -1.0 / 5.0, 8.0 / 315.0, -1.0 / 560.0)
IMAGE_SCALE = 1.0 / 64.0


def padded_2(array, sides, width):
    for axis, dim in sides:
        size, length = (lax.axis_size(axis), array.shape[dim])
        up = [(i, (i + 1) % size) for i in range(size - 1)]
        down = [(j, i) for i, j in up]
        last = lax.slice_in_dim(array, length - width, length, axis=dim)
        first = lax.slice_in_dim(array, 0, width, axis=dim)
        before = lax.ppermute(last, axis, up)
        after = lax.ppermute(first, axis, down)
        array = jnp.concatenate([before, array, after], axis=dim)
    return array


def laplace(padded, depth_cells, row_cells, column_cells):
    r = 4
    center = padded[r : r + depth_cells, r : r + row_cells, r : r + column_cells]
    summed = 3.0 * COEFFS[0] * center
    for k in range(1, 5):
        nearby = padded[r + k : r + k + depth_cells, r : r + row_cells, r : r + column_cells]
        nearby = (
            nearby + padded[r - k : r - k + depth_cells, r : r + row_cells, r : r + column_cells]
        )
        nearby = (
            nearby + padded[r : r + depth_cells, r + k : r + k + row_cells, r : r + column_cells]
        )
        nearby = (
            nearby + padded[r : r + depth_cells, r - k : r - k + row_cells, r : r + column_cells]
        )
        nearby = (
            nearby + padded[r : r + depth_cells, r : r + row_cells, r + k : r + k + column_cells]
        )
        nearby = (
            nearby + padded[r : r + depth_cells, r : r + row_cells, r - k : r - k + column_cells]
        )
        summed = summed + COEFFS[k] * nearby
    return summed


def wave_operator(field):
    padded = padded_2(field, (("sub", 0),), RADIUS)
    padded = jnp.pad(padded, ((0, 0), (4, 4), (4, 4)))
    return laplace(padded, field.shape[0], AX, AY)


def adjoint_operator(field):
    padded = padded_2(field, (("sub", 0),), RADIUS)
    padded = jnp.pad(padded, ((0, 0), (4, 4), (4, 4)))
    return laplace(padded, field.shape[0], AX, AY)


def slot_layout(row_start, col_start, owner_row, owner_col, own_cols, caps):
    block_row = (owner_row - row_start) % AP_ROWS
    first_col = (owner_col - col_start // TILE) % own_cols
    block_col = first_col + own_cols * jnp.arange(caps, dtype=jnp.int32)
    usable = block_col <= AP_COLS
    return (block_row, block_col, usable)


def owner_slots(row_table, col_table, shot_list, groups, own_cols, caps):
    myself = lax.axis_index("shot")
    owner_row = myself // own_cols
    owner_col = myself % own_cols
    senders = jnp.arange(groups, dtype=jnp.int32)[:, None]
    if SHOTS_DEV == 1 and list(shot_list) == [0]:
        row_start = row_table[:groups].reshape(groups, 1, 1)
        col_start = col_table[:groups].reshape(groups, 1, 1)
    else:
        picked = senders * SHOTS_DEV + jnp.asarray(shot_list, dtype=jnp.int32)[None, :]
        row_start = row_table[picked][..., None]
        col_start = col_table[picked][..., None]
    block_row, block_col, usable = slot_layout(
        row_start, col_start, owner_row, owner_col, own_cols, caps
    )
    tile_row = row_start + block_row
    tile_col = col_start // TILE + block_col
    local = tile_row // AP_ROWS * RY + tile_col // own_cols
    local = jnp.clip(local, 0, TILE_DEV - 1)
    return (local.reshape(-1), usable.reshape(-1))


def lane_column():
    return jnp.arange(TILE * TILE, dtype=jnp.int32) % TILE


def merge_slots(pair, spare_ok, offset):
    lower = spare_ok & (lane_column() < offset)
    return jnp.where(lower, pair[:, 1], pair[:, 0])


def outgoing(velocity_tiles, row_table, col_table, shot_list, groups, own_cols, caps):
    local, usable = owner_slots(row_table, col_table, shot_list, groups, own_cols, caps)
    chosen = velocity_tiles[local]
    chosen = jnp.where(usable[:, None, None], chosen, 0.0)
    chosen = chosen.reshape(groups, caps, velocity_tiles.shape[1], velocity_tiles.shape[2])
    usable = usable.reshape(groups, caps)
    offset = (col_table[:groups] % TILE).reshape(groups, 1, 1)
    merged = merge_slots(chosen, usable[:, 1, None, None], offset)
    return merged.reshape(groups, 1, velocity_tiles.shape[1], velocity_tiles.shape[2])


def accumulate(gradient, returned, row_table, col_table, shot_list, groups, own_cols, caps):
    local, usable = owner_slots(row_table, col_table, shot_list, groups, own_cols, caps)
    usable = usable.reshape(groups, caps)
    offset = (col_table[:groups] % TILE).reshape(groups, 1, 1)
    lower = lane_column() < offset
    piece = returned.reshape(groups, gradient.shape[1], gradient.shape[2])
    spare = usable[:, 1, None, None]
    first = jnp.where(spare & lower, 0.0, piece)
    second = jnp.where(spare & lower, piece, 0.0)
    hot = (local[:, None] == jnp.arange(gradient.shape[0], dtype=jnp.int32)[None, :]) & usable.reshape(-1)[:, None]
    hot = hot.astype(jnp.float32).reshape(groups, caps, -1)
    summed = jnp.einsum(
        "st,sf->tf", hot[:, 0], first.reshape(groups, -1), precision=lax.Precision.HIGHEST
    )
    summed = summed + jnp.einsum(
        "st,sf->tf", hot[:, 1], second.reshape(groups, -1), precision=lax.Precision.HIGHEST
    )
    return gradient + summed.reshape(gradient.shape)


def assemble(received, row_start, col_start, own_cols):
    depth_cells = received.shape[2]
    block = received.reshape(AP_ROWS, own_cols, depth_cells, TILE, TILE)
    block = block.transpose(2, 0, 3, 1, 4).reshape(depth_cells, AX, AY)
    block = jnp.roll(block, -(row_start * TILE), axis=1)
    return jnp.roll(block, -col_start, axis=2)


def disperse(image, row_start, col_start, groups, own_cols, caps):
    depth_cells = image.shape[0]
    rolled = jnp.roll(image, row_start * TILE, axis=1)
    rolled = jnp.roll(rolled, col_start, axis=2)
    pieces = rolled.reshape(depth_cells, AP_ROWS, TILE, own_cols, TILE)
    pieces = pieces.transpose(1, 3, 0, 2, 4)
    return pieces.reshape(groups, 1, depth_cells, TILE * TILE)


X_CHIPS = 4
GROUP_ROW = 8


def crossing(group):
    return (group // GROUP_ROW * 2 + group % 2) % X_CHIPS


def mirror(group):
    return group % 2


def block_of(group, sub):
    cross = crossing(group)
    x, side = sub // 2, sub % 2
    flip = mirror(group)
    half = side + flip - 2 * side * flip
    low = (x - cross + 2 * X_CHIPS - 1) % X_CHIPS
    high = X_CHIPS + (cross - x + X_CHIPS) % X_CHIPS
    return (1 - half) * low + half * high


def device_of(group, block):
    cross = crossing(group)
    half = block // X_CHIPS
    low = (cross + 1 + block) % X_CHIPS
    high = (cross - block + 2 * X_CHIPS) % X_CHIPS
    flip = mirror(group)
    side = half + flip - 2 * half * flip
    return ((1 - half) * low + half * high) * 2 + side


def shift_rows(c, k, rows):
    if k > 0:
        moved = pltpu.roll(c, AX - k, 0)
        return jnp.where(rows < AX - k, moved, 0.0)
    moved = pltpu.roll(c, -k, 0)
    return jnp.where(rows >= -k, moved, 0.0)


def shift_lanes(c, k, lanes):
    if k > 0:
        moved = pltpu.roll(c, AY - k, 1)
        return jnp.where(lanes < AY - k, moved, 0.0)
    moved = pltpu.roll(c, -k, 1)
    return jnp.where(lanes >= -k, moved, 0.0)


def plane_stencil(buf, r, p, rows, lanes):
    c = buf[r, p]
    summed = (3.0 * COEFFS[0]) * c
    for k in range(1, 5):
        nearby = buf[r, p + k] + buf[r, p - k]
        nearby = nearby + shift_rows(c, k, rows)
        nearby = nearby + shift_rows(c, -k, rows)
        nearby = nearby + shift_lanes(c, k, lanes)
        nearby = nearby + shift_lanes(c, -k, lanes)
        summed = summed + COEFFS[k] * nearby
    return summed


def split_bf16(values):
    high = values.astype(jnp.bfloat16)
    rest = values - high.astype(jnp.float32)
    middle = rest.astype(jnp.bfloat16)
    low = (rest - middle.astype(jnp.float32)).astype(jnp.bfloat16)
    return (high, middle, low)


def migrate_kernel(
    src_ref, wave_ref, rrow_ref, rcol_ref, resid_ref, model_ref, pf_ref, qa_ref,
    img_ref, pad_p, pad_q, lap, qs, inject, img_loc, img_scr, send_sem, recv_sem, image_sem,
):
    group = lax.axis_index("shot")
    sub = lax.axis_index("sub")
    me = block_of(group, sub)
    n_sub = lax.axis_size("sub")
    depth = model_ref.shape[0]
    halo = jnp.zeros((RADIUS, AX, AY), jnp.float32)
    for r in range(NT):
        for buf in (pad_p, pad_q):
            buf[r, 0:RADIUS] = halo
            buf[r, RADIUS + depth : 2 * RADIUS + depth] = halo
    pad_p[0, RADIUS : RADIUS + depth] = pf_ref[0]
    pad_q[0, RADIUS : RADIUS + depth] = model_ref[...] * qa_ref[0]
    up_dev = device_of(group, (me + 1) % n_sub)
    down_dev = device_of(group, (me + n_sub - 1) % n_sub)
    target = device_of(group, sub)
    moved = target != sub
    mesh_id = pl.DeviceIdType.MESH
    barrier = pltpu.get_barrier_semaphore()
    pl.semaphore_signal(barrier, 1, device_id={"sub": up_dev}, device_id_type=mesh_id)
    pl.semaphore_signal(barrier, 1, device_id={"sub": down_dev}, device_id_type=mesh_id)

    @pl.when(moved)
    def _():
        pl.semaphore_signal(barrier, 1, device_id={"sub": target}, device_id_type=mesh_id)
        pl.semaphore_signal(barrier, 1, device_id={"sub": me}, device_id_type=mesh_id)
        pl.semaphore_wait(barrier, 4)

    @pl.when(jnp.logical_not(moved))
    def _():
        pl.semaphore_wait(barrier, 2)
    rows = lax.broadcasted_iota(jnp.int32, (AX, AY), 0)
    lanes = lax.broadcasted_iota(jnp.int32, (AX, AY), 1)
    n_rec = rcol_ref.shape[0]
    src_level = src_ref[0]
    src_spot = (rows == src_ref[1]) & (lanes == src_ref[2])

    def build_injection(step):
        hit_y = lax.broadcasted_iota(jnp.int32, (n_rec, AY), 1) == rcol_ref[...]
        spread = jnp.where(hit_y, resid_ref[:, step : step + 1], 0.0)
        parts = split_bf16(spread)
        rec_level = rrow_ref[0:1, :]
        hit_x = lax.broadcasted_iota(jnp.int32, (AX, n_rec), 0) == rrow_ref[1:2, :]

        def plane(j, carry):
            picks = (hit_x & (rec_level == j)).astype(jnp.bfloat16)
            total = jnp.dot(picks, parts[0], preferred_element_type=jnp.float32)
            total = total + jnp.dot(picks, parts[1], preferred_element_type=jnp.float32)
            total = total + jnp.dot(picks, parts[2], preferred_element_type=jnp.float32)
            inject[j] = total
            return carry

        lax.fori_loop(0, depth, plane, 0)

    def exchange(r, f):
        buf = (pad_p, pad_q)[f]
        down = pltpu.make_async_remote_copy(
            src_ref=buf.at[r, RADIUS : 2 * RADIUS],
            dst_ref=buf.at[r, RADIUS + depth : 2 * RADIUS + depth],
            send_sem=send_sem.at[r, f, 0],
            recv_sem=recv_sem.at[r, f, 0],
            device_id={"sub": down_dev},
            device_id_type=pl.DeviceIdType.MESH,
        )
        up = pltpu.make_async_remote_copy(
            src_ref=buf.at[r, depth : RADIUS + depth],
            dst_ref=buf.at[r, 0:RADIUS],
            send_sem=send_sem.at[r, f, 1],
            recv_sem=recv_sem.at[r, f, 1],
            device_id={"sub": up_dev},
            device_id_type=pl.DeviceIdType.MESH,
        )

        @pl.when(me > 0)
        def _():
            down.start()

        @pl.when(me < n_sub - 1)
        def _():
            up.start()

        return (down, up)

    def finish(pair):
        down, up = pair

        @pl.when(me > 0)
        def _():
            down.wait_send()
            up.wait_recv()

        @pl.when(me < n_sub - 1)
        def _():
            up.wait_send()
            down.wait_recv()

    def forward_round(r):
        def plane(j, carry):
            p = j + RADIUS
            lp = plane_stencil(pad_p, r, p, rows, lanes)
            lap[r, j] = lp
            if r < NT - 1:
                before = pf_ref[1, j] if r == 0 else pad_p[r - 1, p]
                following = 2.0 * pad_p[r, p] - before + model_ref[j] * lp
                source = jnp.where(src_spot & (src_level == j), wave_ref[r], 0.0)
                pad_p[r + 1, p] = following + source
            return carry

        lax.fori_loop(0, depth, plane, 0)

    def adjoint_round(r):
        def plane(j, carry):
            p = j + RADIUS
            lq = plane_stencil(pad_q, r, p, rows, lanes)
            now = qa_ref[0, j] if r == 0 else qs[r - 1, j]
            if r == 0:
                later = qa_ref[1, j]
            elif r == 1:
                later = qa_ref[0, j]
            else:
                later = qs[r - 2, j]
            result = 2.0 * now - later + lq
            result = result + inject[j]
            if r < NT - 1:
                qs[r, j] = result
                pad_q[r + 1, p] = model_ref[j] * result
            else:
                image = jnp.zeros((AX, AY), jnp.float32)
                for s in range(NT - 1):
                    image = image + qs[s, j] * lap[NT - 1 - s, j]
                image = image + result * lap[0, j]
                img_loc[j] = IMAGE_SCALE * image
            return carry

        lax.fori_loop(0, depth, plane, 0)

    fwd = exchange(0, 0)
    adj = exchange(0, 1)
    build_injection(NT - 1)
    for r in range(NT):
        finish(fwd)
        forward_round(r)
        if r < NT - 1:
            fwd = exchange(r + 1, 0)
        finish(adj)
        adjoint_round(r)
        if r < NT - 1:
            adj = exchange(r + 1, 1)
            build_injection(NT - 2 - r)
    image_copy = pltpu.make_async_remote_copy(
        src_ref=img_loc,
        dst_ref=img_scr,
        send_sem=image_sem.at[0],
        recv_sem=image_sem.at[1],
        device_id={"sub": me},
        device_id_type=mesh_id,
    )

    @pl.when(moved)
    def _():
        image_copy.start()
        image_copy.wait_send()
        image_copy.wait_recv()
        img_ref[...] = img_scr[...]

    @pl.when(jnp.logical_not(moved))
    def _():
        img_ref[...] = img_loc[...]


def migrate(model, state_fwd, state_adj, wave, source, receivers, resid):
    depth_cells = model.shape[0]
    plane = AX * AY
    offset = block_of(lax.axis_index("shot"), lax.axis_index("sub")) * depth_cells

    def level_of(cells):
        level = cells // plane - offset
        inside = (level >= 0) & (level < depth_cells)
        return jnp.where(inside, level, -1)

    src = jnp.stack([level_of(source), source % plane // AY, source % AY]).astype(jnp.int32)
    rrow = jnp.stack([level_of(receivers), receivers % plane // AY]).astype(jnp.int32)
    rcol = (receivers % AY).astype(jnp.int32).reshape(-1, 1)
    vmem = pl.BlockSpec(memory_space=pltpu.VMEM)
    smem = pl.BlockSpec(memory_space=pltpu.SMEM)
    padded = (NT, depth_cells + 2 * RADIUS, AX, AY)
    field = (NT, depth_cells, AX, AY)
    return pl.pallas_call(
        migrate_kernel,
        out_shape=jax.ShapeDtypeStruct(model.shape, jnp.float32),
        in_specs=[smem, smem] + [vmem] * 6,
        out_specs=vmem,
        scratch_shapes=[
            pltpu.VMEM(padded, jnp.float32),
            pltpu.VMEM(padded, jnp.float32),
            pltpu.VMEM(field, jnp.float32),
            pltpu.VMEM(field, jnp.float32),
            pltpu.VMEM(model.shape, jnp.float32),
            pltpu.VMEM(model.shape, jnp.float32),
            pltpu.VMEM(model.shape, jnp.float32),
            pltpu.SemaphoreType.DMA((NT, 2, 2)),
            pltpu.SemaphoreType.DMA((NT, 2, 2)),
            pltpu.SemaphoreType.DMA((2,)),
        ],
        compiler_params=pltpu.CompilerParams(collective_id=0, has_side_effects=True),
    )(
        src,
        wave.astype(jnp.float32),
        rrow,
        rcol,
        resid.T,
        model,
        state_fwd.astype(jnp.float32),
        state_adj.astype(jnp.float32),
    )


def body(
    velocity_tiles,
    forward_state,
    adjoint_state,
    wavelet,
    source_cell,
    receiver_cell,
    residual,
    aperture_row,
    aperture_col,
):
    groups = lax.axis_size("shot")
    own_cols = groups // AP_ROWS
    caps = (AP_COLS + own_cols) // own_cols
    assert own_cols == AP_COLS and caps == 2 and forward_state.shape[0] == 1
    n_sub = lax.axis_size("sub")
    assert n_sub == 2 * X_CHIPS and groups % GROUP_ROW == 0
    outbound = [
        (g * n_sub + b, g * n_sub + device_of(g, b)) for g in range(groups) for b in range(n_sub)
    ]
    myself = lax.axis_index("shot")
    shots_here = forward_state.shape[0]
    gradient = jnp.zeros(velocity_tiles.shape, jnp.float32)
    every_shot = list(range(shots_here))
    states_moved = []
    for k in range(shots_here):
        states = jnp.concatenate(
            [forward_state[k].astype(jnp.float32), adjoint_state[k].astype(jnp.float32)]
        )
        states_moved.append(lax.ppermute(states, ("shot", "sub"), outbound))
    sending = outgoing(
        velocity_tiles, aperture_row, aperture_col, every_shot, groups, own_cols, caps
    )
    fetched = lax.all_to_all(sending, "shot", split_axis=0, concat_axis=0, tiled=True)
    images = []
    for k in every_shot:
        shot_id = myself * SHOTS_DEV + k
        row_start = aperture_row[shot_id]
        col_start = aperture_col[shot_id]
        model = assemble(fetched, row_start, col_start, own_cols)
        model = lax.ppermute(model, ("shot", "sub"), outbound)
        states = states_moved[k]
        image = migrate(
            model,
            states[0:2],
            states[2:4],
            wavelet[k],
            source_cell[k],
            receiver_cell[k],
            residual[k],
        )
        images.append(disperse(image, row_start, col_start, groups, own_cols, caps))
    returned = lax.all_to_all(images[0], "shot", split_axis=0, concat_axis=0, tiled=True)
    gradient = accumulate(
        gradient, returned, aperture_row, aperture_col, every_shot, groups, own_cols, caps
    )
    return gradient


def solution(mesh):
    placed = (
        P("shot", "sub", None),
        P("shot", None, "sub", None, None),
        P("shot", None, "sub", None, None),
        P("shot", None),
        P("shot"),
        P("shot", None),
        P("shot", None, None),
        P(),
        P(),
    )
    return jax.shard_map(
        body, mesh=mesh, in_specs=placed, out_specs=P("shot", "sub", None), check_vma=False
    )
```
